128 devices in a mesh: lat: 8 (over x, core), lon: 16 (over y, z).
Axes of the slice: x: 4, y: 4, z: 4, core: 2. Of those that a mesh axis runs over, the one named last changes fastest.
Arguments:
- node_latent: bfloat16 [128, 512, 512], P('lat', 'lon'), may hold values from -6 to 6
- edge_latent: bfloat16 [262144, 512], P(('lat', 'lon')), may hold values from -6 to 6
- sender: int32 [262144], P(('lat', 'lon')), may hold values from -1 to 65535, as said below
- receiver: int32 [262144], P(('lat', 'lon')), may hold values from -1 to 127, as said below
- block_tile: int32 [2048], P(('lat', 'lon')), may hold values from 0 to 3, as said below
- w_first: bfloat16 [1536, 512], replicated, may hold values from -0.15625 to 0.15625
- w_second: bfloat16 [512, 512], replicated, may hold values from -0.25 to 0.25
- edge_gain: float32 [512], replicated, may hold values from 0.5 to 1.5
- w_node_first: bfloat16 [1024, 512], replicated, may hold values from -0.1875 to 0.1875
- w_node_second: bfloat16 [512, 512], replicated, may hold values from -0.25 to 0.25
- node_gain: float32 [512], replicated, may hold values from 0.5 to 1.5
Outputs:
- node_out: bfloat16 [128, 512, 512], P('lat', 'lon')
- edge_out: bfloat16 [262144, 512], P(('lat', 'lon'))
The draws below stay inside these ranges and needn't reach their ends.
Inputs may be any that keep to these rules, and one draw needn't show every extreme that they name: `sender`: -1 on padded slots; otherwise the id of one of the eight grid neighbours of the edge's receiver node (columns wrap around, rows do not), or of a node whose row and column are both multiples of 4, anywhere on the grid. `receiver`: padded slots (-1) stand at the end of each block, at least 32 slots of a block are live, and live values never fall within a block. `block_tile`: never falls from one block of a device to the next, over the device's 16 blocks.
All inputs are finite; a program needn't handle non-finite values.
Results may differ from the reference program's by a relative error of at most 0.008.
Values may be sent and summed in bfloat16 or wider, within the bound.
No kernel may reach another device: no remote copies, remote signals or barrier semaphores. Data moves between devices by JAX's collectives and lax.ppermute only.
A program may use at most 128 MiB of HBM per device.

```python
import jax
import jax.numpy as jnp
import numpy as np
from jax import lax

D = 512
PR = 16
PC = 32
BLOCKS_DEV = 16
BLK = 128
TILE_NODES = 128
NODE_DEV = 512
EDGE_DEV = 2048
NLAT = 128
NLON = 512
NODES = 65536
EDGES = 262144
N_LAT = 8
N_LON = 16
DEVICES = 128


def edge_plan(key):
    folded = jax.random.fold_in(key, 1013)
    subkeys = jax.random.split(folded, 7)
    grid_rows = PR * N_LAT
    grid_cols = PC * N_LON
    tile_count = PR // 4
    shape = (DEVICES, BLOCKS_DEV, BLK)
    device = jnp.arange(DEVICES, dtype=jnp.int32)[:, None]
    block_pos = jnp.arange(BLOCKS_DEV, dtype=jnp.int32)[None, :]
    offset = jax.random.randint(subkeys[0], (DEVICES, 1), -1, 2)
    tile_of = jnp.clip((block_pos + offset) * tile_count // BLOCKS_DEV, 0, tile_count - 1).astype(jnp.int32)
    live_count = jax.random.randint(subkeys[1], (DEVICES, BLOCKS_DEV, 1), BLK // 4, BLK + 1)
    slot_pos = jnp.arange(BLK, dtype=jnp.int32)[None, None, :]
    live_slot = slot_pos < live_count
    within = jnp.sort(jax.random.randint(subkeys[2], shape, 0, 4 * PC), axis=2)
    receiver = jnp.where(live_slot, within, -1)
    local_index = tile_of[:, :, None] * (4 * PC) + within
    lat_band = (device // N_LON)[:, :, None]
    lon_sector = (device % N_LON)[:, :, None]
    recv_row = lat_band * PR + local_index // PC
    recv_col = lon_sector * PC + local_index % PC
    picked = jax.random.randint(subkeys[3], shape, 0, 8)
    row_table = jnp.array(np.array([-1, -1, -1, 0, 0, 1, 1, 1], np.int32))
    col_table = jnp.array(np.array([-1, 0, 1, -1, 1, -1, 0, 1], np.int32))
    step_row = row_table[picked]
    step_col = col_table[picked]
    near_row = recv_row + step_row
    near_row = jnp.where((near_row < 0) | (near_row >= grid_rows), recv_row - step_row, near_row)
    near_col = (recv_col + step_col) % grid_cols
    is_polar = (lat_band == 0) | (lat_band == N_LAT - 1)
    coin_flip = jax.random.randint(subkeys[4], shape, 0, 4)
    is_far = coin_flip < jnp.where(is_polar, 2, 1)
    coarse_row = 4 * jax.random.randint(subkeys[5], shape, 0, grid_rows // 4)
    coarse_col = 4 * jax.random.randint(subkeys[6], shape, 0, grid_cols // 4)
    sender = jnp.where(is_far, coarse_row * grid_cols + coarse_col, near_row * grid_cols + near_col)
    sender = jnp.where(live_slot, sender, -1)
    return (sender.reshape(-1).astype(jnp.int32), receiver.reshape(-1).astype(jnp.int32), tile_of.reshape(-1))


def draw_sender(key, part):
    return edge_plan(key)[0]


def draw_receiver(key, part):
    return edge_plan(key)[1]


def draw_block_tile(key, part):
    return edge_plan(key)[2]


def shard_levels(stream_key, extent, shards, low, high):
    loudness, own = 1.0, jax.random.fold_in(stream_key, 6)
    for dim, blocks in shards:
        steps = jnp.exp(jax.random.uniform(jax.random.fold_in(own, dim), (blocks,), jnp.float32, low / len(shards), high / len(shards)))
        loudness = loudness * jnp.repeat(steps, extent[dim] // blocks).reshape([-1 if axis == dim else 1 for axis in range(len(extent))])
    return loudness


def noise(own_key, dims, scale, reach, shards=(), held_as=jnp.bfloat16):
    values = jax.random.normal(own_key, dims, jnp.float32) * scale
    if len(shards) > 0:
        values = shard_levels(own_key, dims, shards, -0.22, 0.18) * values
    return jnp.clip(values, min=-reach, max=reach).astype(held_as)


def setup_inputs(seed: int = 0) -> dict:
    keys = jax.random.split(jax.random.key(seed), 12)
    return {
        "node_latent": noise(keys[0], (NLAT, NLON, D), 1.0, 6.0, ((0, 8), (1, 16))),
        "edge_latent": noise(keys[1], (EDGES, D), 1.0, 6.0, ((0, 128),)),
        "sender": draw_sender(jax.random.fold_in(keys[11], 71), 0),
        "receiver": draw_receiver(jax.random.fold_in(keys[11], 71), 0),
        "block_tile": draw_block_tile(jax.random.fold_in(keys[11], 71), 0),
        "w_first": noise(keys[5], (3 * D, D), (3 * D) ** -0.5, 0.15625),
        "w_second": noise(keys[6], (D, D), D ** -0.5, 0.25),
        "edge_gain": jnp.clip(1.0 + 0.1 * jax.random.normal(keys[7], (D,), jnp.float32), 0.5, 1.5),
        "w_node_first": noise(keys[8], (2 * D, D), (2 * D) ** -0.5, 0.1875),
        "w_node_second": noise(keys[9], (D, D), D ** -0.5, 0.25),
        "node_gain": jnp.clip(1.0 + 0.1 * jax.random.normal(keys[10], (D,), jnp.float32), 0.5, 1.5),
    }


def layer_norm(values, gain_vec):
    average = lax.optimization_barrier(jnp.mean(values, -1, keepdims=True))
    centred = values - average
    spread = lax.optimization_barrier(jnp.mean(centred * centred, -1, keepdims=True))
    return centred * lax.rsqrt(spread + 1e-05) * gain_vec

def reference(node_latent, edge_latent, sender, receiver, block_tile, w_first, w_second, edge_gain, w_node_first, w_node_second, node_gain):
    node_rows = node_latent.reshape(NODES, D)
    edge_parts = edge_latent.reshape(DEVICES, EDGE_DEV, D)
    send_parts = sender.reshape(DEVICES, EDGE_DEV)
    recv_parts = receiver.reshape(DEVICES, EDGE_DEV)
    tile_parts = jnp.broadcast_to(block_tile.reshape(DEVICES, BLOCKS_DEV, 1), (DEVICES, BLOCKS_DEV, BLK)).reshape(DEVICES, EDGE_DEV)

    def one_device(pieces):
        edge_rows, senders, receivers, tile_of, device = pieces
        live_slot = receivers >= 0
        local_index = tile_of * TILE_NODES + jnp.maximum(receivers, 0)
        lat_band = device // N_LON
        lon_sector = device % N_LON
        recv_row = lat_band * PR + local_index // PC
        recv_col = lon_sector * PC + local_index % PC
        recv_rows = node_rows[recv_row * NLON + recv_col]
        send_rows = node_rows[jnp.maximum(senders, 0)]
        joined = jnp.concatenate([edge_rows, send_rows, recv_rows], axis=1)
        first_sum = jnp.dot(joined, w_first, preferred_element_type=jnp.float32)
        hidden = jax.nn.silu(first_sum).astype(jnp.bfloat16)
        second_sum = jnp.dot(hidden, w_second, preferred_element_type=jnp.float32)
        message = layer_norm(second_sum, edge_gain).astype(jnp.bfloat16)
        updated = jnp.where(live_slot[:, None], edge_rows.astype(jnp.float32) + message.astype(jnp.float32), jnp.zeros((), jnp.float32)).astype(jnp.bfloat16)
        segment = jnp.where(live_slot, local_index, NODE_DEV).astype(jnp.int32)
        summed = jax.ops.segment_sum(message.astype(jnp.float32), segment, num_segments=NODE_DEV + 1)[:NODE_DEV]
        return (updated, summed)
    device_ids = jnp.arange(DEVICES, dtype=jnp.int32)
    updated, summed = lax.map(one_device, (edge_parts, send_parts, recv_parts, tile_parts, device_ids))
    aggregate = summed.reshape(N_LAT, N_LON, PR, PC, D).transpose(0, 2, 1, 3, 4).reshape(NODES, D).astype(jnp.bfloat16)
    node_join = jnp.concatenate([node_rows, aggregate], axis=1)
    node_hidden = jax.nn.silu(jnp.dot(node_join, w_node_first, preferred_element_type=jnp.float32)).astype(jnp.bfloat16)
    node_second = jnp.dot(node_hidden, w_node_second, preferred_element_type=jnp.float32)
    node_out = (node_rows.astype(jnp.float32) + layer_norm(node_second, node_gain)).astype(jnp.bfloat16)
    return (node_out.reshape(NLAT, NLON, D), updated.reshape(EDGES, D))
```

```python
import jax
import jax.numpy as jnp
from jax import lax
from jax.experimental import pallas as pl
from jax.experimental.pallas import tpu as pltpu
from jax.sharding import PartitionSpec as P

F = 512
BLK = 128
GROUP = 4
ROWS = GROUP * BLK
PIECE = 512
RIM = 40
BF = jnp.bfloat16
F32 = jnp.float32


def device_of(x, c, y, z):
    return (x % 4 * 2 + c) * 16 + y % 4 * 4 + z % 4


def shift(axis, by_core):
    pairs = []
    for x in range(4):
        for c in range(2):
            for y in range(4):
                for z in range(4):
                    to = {"x": x, "y": y, "z": z}
                    to[axis] += by_core[c]
                    pairs.append((device_of(x, c, y, z), device_of(to["x"], c, to["y"], to["z"])))
    return pairs


def other_core(value):
    pairs = [
        (device_of(x, c, y, z), device_of(x, 1 - c, y, z))
        for x in range(4)
        for c in range(2)
        for y in range(4)
        for z in range(4)
    ]
    return lax.ppermute(value, ("lat", "lon"), pairs)


def move(value, axis, by_core):
    return lax.ppermute(value, ("lat", "lon"), shift(axis, by_core))


def ring(own, axis):
    ahead = move(own, axis, (1, -1))
    behind = move(own, axis, (-1, 1))
    across = move(ahead, axis, (1, -1))
    return own, ahead, behind, across


def ring_place(offset, core):
    near = jnp.where((offset == 1) == (core == 1), 1, 2)
    return jnp.where(offset == 0, 0, jnp.where(offset == 2, 3, near))


def silu(v):
    half = 0.5 * v
    return half + half * jnp.tanh(half)


def normed(values, gain):
    centred = values - jnp.mean(values, -1, keepdims=True)
    spread = jnp.mean(centred * centred, -1, keepdims=True)
    return centred * lax.rsqrt(spread + 1e-05) * gain


def dot(a, b):
    return jnp.dot(a, b, preferred_element_type=F32)


def chosen(recv_row):
    return (lax.broadcasted_iota(jnp.int32, (BLK, BLK), 0) == recv_row).astype(BF)


def early_kernel(tiles, edge_ref, recv_ref, node_ref, we_ref, wr_ref, wn_ref, pre_ref, nf_ref, got_ref):
    step = pl.program_id(0)

    @pl.when(step == 0)
    def _():
        nf_ref[...] = dot(node_ref[...], wn_ref[...])

    for k in range(GROUP):
        tile = pl.multiple_of(tiles[step * GROUP + k] * BLK, BLK)
        hot = chosen(recv_ref[k : k + 1, :])
        rows = lax.dot_general(
            hot,
            node_ref[pl.ds(tile, BLK), :],
            (((0,), (0,)), ((), ())),
            preferred_element_type=F32,
        )
        got_ref[k * BLK : (k + 1) * BLK, :] = rows.astype(BF)
    pre_ref[...] = dot(edge_ref[...], we_ref[...]) + dot(got_ref[...], wr_ref[...])


def late_kernel(
    table_index,
    tiles,
    lives,
    *refs,
):
    pieces = refs[:13]
    (
        pre_ref,
        edge_ref,
        recv_ref,
        nf_ref,
        node_ref,
        ws_ref,
        w2_ref,
        eg_ref,
        wn_ref,
        wn2_ref,
        ng_ref,
        out_ref,
        node_out_ref,
        table,
        sent,
        agg,
        sem,
    ) = refs[13:]
    step = pl.program_id(0)

    @pl.when(step == 0)
    def _():
        copies = []
        start = 0
        for i, piece in enumerate(pieces):
            rows = piece.shape[0]
            copies.append(pltpu.make_async_copy(piece, table.at[pl.ds(start, rows)], sem.at[i]))
            start += rows
        for copy in copies:
            copy.start()
        agg[...] = jnp.zeros_like(agg)
        for copy in copies:
            copy.wait()

    def fetch(i, carry):
        for u in range(16):
            e = i * 16 + u
            row = table[table_index[step * ROWS + e]]
            sent[pl.ds(pl.multiple_of(e * 4, 4), 4), :] = row.astype(F32)
        return carry

    lax.fori_loop(0, ROWS // 16, fetch, 0)
    send = jnp.concatenate(
        [sent[pl.ds(j, ROWS, stride=4), :].astype(BF) for j in range(4)], axis=1
    )
    hidden = silu(pre_ref[...] + dot(send, ws_ref[...])).astype(BF)
    message = normed(dot(hidden, w2_ref[...]), eg_ref[...]).astype(BF)
    place = lax.broadcasted_iota(jnp.int32, (BLK, F), 0)
    for k in range(GROUP):
        part = message[k * BLK : (k + 1) * BLK, :]
        edge = edge_ref[k * BLK : (k + 1) * BLK, :]
        live = place < lives[step * GROUP + k]
        out_ref[k * BLK : (k + 1) * BLK, :] = jnp.where(
            live, edge.astype(F32) + part.astype(F32), 0.0
        ).astype(BF)
        tile = pl.multiple_of(tiles[step * GROUP + k] * BLK, BLK)
        agg[pl.ds(tile, BLK), :] += dot(chosen(recv_ref[k : k + 1, :]), part)

    @pl.when(step == pl.num_programs(0) - 1)
    def _():
        first = nf_ref[...] + dot(agg[...].astype(BF), wn_ref[...])
        second = dot(silu(first).astype(BF), wn2_ref[...])
        node_out_ref[...] = (
            node_ref[...].astype(F32) + normed(second, ng_ref[...])
        ).astype(BF)


def per_device(
    node_latent,
    edge_latent,
    sender,
    receiver,
    block_tile,
    w_first,
    w_second,
    edge_gain,
    w_node_first,
    w_node_second,
    node_gain,
):
    patch_rows, patch_cols, features = node_latent.shape
    lat_index = lax.axis_index("lat")
    lon_index = lax.axis_index("lon")
    lat_count, lon_count = lax.axis_size("lat"), lax.axis_size("lon")
    grid_cols = patch_cols * lon_count
    blocks = block_tile.shape[0]
    nodes = patch_rows * patch_cols
    own_rows = node_latent.reshape(nodes, features)

    coarse_own = node_latent[::4, ::4].reshape(-1, 4, 128)
    line = jnp.concatenate(ring(coarse_own, "z"), 0)
    plane = jnp.concatenate(ring(line, "y"), 0)
    halves = ring(plane, "x")
    far_pieces = list(halves) + [other_core(part) for part in halves]

    right = [(i, (i + 1) % lon_count) for i in range(lon_count)]
    left = [(j, i) for i, j in right]
    up = [(i, i + 1) for i in range(lat_count - 1)]
    down = [(j, i) for i, j in up]
    west = lax.ppermute(node_latent[:, -1:], "lon", right)
    east = lax.ppermute(node_latent[:, :1], "lon", left)
    row_of = lambda r: jnp.concatenate([west[r], node_latent[r], east[r]], 0)
    north = lax.ppermute(row_of(patch_rows - 1), "lat", up)
    south = lax.ppermute(row_of(0), "lat", down)
    lanes = lambda a: a.reshape(-1, 4, 128)
    pad = lambda a: jnp.pad(lanes(a), ((0, RIM - patch_cols - 2), (0, 0), (0, 0)))
    near_pieces = [lanes(own_rows), lanes(west), lanes(east), pad(north), pad(south)]

    senders = jnp.maximum(sender, 0)
    send_row = senders // grid_cols
    send_col = senders % grid_cols
    row = send_row - lat_index * patch_rows
    col = (send_col - lon_index * patch_cols + 1) % grid_cols - 1
    is_near = (row >= -1) & (row <= patch_rows) & (col <= patch_cols)
    side = jnp.where(col < 0, nodes + row, nodes + patch_rows + row)
    inner = jnp.where((col < 0) | (col >= patch_cols), side, row * patch_cols + col)
    rim = nodes + 2 * patch_rows
    near_index = jnp.where(
        row < 0, rim + col + 1, jnp.where(row >= patch_rows, rim + RIM + col + 1, inner)
    )
    near_count = rim + 2 * RIM
    src_lat, src_lon = send_row // patch_rows, send_col // patch_cols
    src_core, core = src_lat % 2, lat_index % 2
    at_x = ring_place((src_lat // 2 - lat_index // 2) % 4, src_core)
    at_y = ring_place((src_lon // 4 - lon_index // 4) % 4, src_core)
    at_z = ring_place((src_lon % 4 - lon_index % 4) % 4, src_core)
    half = jnp.where(src_core == core, 0, 1)
    within = send_row % patch_rows // 4 * (patch_cols // 4) + send_col % patch_cols // 4
    per = patch_rows // 4 * (patch_cols // 4)
    far_index = near_count + ((((half * 4 + at_x) * 4 + at_y) * 4 + at_z) * per + within)
    table_index = jnp.where(is_near, near_index, far_index)
    recv_rows = receiver.reshape(blocks // GROUP, GROUP, BLK)
    lives = jnp.sum((receiver >= 0).astype(jnp.int32).reshape(blocks, BLK), 1)

    steps = blocks // GROUP
    whole = lambda shape: pl.BlockSpec(shape, lambda i, *_: (0,) * len(shape))
    part = pl.BlockSpec((ROWS, F), lambda i, *_: (i, 0))
    recv_spec = pl.BlockSpec((None, GROUP, BLK), lambda i, *_: (i, 0, 0))
    weight = lambda k: pl.BlockSpec((F, F), lambda i, *_: (k, 0))
    anywhere = pl.BlockSpec(memory_space=pl.ANY)
    pre, node_first = pl.pallas_call(
        early_kernel,
        name="early",
        grid_spec=pltpu.PrefetchScalarGridSpec(
            num_scalar_prefetch=1,
            grid=(steps,),
            in_specs=[part, recv_spec, whole((nodes, F)), weight(0), weight(2), weight(0)],
            out_specs=[part, whole((nodes, F))],
            scratch_shapes=[pltpu.VMEM((ROWS, F), BF)],
        ),
        out_shape=[
            jax.ShapeDtypeStruct((blocks * BLK, F), F32),
            jax.ShapeDtypeStruct((nodes, F), F32),
        ],
        compiler_params=pltpu.CompilerParams(vmem_limit_bytes=20 << 20),
        cost_estimate=pl.CostEstimate(
            flops=6 * 10**9, bytes_accessed=9 * 10**6, transcendentals=0
        ),
    )(block_tile, edge_latent, recv_rows, own_rows, w_first, w_first, w_node_first)

    pieces = near_pieces + far_pieces
    table_rows = sum(piece.shape[0] for piece in pieces)
    edge_out, node_out = pl.pallas_call(
        late_kernel,
        name="late",
        grid_spec=pltpu.PrefetchScalarGridSpec(
            num_scalar_prefetch=3,
            grid=(steps,),
            in_specs=[anywhere] * len(pieces)
            + [
                part,
                part,
                recv_spec,
                whole((nodes, F)),
                whole((nodes, F)),
                weight(1),
                whole((F, F)),
                whole((1, F)),
                weight(1),
                whole((F, F)),
                whole((1, F)),
            ],
            out_specs=[part, whole((nodes, F))],
            scratch_shapes=[
                pltpu.VMEM((table_rows, 4, 128), BF),
                pltpu.VMEM((ROWS * 4, 128), F32),
                pltpu.VMEM((nodes, F), F32),
                pltpu.SemaphoreType.DMA((len(pieces),)),
            ],
        ),
        out_shape=[
            jax.ShapeDtypeStruct((blocks * BLK, F), BF),
            jax.ShapeDtypeStruct((nodes, F), BF),
        ],
        compiler_params=pltpu.CompilerParams(vmem_limit_bytes=40 << 20),
        cost_estimate=pl.CostEstimate(
            flops=8 * 10**9, bytes_accessed=16 * 10**6, transcendentals=0
        ),
    )(
        table_index,
        block_tile,
        lives,
        *pieces,
        pre,
        edge_latent,
        recv_rows,
        node_first,
        own_rows,
        w_first,
        w_second,
        edge_gain.reshape(1, F),
        w_node_first,
        w_node_second,
        node_gain.reshape(1, F),
    )
    return node_out.reshape(patch_rows, patch_cols, features), edge_out


def solution(mesh):
    return jax.shard_map(
        per_device,
        mesh=mesh,
        in_specs=(
            P("lat", "lon", None),
            P(("lat", "lon"), None),
            P(("lat", "lon")),
            P(("lat", "lon")),
            P(("lat", "lon")),
            P(),
            P(),
            P(),
            P(),
            P(),
            P(),
        ),
        out_specs=(P("lat", "lon", None), P(("lat", "lon"), None)),
        check_vma=False,
    )
```

```python
import jax
import jax.numpy as jnp
from jax import lax
from jax.experimental import pallas as pl
from jax.experimental.pallas import tpu as pltpu
from jax.sharding import PartitionSpec as P

F = 512
BLK = 128
GROUP = 4
ROWS = GROUP * BLK
RIM = 40
NEAR = 5
FAR = 8
VMEM = 56 << 20
BF = jnp.bfloat16
F32 = jnp.float32


def device_of(x, c, y, z):
    return (x % 4 * 2 + c) * 16 + y % 4 * 4 + z % 4


def shift(axis, by_core):
    pairs = []
    for x in range(4):
        for c in range(2):
            for y in range(4):
                for z in range(4):
                    to = {"x": x, "y": y, "z": z}
                    to[axis] += by_core[c]
                    pairs.append((device_of(x, c, y, z), device_of(to["x"], c, to["y"], to["z"])))
    return pairs


def other_core(value):
    pairs = [
        (device_of(x, c, y, z), device_of(x, 1 - c, y, z))
        for x in range(4)
        for c in range(2)
        for y in range(4)
        for z in range(4)
    ]
    return lax.ppermute(value, ("lat", "lon"), pairs)


def move(value, axis, by_core):
    return lax.ppermute(value, ("lat", "lon"), shift(axis, by_core))


def ring(own, axis):
    ahead = move(own, axis, (1, -1))
    behind = move(own, axis, (-1, 1))
    across = move(ahead, axis, (1, -1))
    return own, ahead, behind, across


def ring_place(offset, core):
    near = jnp.where((offset == 1) == (core == 1), 1, 2)
    return jnp.where(offset == 0, 0, jnp.where(offset == 2, 3, near))


def silu(v):
    half = 0.5 * v
    return half + half * jnp.tanh(half)


def normed(values, gain):
    centred = values - jnp.mean(values, -1, keepdims=True)
    spread = jnp.mean(centred * centred, -1, keepdims=True)
    return centred * lax.rsqrt(spread + 1e-05) * gain


def dot(a, b):
    return jnp.dot(a, b, preferred_element_type=F32)


def chosen(recv_row):
    return (lax.broadcasted_iota(jnp.int32, (BLK, BLK), 0) == recv_row).astype(BF)


def fetch(count, unroll, entry, table, sent):
    def body(i, carry):
        for u in range(unroll):
            slot, row = entry(i * unroll + u)
            sent[pl.ds(pl.multiple_of(slot * 4, 4), 4), :] = table[row].astype(F32)
        return carry

    lax.fori_loop(0, count, body, 0)


def sent_rows(sent):
    return jnp.concatenate(
        [sent[pl.ds(j, ROWS, stride=4), :].astype(BF) for j in range(4)], axis=1
    )


def load_table(pieces, table, sem):
    copies = []
    start = 0
    for i, piece in enumerate(pieces):
        rows = piece.shape[0]
        copies.append(pltpu.make_async_copy(piece, table.at[pl.ds(start, rows)], sem.at[i]))
        start += rows
    for copy in copies:
        copy.start()
    return copies


def early_kernel(near_index, tiles, *refs):
    pieces = refs[:NEAR]
    (
        edge_ref,
        recv_ref,
        node_ref,
        we_ref,
        ws_ref,
        wr_ref,
        wn_ref,
        pre_ref,
        nf_ref,
        table,
        sent,
        got_ref,
        sem,
    ) = refs[NEAR:]
    step = pl.program_id(0)

    @pl.when(step == 0)
    def _():
        copies = load_table(pieces, table, sem)
        nf_ref[...] = dot(node_ref[...], wn_ref[...])
        for copy in copies:
            copy.wait()

    fetch(ROWS // 16, 16, lambda e: (e, near_index[step * ROWS + e]), table, sent)
    for k in range(GROUP):
        tile = pl.multiple_of(tiles[step * GROUP + k] * BLK, BLK)
        hot = chosen(recv_ref[k : k + 1, :])
        rows = lax.dot_general(
            hot,
            node_ref[pl.ds(tile, BLK), :],
            (((0,), (0,)), ((), ())),
            preferred_element_type=F32,
        )
        got_ref[k * BLK : (k + 1) * BLK, :] = rows.astype(BF)
    pre_ref[...] = (
        dot(edge_ref[...], we_ref[...])
        + dot(got_ref[...], wr_ref[...])
        + dot(sent_rows(sent), ws_ref[...])
    )


def late_kernel(far_list, far_count, tiles, lives, *refs):
    pieces = refs[:FAR]
    (
        pre_ref,
        edge_ref,
        recv_ref,
        nf_ref,
        node_ref,
        ws_ref,
        w2_ref,
        eg_ref,
        wn_ref,
        wn2_ref,
        ng_ref,
        out_ref,
        node_out_ref,
        table,
        sent,
        agg,
        sem,
    ) = refs[FAR:]
    step = pl.program_id(0)
    sent[...] = jnp.zeros_like(sent)

    @pl.when(step == 0)
    def _():
        copies = load_table(pieces, table, sem)
        agg[...] = jnp.zeros_like(agg)
        for copy in copies:
            copy.wait()

    def entry(i):
        packed = far_list[step * ROWS + i]
        return packed % 1024, packed // 1024

    fetch((far_count[step] + 7) // 8, 8, entry, table, sent)
    hidden = silu(pre_ref[...] + dot(sent_rows(sent), ws_ref[...])).astype(BF)
    message = normed(dot(hidden, w2_ref[...]), eg_ref[...]).astype(BF)
    place = lax.broadcasted_iota(jnp.int32, (BLK, F), 0)
    for k in range(GROUP):
        part = message[k * BLK : (k + 1) * BLK, :]
        edge = edge_ref[k * BLK : (k + 1) * BLK, :]
        live = place < lives[step * GROUP + k]
        out_ref[k * BLK : (k + 1) * BLK, :] = jnp.where(
            live, edge.astype(F32) + part.astype(F32), 0.0
        ).astype(BF)
        tile = pl.multiple_of(tiles[step * GROUP + k] * BLK, BLK)
        agg[pl.ds(tile, BLK), :] += dot(chosen(recv_ref[k : k + 1, :]), part)

    @pl.when(step == pl.num_programs(0) - 1)
    def _():
        first = nf_ref[...] + dot(agg[...].astype(BF), wn_ref[...])
        second = dot(silu(first).astype(BF), wn2_ref[...])
        node_out_ref[...] = (
            node_ref[...].astype(F32) + normed(second, ng_ref[...])
        ).astype(BF)


def far_lists(is_far, far_index, steps):
    place = jnp.arange(ROWS, dtype=jnp.int32)
    far = is_far.reshape(steps, ROWS)
    flag = far.astype(jnp.int32)
    before = place[:, None] > place[None, :]
    rank = jnp.sum(jnp.where(before[None], flag[:, None, :], 0), 2)
    packed = far_index.reshape(steps, ROWS) * 1024 + place - ROWS
    hit = (rank[:, None, :] == place[None, :, None]) & far[:, None, :]
    return (ROWS + jnp.sum(jnp.where(hit, packed[:, None, :], 0), 2)).reshape(-1), jnp.sum(flag, 1)


def per_device(
    node_latent,
    edge_latent,
    sender,
    receiver,
    block_tile,
    w_first,
    w_second,
    edge_gain,
    w_node_first,
    w_node_second,
    node_gain,
):
    patch_rows, patch_cols, features = node_latent.shape
    lat_index = lax.axis_index("lat")
    lon_index = lax.axis_index("lon")
    lat_count, lon_count = lax.axis_size("lat"), lax.axis_size("lon")
    grid_cols = patch_cols * lon_count
    blocks = block_tile.shape[0]
    steps = blocks // GROUP
    nodes = patch_rows * patch_cols
    own_rows = node_latent.reshape(nodes, features)
    lanes = lambda a: a.reshape(-1, 4, 128)

    right = [(i, (i + 1) % lon_count) for i in range(lon_count)]
    left = [(j, i) for i, j in right]
    up = [(i, i + 1) for i in range(lat_count - 1)]
    down = [(j, i) for i, j in up]

    coarse_own = lanes(node_latent[::4, ::4])
    west = lax.ppermute(node_latent[:, -1:], "lon", right)
    east = lax.ppermute(node_latent[:, :1], "lon", left)
    line = jnp.concatenate(ring(coarse_own, "z"), 0)
    line, west, east = lax.optimization_barrier((line, west, east))
    row_of = lambda r: jnp.concatenate([west[r], node_latent[r], east[r]], 0)
    north = lax.ppermute(row_of(patch_rows - 1), "lat", up)
    south = lax.ppermute(row_of(0), "lat", down)
    plane = jnp.concatenate(ring(line, "y"), 0)
    plane, north, south = lax.optimization_barrier((plane, north, south))
    own, ahead, behind, across = ring(plane, "x")

    pad = lambda a: jnp.pad(lanes(a), ((0, RIM - patch_cols - 2), (0, 0), (0, 0)))
    near_pieces = [lanes(own_rows), lanes(west), lanes(east), pad(north), pad(south)]

    senders = jnp.maximum(sender, 0)
    send_row = senders // grid_cols
    send_col = senders % grid_cols
    row = send_row - lat_index * patch_rows
    col = (send_col - lon_index * patch_cols + 1) % grid_cols - 1
    is_near = (row >= -1) & (row <= patch_rows) & (col <= patch_cols)
    side = jnp.where(col < 0, nodes + row, nodes + patch_rows + row)
    inner = jnp.where((col < 0) | (col >= patch_cols), side, row * patch_cols + col)
    rim = nodes + 2 * patch_rows
    near_index = jnp.where(
        row < 0, rim + col + 1, jnp.where(row >= patch_rows, rim + RIM + col + 1, inner)
    )
    no_row = rim + patch_cols + 2
    near_index = jnp.where(is_near, near_index, no_row)
    src_lat, src_lon = send_row // patch_rows, send_col // patch_cols
    src_core, core = src_lat % 2, lat_index % 2
    at_x = ring_place((src_lat // 2 - lat_index // 2) % 4, src_core)
    at_y = ring_place((src_lon // 4 - lon_index // 4) % 4, src_core)
    at_z = ring_place((src_lon % 4 - lon_index % 4) % 4, src_core)
    half = jnp.where(src_core == core, 0, 1)
    within = send_row % patch_rows // 4 * (patch_cols // 4) + send_col % patch_cols // 4
    per = patch_rows // 4 * (patch_cols // 4)
    far_index = (((half * 4 + at_x) * 4 + at_y) * 4 + at_z) * per + within
    far_list, far_count = far_lists((receiver >= 0) & ~is_near, far_index, steps)
    recv_rows = receiver.reshape(steps, GROUP, BLK)
    lives = jnp.sum((receiver >= 0).astype(jnp.int32).reshape(blocks, BLK), 1)

    whole = lambda shape: pl.BlockSpec(shape, lambda i, *_: (0,) * len(shape))
    part = pl.BlockSpec((ROWS, F), lambda i, *_: (i, 0))
    recv_spec = pl.BlockSpec((None, GROUP, BLK), lambda i, *_: (i, 0, 0))
    weight = lambda k: pl.BlockSpec((F, F), lambda i, *_: (k, 0))
    anywhere = pl.BlockSpec(memory_space=pl.ANY)
    near_rows = sum(piece.shape[0] for piece in near_pieces)
    pre, node_first = pl.pallas_call(
        early_kernel,
        name="early",
        grid_spec=pltpu.PrefetchScalarGridSpec(
            num_scalar_prefetch=2,
            grid=(steps,),
            in_specs=[anywhere] * NEAR
            + [part, recv_spec, whole((nodes, F)), weight(0), weight(1), weight(2), weight(0)],
            out_specs=[part, whole((nodes, F))],
            scratch_shapes=[
                pltpu.VMEM((near_rows, 4, 128), BF),
                pltpu.VMEM((ROWS * 4, 128), F32),
                pltpu.VMEM((ROWS, F), BF),
                pltpu.SemaphoreType.DMA((NEAR,)),
            ],
        ),
        out_shape=[
            jax.ShapeDtypeStruct((blocks * BLK, F), F32),
            jax.ShapeDtypeStruct((nodes, F), F32),
        ],
        compiler_params=pltpu.CompilerParams(vmem_limit_bytes=VMEM),
        cost_estimate=pl.CostEstimate(
            flops=4 * 10**9, bytes_accessed=10 * 10**6, transcendentals=0
        ),
    )(
        near_index,
        block_tile,
        *near_pieces,
        edge_latent,
        recv_rows,
        own_rows,
        w_first,
        w_first,
        w_first,
        w_node_first,
    )

    across, pre = lax.optimization_barrier((across, pre))
    halves = [own, ahead, behind, across]
    far_pieces = halves + [other_core(piece) for piece in halves]
    far_rows = sum(piece.shape[0] for piece in far_pieces)
    edge_out, node_out = pl.pallas_call(
        late_kernel,
        name="late",
        grid_spec=pltpu.PrefetchScalarGridSpec(
            num_scalar_prefetch=4,
            grid=(steps,),
            in_specs=[anywhere] * FAR
            + [
                part,
                part,
                recv_spec,
                whole((nodes, F)),
                whole((nodes, F)),
                weight(1),
                whole((F, F)),
                whole((1, F)),
                weight(1),
                whole((F, F)),
                whole((1, F)),
            ],
            out_specs=[part, whole((nodes, F))],
            scratch_shapes=[
                pltpu.VMEM((far_rows, 4, 128), BF),
                pltpu.VMEM((ROWS * 4 + 32, 128), F32),
                pltpu.VMEM((nodes, F), F32),
                pltpu.SemaphoreType.DMA((FAR,)),
            ],
        ),
        out_shape=[
            jax.ShapeDtypeStruct((blocks * BLK, F), BF),
            jax.ShapeDtypeStruct((nodes, F), BF),
        ],
        compiler_params=pltpu.CompilerParams(vmem_limit_bytes=VMEM),
        cost_estimate=pl.CostEstimate(
            flops=4 * 10**9, bytes_accessed=16 * 10**6, transcendentals=2 * 10**6
        ),
    )(
        far_list,
        far_count,
        block_tile,
        lives,
        *far_pieces,
        pre,
        edge_latent,
        recv_rows,
        node_first,
        own_rows,
        w_first,
        w_second,
        edge_gain.reshape(1, F),
        w_node_first,
        w_node_second,
        node_gain.reshape(1, F),
    )
    return node_out.reshape(patch_rows, patch_cols, features), edge_out


def solution(mesh):
    return jax.shard_map(
        per_device,
        mesh=mesh,
        in_specs=(
            P("lat", "lon", None),
            P(("lat", "lon"), None),
            P(("lat", "lon")),
            P(("lat", "lon")),
            P(("lat", "lon")),
            P(),
            P(),
            P(),
            P(),
            P(),
            P(),
        ),
        out_specs=(P("lat", "lon", None), P(("lat", "lon"), None)),
        check_vma=False,
    )
```

```python
import jax
import jax.numpy as jnp
from jax import lax
from jax.experimental import pallas as pl
from jax.experimental.pallas import tpu as pltpu
from jax.sharding import PartitionSpec as P

F = 512
BLK = 128
GROUP = 4
ROWS = GROUP * BLK
RIM = 40
NEAR = 5
FAR = 8
VMEM = 56 << 20
BF = jnp.bfloat16
F32 = jnp.float32


def device_of(x, c, y, z):
    return (x % 4 * 2 + c) * 16 + y % 4 * 4 + z % 4


def shift(axis, by_core):
    pairs = []
    for x in range(4):
        for c in range(2):
            for y in range(4):
                for z in range(4):
                    to = {"x": x, "y": y, "z": z}
                    to[axis] += by_core[c]
                    pairs.append((device_of(x, c, y, z), device_of(to["x"], c, to["y"], to["z"])))
    return pairs


def other_core(value):
    pairs = [
        (device_of(x, c, y, z), device_of(x, 1 - c, y, z))
        for x in range(4)
        for c in range(2)
        for y in range(4)
        for z in range(4)
    ]
    return lax.ppermute(value, ("lat", "lon"), pairs)


def move(value, axis, by_core):
    return lax.ppermute(value, ("lat", "lon"), shift(axis, by_core))


def ring_place(offset, core):
    near = jnp.where((offset == 1) == (core == 1), 1, 2)
    return jnp.where(offset == 0, 0, jnp.where(offset == 2, 3, near))


def silu(v):
    half = 0.5 * v
    return half + half * jnp.tanh(half)


def normed(values, gain):
    centred = values - jnp.mean(values, -1, keepdims=True)
    spread = jnp.mean(centred * centred, -1, keepdims=True)
    return centred * lax.rsqrt(spread + 1e-05) * gain


def dot(a, b):
    return jnp.dot(a, b, preferred_element_type=F32)


def chosen(recv_row):
    return (lax.broadcasted_iota(jnp.int32, (BLK, BLK), 0) == recv_row).astype(BF)


def fetch(count, unroll, entry, table, sent):
    def body(i, carry):
        for u in range(unroll):
            slot, row = entry(i * unroll + u)
            sent[pl.ds(pl.multiple_of(slot * 4, 4), 4), :] = table[row].astype(F32)
        return carry

    lax.fori_loop(0, count, body, 0)


def sent_rows(sent, base=0):
    return jnp.concatenate(
        [sent[pl.ds(base * 4 + j, ROWS, stride=4), :].astype(BF) for j in range(4)], axis=1
    )


def load_table(pieces, table, sem):
    copies = []
    start = 0
    for i, piece in enumerate(pieces):
        rows = piece.shape[0]
        copies.append(pltpu.make_async_copy(piece, table.at[pl.ds(start, rows)], sem.at[i]))
        start += rows
    for copy in copies:
        copy.start()
    return copies


def early_kernel(near_index, tiles, *refs):
    pieces = refs[:NEAR]
    (
        edge_ref,
        recv_ref,
        node_ref,
        we_ref,
        ws_ref,
        wr_ref,
        wn_ref,
        pre_ref,
        nf_ref,
        table,
        sent,
        got_ref,
        sem,
    ) = refs[NEAR:]
    step = pl.program_id(0)

    @pl.when(step == 0)
    def _():
        copies = load_table(pieces, table, sem)
        nf_ref[...] = dot(node_ref[...], wn_ref[...])
        for copy in copies:
            copy.wait()

    fetch(ROWS // 16, 16, lambda e: (e, near_index[step * ROWS + e]), table, sent)
    for k in range(GROUP):
        tile = pl.multiple_of(tiles[step * GROUP + k] * BLK, BLK)
        hot = chosen(recv_ref[k : k + 1, :])
        rows = lax.dot_general(
            hot,
            node_ref[pl.ds(tile, BLK), :],
            (((0,), (0,)), ((), ())),
            preferred_element_type=F32,
        )
        got_ref[k * BLK : (k + 1) * BLK, :] = rows.astype(BF)
    pre_ref[...] = (
        dot(edge_ref[...], we_ref[...])
        + dot(got_ref[...], wr_ref[...])
        + dot(sent_rows(sent), ws_ref[...])
    ).astype(BF)


def late_kernel(far_list, far_count, tiles, lives, *refs):
    pieces = refs[:FAR]
    (
        pre_hbm,
        edge_hbm,
        nf_hbm,
        node_hbm,
        w1_hbm,
        w2_hbm,
        wn_hbm,
        wn2_hbm,
        recv_ref,
        eg_ref,
        ng_ref,
        out_hbm,
        node_out_ref,
        table,
        sent,
        pre,
        edge,
        out,
        agg,
        nf,
        node,
        ws,
        w2,
        wn,
        wn2,
        sem,
        in_sem,
        out_sem,
    ) = refs[FAR:]
    steps = recv_ref.shape[0] // GROUP
    rows_of = lambda g: pl.ds(g * ROWS, ROWS)
    copies = load_table(pieces, table, sem)
    first = [
        pltpu.make_async_copy(w1_hbm.at[pl.ds(F, F)], ws, in_sem.at[0]),
        pltpu.make_async_copy(w2_hbm, w2, in_sem.at[1]),
    ]
    parts = []
    for g in range(steps):
        parts.append(
            [
                pltpu.make_async_copy(pre_hbm.at[rows_of(g)], pre.at[rows_of(g)], in_sem.at[6 + 2 * g]),
                pltpu.make_async_copy(edge_hbm.at[rows_of(g)], edge.at[rows_of(g)], in_sem.at[7 + 2 * g]),
            ]
        )
    last = [
        pltpu.make_async_copy(nf_hbm, nf, in_sem.at[2]),
        pltpu.make_async_copy(node_hbm, node, in_sem.at[3]),
        pltpu.make_async_copy(wn_hbm.at[pl.ds(F, F)], wn, in_sem.at[4]),
        pltpu.make_async_copy(wn2_hbm, wn2, in_sem.at[5]),
    ]
    for copy in first + sum(parts, []) + last:
        copy.start()
    sent[...] = jnp.zeros_like(sent)
    agg[...] = jnp.zeros_like(agg)
    for copy in copies:
        copy.wait()

    for g in range(steps):

        def entry(i):
            packed = far_list[g * ROWS + i]
            return packed & 4095, packed >> 12

        fetch((far_count[g] + 7) >> 3, 8, entry, table, sent)
    for copy in first:
        copy.wait()
    place = lax.broadcasted_iota(jnp.int32, (BLK, F), 0)
    stores = []
    for g in range(steps):
        for copy in parts[g]:
            copy.wait()
        base = g * ROWS
        total = pre[rows_of(g), :].astype(F32) + dot(sent_rows(sent, base), ws[...])
        message = normed(dot(silu(total).astype(BF), w2[...]), eg_ref[...]).astype(BF)
        for k in range(GROUP):
            b = g * GROUP + k
            part = message[k * BLK : (k + 1) * BLK, :]
            at = pl.ds(base + k * BLK, BLK)
            live = place < lives[b]
            out[at, :] = jnp.where(
                live, edge[at, :].astype(F32) + part.astype(F32), 0.0
            ).astype(BF)
            tile = pl.multiple_of(tiles[b] * BLK, BLK)
            agg[pl.ds(tile, BLK), :] += dot(chosen(recv_ref[b : b + 1, :]), part)
        store = pltpu.make_async_copy(out.at[rows_of(g)], out_hbm.at[rows_of(g)], out_sem.at[g])
        store.start()
        stores.append(store)
    for copy in last:
        copy.wait()
    first_sum = nf[...] + dot(agg[...].astype(BF), wn[...])
    second = dot(silu(first_sum).astype(BF), wn2[...])
    node_out_ref[...] = (node[...].astype(F32) + normed(second, ng_ref[...])).astype(BF)
    for store in stores:
        store.wait()


def far_lists(is_far, far_index, steps):
    place = jnp.arange(ROWS, dtype=jnp.int32)
    slots = steps * ROWS
    far = is_far.reshape(steps, ROWS)
    flag = far.astype(jnp.int32)
    before = place[:, None] > place[None, :]
    rank = jnp.sum(jnp.where(before[None], flag[:, None, :], 0), 2)
    packed = (far_index * 4096 + jnp.arange(slots, dtype=jnp.int32) - slots).reshape(steps, ROWS)
    hit = (rank[:, None, :] == place[None, :, None]) & far[:, None, :]
    return (slots + jnp.sum(jnp.where(hit, packed[:, None, :], 0), 2)).reshape(-1), jnp.sum(flag, 1)


def specs():
    whole = lambda shape: pl.BlockSpec(shape, lambda i, *_: (0,) * len(shape))
    part = pl.BlockSpec((ROWS, F), lambda i, *_: (i, 0))
    recv_spec = pl.BlockSpec((None, GROUP, BLK), lambda i, *_: (i, 0, 0))
    weight = lambda k: pl.BlockSpec((F, F), lambda i, *_: (k, 0))
    anywhere = pl.BlockSpec(memory_space=pl.ANY)
    return whole, part, recv_spec, weight, anywhere


def early_call(near_index, block_tile, near_pieces, edge_latent, recv_rows, own_rows, w_first, w_node_first):
    whole, part, recv_spec, weight, anywhere = specs()
    blocks, nodes = block_tile.shape[0], own_rows.shape[0]
    steps = blocks // GROUP
    near_rows = sum(piece.shape[0] for piece in near_pieces)
    return pl.pallas_call(
        early_kernel,
        name="early",
        grid_spec=pltpu.PrefetchScalarGridSpec(
            num_scalar_prefetch=2,
            grid=(steps,),
            in_specs=[anywhere] * NEAR
            + [part, recv_spec, whole((nodes, F)), weight(0), weight(1), weight(2), weight(0)],
            out_specs=[part, whole((nodes, F))],
            scratch_shapes=[
                pltpu.VMEM((near_rows, 4, 128), BF),
                pltpu.VMEM((ROWS * 4, 128), F32),
                pltpu.VMEM((ROWS, F), BF),
                pltpu.SemaphoreType.DMA((NEAR,)),
            ],
        ),
        out_shape=[
            jax.ShapeDtypeStruct((blocks * BLK, F), BF),
            jax.ShapeDtypeStruct((nodes, F), F32),
        ],
        compiler_params=pltpu.CompilerParams(vmem_limit_bytes=VMEM),
        cost_estimate=pl.CostEstimate(
            flops=4 * 10**9, bytes_accessed=10 * 10**6, transcendentals=0
        ),
    )(
        near_index,
        block_tile,
        *near_pieces,
        edge_latent,
        recv_rows,
        own_rows,
        w_first,
        w_first,
        w_first,
        w_node_first,
    )


def late_call(
    far_list,
    far_count,
    block_tile,
    lives,
    far_pieces,
    pre,
    edge_latent,
    receiver,
    node_first,
    own_rows,
    w_first,
    w_second,
    edge_gain,
    w_node_first,
    w_node_second,
    node_gain,
):
    blocks, nodes = block_tile.shape[0], own_rows.shape[0]
    slots, steps = blocks * BLK, blocks // GROUP
    far_rows = sum(piece.shape[0] for piece in far_pieces)
    anywhere = pl.BlockSpec(memory_space=pl.ANY)
    local = pl.BlockSpec(memory_space=pltpu.VMEM)
    scalars = pl.BlockSpec(memory_space=pltpu.SMEM)
    square = pltpu.VMEM((F, F), BF)
    return pl.pallas_call(
        late_kernel,
        name="late",
        in_specs=[scalars] * 4 + [anywhere] * (FAR + 8) + [local] * 3,
        out_specs=[anywhere, local],
        scratch_shapes=[
            pltpu.VMEM((far_rows, 4, 128), BF),
            pltpu.VMEM((slots * 4 + 32, 128), F32),
            pltpu.VMEM((slots, F), BF),
            pltpu.VMEM((slots, F), BF),
            pltpu.VMEM((slots, F), BF),
            pltpu.VMEM((nodes, F), F32),
            pltpu.VMEM((nodes, F), F32),
            pltpu.VMEM((nodes, F), BF),
            square,
            square,
            square,
            square,
            pltpu.SemaphoreType.DMA((FAR,)),
            pltpu.SemaphoreType.DMA((6 + 2 * steps,)),
            pltpu.SemaphoreType.DMA((steps,)),
        ],
        out_shape=[
            jax.ShapeDtypeStruct((slots, F), BF),
            jax.ShapeDtypeStruct((nodes, F), BF),
        ],
        compiler_params=pltpu.CompilerParams(vmem_limit_bytes=VMEM),
        cost_estimate=pl.CostEstimate(
            flops=4 * 10**9, bytes_accessed=14 * 10**6, transcendentals=2 * 10**6
        ),
    )(
        far_list,
        far_count,
        block_tile,
        lives,
        *far_pieces,
        pre,
        edge_latent,
        node_first,
        own_rows,
        w_first,
        w_second,
        w_node_first,
        w_node_second,
        receiver.reshape(blocks, BLK),
        edge_gain.reshape(1, F),
        node_gain.reshape(1, F),
    )


def per_device(
    node_latent,
    edge_latent,
    sender,
    receiver,
    block_tile,
    w_first,
    w_second,
    edge_gain,
    w_node_first,
    w_node_second,
    node_gain,
):
    patch_rows, patch_cols, features = node_latent.shape
    lat_index = lax.axis_index("lat")
    lon_index = lax.axis_index("lon")
    lat_count, lon_count = lax.axis_size("lat"), lax.axis_size("lon")
    grid_cols = patch_cols * lon_count
    blocks = block_tile.shape[0]
    steps = blocks // GROUP
    nodes = patch_rows * patch_cols
    own_rows = node_latent.reshape(nodes, features)
    lanes = lambda a: a.reshape(-1, 4, 128)

    right = [(i, (i + 1) % lon_count) for i in range(lon_count)]
    left = [(j, i) for i, j in right]
    up = [(i, i + 1) for i in range(lat_count - 1)]
    down = [(j, i) for i, j in up]

    coarse_own = lanes(node_latent[::4, ::4])
    copies = jnp.broadcast_to(coarse_own, (lon_count, *coarse_own.shape))
    copies, latent = lax.optimization_barrier((copies, node_latent))
    plane = lanes(lax.all_to_all(copies, "lon", split_axis=0, concat_axis=0, tiled=True))

    west = lax.ppermute(latent[:, -1:], "lon", right)
    east = lax.ppermute(latent[:, :1], "lon", left)
    row_of = lambda r: jnp.concatenate([west[r], latent[r], east[r]], 0)
    north = lax.ppermute(row_of(patch_rows - 1), "lat", up)
    south = lax.ppermute(row_of(0), "lat", down)
    plane, north, south = lax.optimization_barrier((plane, north, south))
    own, ahead, behind = plane, move(plane, "x", (1, -1)), move(plane, "x", (-1, 1))

    pad = lambda a: jnp.pad(lanes(a), ((0, RIM - patch_cols - 2), (0, 0), (0, 0)))
    near_pieces = [lanes(own_rows), lanes(west), lanes(east), pad(north), pad(south)]

    senders = jnp.maximum(sender, 0)
    send_row = senders // grid_cols
    send_col = senders % grid_cols
    row = send_row - lat_index * patch_rows
    col = (send_col - lon_index * patch_cols + 1) % grid_cols - 1
    is_near = (row >= -1) & (row <= patch_rows) & (col <= patch_cols)
    side = jnp.where(col < 0, nodes + row, nodes + patch_rows + row)
    inner = jnp.where((col < 0) | (col >= patch_cols), side, row * patch_cols + col)
    rim = nodes + 2 * patch_rows
    near_index = jnp.where(
        row < 0, rim + col + 1, jnp.where(row >= patch_rows, rim + RIM + col + 1, inner)
    )
    no_row = rim + patch_cols + 2
    near_index = jnp.where(is_near, near_index, no_row)
    src_lat, src_lon = send_row // patch_rows, send_col // patch_cols
    src_core, core = src_lat % 2, lat_index % 2
    at_x = ring_place((src_lat // 2 - lat_index // 2) % 4, src_core)
    half = jnp.where(src_core == core, 0, 1)
    within = send_row % patch_rows // 4 * (patch_cols // 4) + send_col % patch_cols // 4
    per = patch_rows // 4 * (patch_cols // 4)
    far_index = ((half * 4 + at_x) * lon_count + src_lon) * per + within
    far_list, far_count = far_lists((receiver >= 0) & ~is_near, far_index, steps)
    recv_rows = receiver.reshape(steps, GROUP, BLK)
    lives = jnp.sum((receiver >= 0).astype(jnp.int32).reshape(blocks, BLK), 1)

    pre, node_first = early_call(
        near_index, block_tile, near_pieces, edge_latent, recv_rows, own_rows, w_first, w_node_first
    )
    ahead, pre = lax.optimization_barrier((ahead, pre))
    across = move(ahead, "x", (1, -1))
    across, far_list, far_count = lax.optimization_barrier((across, far_list, far_count))
    halves = [own, ahead, behind, across]
    far_pieces = halves + [other_core(piece) for piece in halves]
    edge_out, node_out = late_call(
        far_list,
        far_count,
        block_tile,
        lives,
        far_pieces,
        pre,
        edge_latent,
        receiver,
        node_first,
        own_rows,
        w_first,
        w_second,
        edge_gain,
        w_node_first,
        w_node_second,
        node_gain,
    )
    return node_out.reshape(patch_rows, patch_cols, features), edge_out


def solution(mesh):
    return jax.shard_map(
        per_device,
        mesh=mesh,
        in_specs=(
            P("lat", "lon", None),
            P(("lat", "lon"), None),
            P(("lat", "lon")),
            P(("lat", "lon")),
            P(("lat", "lon")),
            P(),
            P(),
            P(),
            P(),
            P(),
            P(),
        ),
        out_specs=(P("lat", "lon", None), P(("lat", "lon"), None)),
        check_vma=False,
    )
```

```python
import jax
import jax.numpy as jnp
from jax import lax
from jax.experimental import pallas as pl
from jax.experimental.pallas import tpu as pltpu
from jax.sharding import PartitionSpec as P

F = 512
BLK = 128
GROUP = 4
ROWS = GROUP * BLK
RIMS = 4
FAR = 8
VMEM = 56 << 20
BF = jnp.bfloat16
F32 = jnp.float32


def device_of(x, c, y, z):
    return (x % 4 * 2 + c) * 16 + y % 4 * 4 + z % 4


def shift(axis, by_core):
    pairs = []
    for x in range(4):
        for c in range(2):
            for y in range(4):
                for z in range(4):
                    to = {"x": x, "y": y, "z": z}
                    to[axis] += by_core[c]
                    pairs.append((device_of(x, c, y, z), device_of(to["x"], c, to["y"], to["z"])))
    return pairs


def other_core(value):
    pairs = [
        (device_of(x, c, y, z), device_of(x, 1 - c, y, z))
        for x in range(4)
        for c in range(2)
        for y in range(4)
        for z in range(4)
    ]
    return lax.ppermute(value, ("lat", "lon"), pairs)


def move(value, axis, by_core):
    return lax.ppermute(value, ("lat", "lon"), shift(axis, by_core))


def ring_place(offset, core):
    near = jnp.where((offset == 1) == (core == 1), 1, 2)
    return jnp.where(offset == 0, 0, jnp.where(offset == 2, 3, near))


def silu(v):
    half = 0.5 * v
    return half + half * jnp.tanh(half)


def normed(values, gain):
    centred = values - jnp.mean(values, -1, keepdims=True)
    spread = jnp.mean(centred * centred, -1, keepdims=True)
    return centred * lax.rsqrt(spread + 1e-05) * gain


def dot(a, b):
    return jnp.dot(a, b, preferred_element_type=F32)


def chosen(recv_row):
    return (lax.broadcasted_iota(jnp.int32, (BLK, BLK), 0) == recv_row).astype(BF)


def fetch(count, unroll, entry, table, sent):
    def body(i, carry):
        for u in range(unroll):
            slot, row = entry(i * unroll + u)
            sent[pl.ds(pl.multiple_of(slot * 4, 4), 4), :] = table[row].astype(F32)
        return carry

    lax.fori_loop(0, count, body, 0)


def sent_rows(sent, base=0):
    return jnp.concatenate(
        [sent[pl.ds(base * 4 + j, ROWS, stride=4), :].astype(BF) for j in range(4)], axis=1
    )


def load_table(pieces, table, sem):
    copies = []
    start = 0
    for i, piece in enumerate(pieces):
        rows = piece.shape[0]
        copies.append(pltpu.make_async_copy(piece, table.at[pl.ds(start, rows)], sem.at[i]))
        start += rows
    for copy in copies:
        copy.start()
    return copies


def coarse_kernel(node_ref, out_hbm, west_ref, east_ref, top_ref, bottom_ref, wide, tall, block, sem):
    nodes, sides, cols = node_ref.shape[0], west_ref.shape[0], top_ref.shape[0]
    per = block.shape[0]
    run = cols // 4
    starts = []
    at = 0
    for rows in (per, sides, sides, cols, cols):
        starts.append(at)
        at += rows
    for j in range(4):
        wide[j * nodes : (j + 1) * nodes, :] = node_ref[:, j * 128 : (j + 1) * 128].astype(F32)

    def take(start, count, j, first, stride):
        source = pl.ds(j * nodes + first, count, stride=stride)
        tall[pl.ds(start * 4 + j, count, stride=4), :] = wide[source, :]

    for j in range(4):
        for r in range(sides // 4):
            take(starts[0] + r * run, run, j, 4 * r * cols, 4)
        take(starts[1], sides, j, 0, cols)
        take(starts[2], sides, j, cols - 1, cols)
        take(starts[3], cols, j, 0, 1)
        take(starts[4], cols, j, nodes - cols, 1)
    outs = (block, west_ref, east_ref, top_ref, bottom_ref)
    for start, out in zip(starts, outs):
        for i in range(out.shape[0]):
            out[i] = tall[(start + i) * 4 : (start + i) * 4 + 4, :].astype(BF)
        if out is block:
            stores = [
                pltpu.make_async_copy(block, out_hbm.at[d], sem.at[d])
                for d in range(out_hbm.shape[0])
            ]
            for store in stores:
                store.start()
    for store in stores:
        store.wait()


def early_kernel(tiles, edge_ref, recv_ref, node_ref, we_ref, wr_ref, wn_ref, part_ref, nf_ref, got_ref):
    step = pl.program_id(0)

    @pl.when(step == 0)
    def _():
        nf_ref[...] = dot(node_ref[...], wn_ref[...])

    for k in range(GROUP):
        tile = pl.multiple_of(tiles[step * GROUP + k] * BLK, BLK)
        hot = chosen(recv_ref[k : k + 1, :])
        rows = lax.dot_general(
            hot,
            node_ref[pl.ds(tile, BLK), :],
            (((0,), (0,)), ((), ())),
            preferred_element_type=F32,
        )
        got_ref[k * BLK : (k + 1) * BLK, :] = rows.astype(BF)
    part_ref[...] = dot(edge_ref[...], we_ref[...]) + dot(got_ref[...], wr_ref[...])


def near_kernel(near_index, node_ref, *refs):
    rims = refs[:RIMS]
    part_ref, ws_ref, pre_ref, tall, sent = refs[RIMS:]
    nodes = node_ref.shape[0]
    step = pl.program_id(0)

    @pl.when(step == 0)
    def _():
        for j in range(4):
            tall[pl.ds(j, nodes, stride=4), :] = node_ref[:, j * 128 : (j + 1) * 128].astype(F32)
        at = nodes * 4
        for rim in rims:
            for i in range(rim.shape[0]):
                tall[at : at + 4, :] = rim[i].astype(F32)
                at += 4
        tall[at : at + 4, :] = jnp.zeros((4, 128), F32)

    def body(i, carry):
        for u in range(16):
            e = i * 16 + u
            row = near_index[step * ROWS + e]
            sent[pl.ds(pl.multiple_of(e * 4, 4), 4), :] = tall[
                pl.ds(pl.multiple_of(row * 4, 4), 4), :
            ]
        return carry

    lax.fori_loop(0, ROWS // 16, body, 0)
    pre_ref[...] = (part_ref[...] + dot(sent_rows(sent), ws_ref[...])).astype(BF)


def late_kernel(far_list, far_count, tiles, lives, *refs):
    pieces = refs[:FAR]
    (
        pre_hbm,
        edge_hbm,
        nf_hbm,
        node_hbm,
        w1_hbm,
        w2_hbm,
        wn_hbm,
        wn2_hbm,
        recv_ref,
        eg_ref,
        ng_ref,
        out_hbm,
        node_out_ref,
        table,
        sent,
        pre,
        edge,
        out,
        agg,
        nf,
        node,
        ws,
        w2,
        wn,
        wn2,
        sem,
        in_sem,
        out_sem,
    ) = refs[FAR:]
    steps = recv_ref.shape[0] // GROUP
    rows_of = lambda g: pl.ds(g * ROWS, ROWS)
    copies = load_table(pieces, table, sem)
    first = [
        pltpu.make_async_copy(w1_hbm.at[pl.ds(F, F)], ws, in_sem.at[0]),
        pltpu.make_async_copy(w2_hbm, w2, in_sem.at[1]),
    ]
    parts = []
    for g in range(steps):
        parts.append(
            [
                pltpu.make_async_copy(pre_hbm.at[rows_of(g)], pre.at[rows_of(g)], in_sem.at[6 + 2 * g]),
                pltpu.make_async_copy(edge_hbm.at[rows_of(g)], edge.at[rows_of(g)], in_sem.at[7 + 2 * g]),
            ]
        )
    last = [
        pltpu.make_async_copy(nf_hbm, nf, in_sem.at[2]),
        pltpu.make_async_copy(node_hbm, node, in_sem.at[3]),
        pltpu.make_async_copy(wn_hbm.at[pl.ds(F, F)], wn, in_sem.at[4]),
        pltpu.make_async_copy(wn2_hbm, wn2, in_sem.at[5]),
    ]
    for copy in first + sum(parts, []) + last:
        copy.start()
    sent[...] = jnp.zeros_like(sent)
    agg[...] = jnp.zeros_like(agg)
    for copy in copies:
        copy.wait()

    for g in range(steps):

        def entry(i):
            packed = far_list[g * ROWS + i]
            return packed & 4095, packed >> 12

        fetch((far_count[g] + 7) >> 3, 8, entry, table, sent)
    for copy in first:
        copy.wait()
    place = lax.broadcasted_iota(jnp.int32, (BLK, F), 0)
    stores = []
    for g in range(steps):
        for copy in parts[g]:
            copy.wait()
        base = g * ROWS
        total = pre[rows_of(g), :].astype(F32) + dot(sent_rows(sent, base), ws[...])
        message = normed(dot(silu(total).astype(BF), w2[...]), eg_ref[...]).astype(BF)
        for k in range(GROUP):
            b = g * GROUP + k
            part = message[k * BLK : (k + 1) * BLK, :]
            at = pl.ds(base + k * BLK, BLK)
            live = place < lives[b]
            out[at, :] = jnp.where(
                live, edge[at, :].astype(F32) + part.astype(F32), 0.0
            ).astype(BF)
            tile = pl.multiple_of(tiles[b] * BLK, BLK)
            agg[pl.ds(tile, BLK), :] += dot(chosen(recv_ref[b : b + 1, :]), part)
        store = pltpu.make_async_copy(out.at[rows_of(g)], out_hbm.at[rows_of(g)], out_sem.at[g])
        store.start()
        stores.append(store)
    for copy in last:
        copy.wait()
    first_sum = nf[...] + dot(agg[...].astype(BF), wn[...])
    second = dot(silu(first_sum).astype(BF), wn2[...])
    node_out_ref[...] = (node[...].astype(F32) + normed(second, ng_ref[...])).astype(BF)
    for store in stores:
        store.wait()


def far_lists(is_far, far_index, steps):
    place = jnp.arange(ROWS, dtype=jnp.int32)
    slots = steps * ROWS
    far = is_far.reshape(steps, ROWS)
    flag = far.astype(jnp.int32)
    before = place[:, None] > place[None, :]
    rank = jnp.sum(jnp.where(before[None], flag[:, None, :], 0), 2)
    packed = (far_index * 4096 + jnp.arange(slots, dtype=jnp.int32) - slots).reshape(steps, ROWS)
    hit = (rank[:, None, :] == place[None, :, None]) & far[:, None, :]
    return (slots + jnp.sum(jnp.where(hit, packed[:, None, :], 0), 2)).reshape(-1), jnp.sum(flag, 1)


def specs():
    whole = lambda shape: pl.BlockSpec(shape, lambda i, *_: (0,) * len(shape))
    part = pl.BlockSpec((ROWS, F), lambda i, *_: (i, 0))
    recv_spec = pl.BlockSpec((None, GROUP, BLK), lambda i, *_: (i, 0, 0))
    weight = lambda k: pl.BlockSpec((F, F), lambda i, *_: (k, 0))
    anywhere = pl.BlockSpec(memory_space=pl.ANY)
    return whole, part, recv_spec, weight, anywhere


def early_call(block_tile, edge_latent, recv_rows, own_rows, w_first, w_node_first):
    whole, part, recv_spec, weight, anywhere = specs()
    blocks, nodes = block_tile.shape[0], own_rows.shape[0]
    return pl.pallas_call(
        early_kernel,
        name="early",
        grid_spec=pltpu.PrefetchScalarGridSpec(
            num_scalar_prefetch=1,
            grid=(blocks // GROUP,),
            in_specs=[part, recv_spec, whole((nodes, F)), weight(0), weight(2), weight(0)],
            out_specs=[part, whole((nodes, F))],
            scratch_shapes=[pltpu.VMEM((ROWS, F), BF)],
        ),
        out_shape=[
            jax.ShapeDtypeStruct((blocks * BLK, F), F32),
            jax.ShapeDtypeStruct((nodes, F), F32),
        ],
        compiler_params=pltpu.CompilerParams(vmem_limit_bytes=VMEM),
        cost_estimate=pl.CostEstimate(
            flops=3 * 10**9, bytes_accessed=10 * 10**6, transcendentals=0
        ),
    )(block_tile, edge_latent, recv_rows, own_rows, w_first, w_first, w_node_first)


def near_call(near_index, own_rows, rims, partial, w_first):
    whole, part, recv_spec, weight, anywhere = specs()
    slots, nodes = partial.shape[0], own_rows.shape[0]
    near_rows = nodes + sum(rim.shape[0] for rim in rims) + 1
    return pl.pallas_call(
        near_kernel,
        name="near",
        grid_spec=pltpu.PrefetchScalarGridSpec(
            num_scalar_prefetch=1,
            grid=(slots // ROWS,),
            in_specs=[whole((nodes, F))] + [whole(rim.shape) for rim in rims] + [part, weight(1)],
            out_specs=part,
            scratch_shapes=[
                pltpu.VMEM((near_rows * 4 + 4, 128), F32),
                pltpu.VMEM((ROWS * 4, 128), F32),
            ],
        ),
        out_shape=jax.ShapeDtypeStruct((slots, F), BF),
        compiler_params=pltpu.CompilerParams(vmem_limit_bytes=VMEM),
        cost_estimate=pl.CostEstimate(
            flops=2 * 10**9, bytes_accessed=8 * 10**6, transcendentals=0
        ),
    )(near_index, own_rows, *rims, partial, w_first)


def late_call(
    far_list,
    far_count,
    block_tile,
    lives,
    far_pieces,
    pre,
    edge_latent,
    receiver,
    node_first,
    own_rows,
    w_first,
    w_second,
    edge_gain,
    w_node_first,
    w_node_second,
    node_gain,
):
    blocks, nodes = block_tile.shape[0], own_rows.shape[0]
    slots, steps = blocks * BLK, blocks // GROUP
    far_rows = sum(piece.shape[0] for piece in far_pieces)
    anywhere = pl.BlockSpec(memory_space=pl.ANY)
    local = pl.BlockSpec(memory_space=pltpu.VMEM)
    scalars = pl.BlockSpec(memory_space=pltpu.SMEM)
    square = pltpu.VMEM((F, F), BF)
    return pl.pallas_call(
        late_kernel,
        name="late",
        in_specs=[scalars] * 4 + [anywhere] * (FAR + 8) + [local] * 3,
        out_specs=[anywhere, local],
        scratch_shapes=[
            pltpu.VMEM((far_rows, 4, 128), BF),
            pltpu.VMEM((slots * 4 + 32, 128), F32),
            pltpu.VMEM((slots, F), BF),
            pltpu.VMEM((slots, F), BF),
            pltpu.VMEM((slots, F), BF),
            pltpu.VMEM((nodes, F), F32),
            pltpu.VMEM((nodes, F), F32),
            pltpu.VMEM((nodes, F), BF),
            square,
            square,
            square,
            square,
            pltpu.SemaphoreType.DMA((FAR,)),
            pltpu.SemaphoreType.DMA((6 + 2 * steps,)),
            pltpu.SemaphoreType.DMA((steps,)),
        ],
        out_shape=[
            jax.ShapeDtypeStruct((slots, F), BF),
            jax.ShapeDtypeStruct((nodes, F), BF),
        ],
        compiler_params=pltpu.CompilerParams(vmem_limit_bytes=VMEM),
        cost_estimate=pl.CostEstimate(
            flops=4 * 10**9, bytes_accessed=14 * 10**6, transcendentals=2 * 10**6
        ),
    )(
        far_list,
        far_count,
        block_tile,
        lives,
        *far_pieces,
        pre,
        edge_latent,
        node_first,
        own_rows,
        w_first,
        w_second,
        w_node_first,
        w_node_second,
        receiver.reshape(blocks, BLK),
        edge_gain.reshape(1, F),
        node_gain.reshape(1, F),
    )


def per_device(
    node_latent,
    edge_latent,
    sender,
    receiver,
    block_tile,
    w_first,
    w_second,
    edge_gain,
    w_node_first,
    w_node_second,
    node_gain,
):
    patch_rows, patch_cols, features = node_latent.shape
    lat_index = lax.axis_index("lat")
    lon_index = lax.axis_index("lon")
    lat_count, lon_count = lax.axis_size("lat"), lax.axis_size("lon")
    grid_cols = patch_cols * lon_count
    blocks = block_tile.shape[0]
    steps = blocks // GROUP
    nodes = patch_rows * patch_cols
    own_rows = node_latent.reshape(nodes, features)
    lanes = lambda a: a.reshape(-1, 4, 128)

    right = [(i, (i + 1) % lon_count) for i in range(lon_count)]
    left = [(j, i) for i, j in right]
    up = [(i, i + 1) for i in range(lat_count - 1)]
    down = [(j, i) for i, j in up]

    per = patch_rows // 4 * (patch_cols // 4)
    lane_rows = lambda rows: jax.ShapeDtypeStruct((rows, 4, 128), BF)
    copies, first_col, last_col, top, bottom = pl.pallas_call(
        coarse_kernel,
        name="coarse",
        in_specs=[pl.BlockSpec(memory_space=pltpu.VMEM)],
        out_specs=[pl.BlockSpec(memory_space=pl.ANY)] + [pl.BlockSpec(memory_space=pltpu.VMEM)] * 4,
        scratch_shapes=[
            pltpu.VMEM((nodes * 4, 128), F32),
            pltpu.VMEM((4 * (per + 2 * patch_rows + 2 * patch_cols), 128), F32),
            pltpu.VMEM((per, 4, 128), BF),
            pltpu.SemaphoreType.DMA((lon_count,)),
        ],
        out_shape=[
            jax.ShapeDtypeStruct((lon_count, per, 4, 128), BF),
            lane_rows(patch_rows),
            lane_rows(patch_rows),
            lane_rows(patch_cols),
            lane_rows(patch_cols),
        ],
        compiler_params=pltpu.CompilerParams(vmem_limit_bytes=VMEM),
    )(own_rows)
    west = lax.ppermute(last_col, "lon", right)
    east = lax.ppermute(first_col, "lon", left)
    plane = lanes(lax.all_to_all(copies, "lon", split_axis=0, concat_axis=0, tiled=True))
    wide = lambda r, rows: jnp.concatenate([west[r : r + 1], rows, east[r : r + 1]], 0)
    north = lax.ppermute(wide(patch_rows - 1, bottom), "lat", up)
    south = lax.ppermute(wide(0, top), "lat", down)
    recv_rows = receiver.reshape(steps, GROUP, BLK)
    copies, edges = lax.optimization_barrier((copies, edge_latent))
    partial, node_first = early_call(
        block_tile, edges, recv_rows, own_rows, w_first, w_node_first
    )
    plane, north, south, partial = lax.optimization_barrier((plane, north, south, partial))

    ahead, behind = move(plane, "x", (1, -1)), move(plane, "x", (-1, 1))
    plane_other = other_core(plane)

    senders = jnp.maximum(sender, 0)
    send_row = senders // grid_cols
    send_col = senders % grid_cols
    row = send_row - lat_index * patch_rows
    col = (send_col - lon_index * patch_cols + 1) % grid_cols - 1
    is_near = (row >= -1) & (row <= patch_rows) & (col <= patch_cols)
    side = jnp.where(col < 0, nodes + row, nodes + patch_rows + row)
    inner = jnp.where((col < 0) | (col >= patch_cols), side, row * patch_cols + col)
    rim, span = nodes + 2 * patch_rows, patch_cols + 2
    near_index = jnp.where(
        row < 0, rim + col + 1, jnp.where(row >= patch_rows, rim + span + col + 1, inner)
    )
    near_index = jnp.where(is_near, near_index, rim + 2 * span)
    src_lat, src_lon = send_row // patch_rows, send_col // patch_cols
    src_core, core = src_lat % 2, lat_index % 2
    at_x = ring_place((src_lat // 2 - lat_index // 2) % 4, src_core)
    half = jnp.where(src_core == core, 0, 1)
    within = send_row % patch_rows // 4 * (patch_cols // 4) + send_col % patch_cols // 4
    far_index = ((half * 4 + at_x) * lon_count + src_lon) * per + within
    far_list, far_count = far_lists((receiver >= 0) & ~is_near, far_index, steps)
    lives = jnp.sum((receiver >= 0).astype(jnp.int32).reshape(blocks, BLK), 1)

    rims = [west, east, north, south]
    pre = near_call(near_index, own_rows, rims, partial, w_first)
    ahead, pre = lax.optimization_barrier((ahead, pre))
    across = move(ahead, "x", (1, -1))
    across, far_list, far_count, lives = lax.optimization_barrier(
        (across, far_list, far_count, lives)
    )
    far_pieces = [plane, ahead, behind, across, plane_other]
    far_pieces += [other_core(piece) for piece in (ahead, behind, across)]
    edge_out, node_out = late_call(
        far_list,
        far_count,
        block_tile,
        lives,
        far_pieces,
        pre,
        edge_latent,
        receiver,
        node_first,
        own_rows,
        w_first,
        w_second,
        edge_gain,
        w_node_first,
        w_node_second,
        node_gain,
    )
    return node_out.reshape(patch_rows, patch_cols, features), edge_out


def solution(mesh):
    return jax.shard_map(
        per_device,
        mesh=mesh,
        in_specs=(
            P("lat", "lon", None),
            P(("lat", "lon"), None),
            P(("lat", "lon")),
            P(("lat", "lon")),
            P(("lat", "lon")),
            P(),
            P(),
            P(),
            P(),
            P(),
            P(),
        ),
        out_specs=(P("lat", "lon", None), P(("lat", "lon"), None)),
        check_vma=False,
    )
```

```python
import jax
import jax.numpy as jnp
from jax import lax
from jax.experimental import pallas as pl
from jax.experimental.pallas import tpu as pltpu
from jax.sharding import PartitionSpec as P

F = 512
BLK = 128
GROUP = 4
ROWS = GROUP * BLK
RIMS = 4
FAR = 8
VMEM = 56 << 20
BF = jnp.bfloat16
F32 = jnp.float32


def device_of(x, c, y, z):
    return (x % 4 * 2 + c) * 16 + y % 4 * 4 + z % 4


def shift(axis, by_core):
    pairs = []
    for x in range(4):
        for c in range(2):
            for y in range(4):
                for z in range(4):
                    to = {"x": x, "y": y, "z": z}
                    to[axis] += by_core[c]
                    pairs.append((device_of(x, c, y, z), device_of(to["x"], c, to["y"], to["z"])))
    return pairs


def other_core(value):
    pairs = [
        (device_of(x, c, y, z), device_of(x, 1 - c, y, z))
        for x in range(4)
        for c in range(2)
        for y in range(4)
        for z in range(4)
    ]
    return lax.ppermute(value, ("lat", "lon"), pairs)


def move(value, axis, by_core):
    return lax.ppermute(value, ("lat", "lon"), shift(axis, by_core))


def ring_place(offset, core):
    near = jnp.where((offset == 1) == (core == 1), 1, 2)
    return jnp.where(offset == 0, 0, jnp.where(offset == 2, 3, near))


def silu(v):
    half = 0.5 * v
    return half + half * jnp.tanh(half)


def normed(values, gain):
    centred = values - jnp.mean(values, -1, keepdims=True)
    spread = jnp.mean(centred * centred, -1, keepdims=True)
    return centred * lax.rsqrt(spread + 1e-05) * gain


def dot(a, b):
    return jnp.dot(a, b, preferred_element_type=F32)


def chosen(recv_row):
    return (lax.broadcasted_iota(jnp.int32, (BLK, BLK), 0) == recv_row).astype(BF)


def fetch(count, unroll, entry, table, sent):
    def body(i, carry):
        for u in range(unroll):
            slot, row = entry(i * unroll + u)
            sent[pl.ds(pl.multiple_of(slot * 4, 4), 4), :] = table[row].astype(F32)
        return carry

    lax.fori_loop(0, count, body, 0)


def sent_rows(sent, base=0):
    return jnp.concatenate(
        [sent[pl.ds(base * 4 + j, ROWS, stride=4), :].astype(BF) for j in range(4)], axis=1
    )


def load_table(pieces, table, sem):
    copies = []
    start = 0
    for i, piece in enumerate(pieces):
        rows = piece.shape[0]
        copies.append(pltpu.make_async_copy(piece, table.at[pl.ds(start, rows)], sem.at[i]))
        start += rows
    for copy in copies:
        copy.start()
    return copies


def coarse_kernel(node_ref, out_hbm, west_ref, east_ref, top_ref, bottom_ref, wide, tall, block, sem):
    nodes, sides, cols = node_ref.shape[0], west_ref.shape[0], top_ref.shape[0]
    per = block.shape[0]
    run = cols // 4
    starts = []
    at = 0
    for rows in (per, sides, sides, cols, cols):
        starts.append(at)
        at += rows
    for j in range(4):
        wide[j * nodes : (j + 1) * nodes, :] = node_ref[:, j * 128 : (j + 1) * 128].astype(F32)

    def take(start, count, j, first, stride):
        source = pl.ds(j * nodes + first, count, stride=stride)
        tall[pl.ds(start * 4 + j, count, stride=4), :] = wide[source, :]

    for j in range(4):
        for r in range(sides // 4):
            take(starts[0] + r * run, run, j, 4 * r * cols, 4)
        take(starts[1], sides, j, 0, cols)
        take(starts[2], sides, j, cols - 1, cols)
        take(starts[3], cols, j, 0, 1)
        take(starts[4], cols, j, nodes - cols, 1)
    outs = (block, west_ref, east_ref, top_ref, bottom_ref)
    for start, out in zip(starts, outs):
        for i in range(out.shape[0]):
            out[i] = tall[(start + i) * 4 : (start + i) * 4 + 4, :].astype(BF)
        if out is block:
            stores = [
                pltpu.make_async_copy(block, out_hbm.at[d], sem.at[d])
                for d in range(out_hbm.shape[0])
            ]
            for store in stores:
                store.start()
    for store in stores:
        store.wait()


def early_kernel(tiles, edge_ref, recv_ref, node_ref, we_ref, wr_ref, wn_ref, part_ref, nf_ref, got_ref):
    step = pl.program_id(0)

    @pl.when(step == 0)
    def _():
        nf_ref[...] = dot(node_ref[...], wn_ref[...])

    for k in range(GROUP):
        tile = pl.multiple_of(tiles[step * GROUP + k] * BLK, BLK)
        hot = chosen(recv_ref[k : k + 1, :])
        rows = lax.dot_general(
            hot,
            node_ref[pl.ds(tile, BLK), :],
            (((0,), (0,)), ((), ())),
            preferred_element_type=F32,
        )
        got_ref[k * BLK : (k + 1) * BLK, :] = rows.astype(BF)
    part_ref[...] = dot(edge_ref[...], we_ref[...]) + dot(got_ref[...], wr_ref[...])


def near_kernel(near_index, node_ref, *refs):
    rims = refs[:RIMS]
    part_ref, ws_ref, pre_ref, tall, sent = refs[RIMS:]
    nodes = node_ref.shape[0]
    step = pl.program_id(0)

    @pl.when(step == 0)
    def _():
        for j in range(4):
            tall[pl.ds(j, nodes, stride=4), :] = node_ref[:, j * 128 : (j + 1) * 128].astype(F32)
        at = nodes * 4
        for rim in rims:
            for i in range(rim.shape[0]):
                tall[at : at + 4, :] = rim[i].astype(F32)
                at += 4
        tall[at : at + 4, :] = jnp.zeros((4, 128), F32)

    def body(i, carry):
        for u in range(16):
            e = i * 16 + u
            row = near_index[step * ROWS + e]
            sent[pl.ds(pl.multiple_of(e * 4, 4), 4), :] = tall[
                pl.ds(pl.multiple_of(row * 4, 4), 4), :
            ]
        return carry

    lax.fori_loop(0, ROWS // 16, body, 0)
    pre_ref[...] = (part_ref[...] + dot(sent_rows(sent), ws_ref[...])).astype(BF)


def late_kernel(far_list, far_count, tiles, lives, *refs):
    pieces = refs[:FAR]
    (
        pre_hbm,
        edge_hbm,
        nf_hbm,
        node_hbm,
        w1_hbm,
        w2_hbm,
        wn_hbm,
        wn2_hbm,
        recv_ref,
        eg_ref,
        ng_ref,
        out_hbm,
        node_out_ref,
        table,
        sent,
        pre,
        edge,
        out,
        agg,
        nf,
        node,
        ws,
        w2,
        wn,
        wn2,
        sem,
        in_sem,
        out_sem,
    ) = refs[FAR:]
    steps = recv_ref.shape[0] // GROUP
    rows_of = lambda g: pl.ds(g * ROWS, ROWS)
    copies = load_table(pieces, table, sem)
    first = [
        pltpu.make_async_copy(w1_hbm.at[pl.ds(F, F)], ws, in_sem.at[0]),
        pltpu.make_async_copy(w2_hbm, w2, in_sem.at[1]),
    ]
    parts = []
    for g in range(steps):
        parts.append(
            [
                pltpu.make_async_copy(pre_hbm.at[rows_of(g)], pre.at[rows_of(g)], in_sem.at[6 + 2 * g]),
                pltpu.make_async_copy(edge_hbm.at[rows_of(g)], edge.at[rows_of(g)], in_sem.at[7 + 2 * g]),
            ]
        )
    last = [
        pltpu.make_async_copy(nf_hbm, nf, in_sem.at[2]),
        pltpu.make_async_copy(node_hbm, node, in_sem.at[3]),
        pltpu.make_async_copy(wn_hbm.at[pl.ds(F, F)], wn, in_sem.at[4]),
        pltpu.make_async_copy(wn2_hbm, wn2, in_sem.at[5]),
    ]
    for copy in first + sum(parts, []) + last:
        copy.start()
    sent[...] = jnp.zeros_like(sent)
    agg[...] = jnp.zeros_like(agg)
    for copy in copies:
        copy.wait()

    for g in range(steps):

        def entry(i):
            packed = far_list[g * ROWS + i]
            return packed & 4095, packed >> 12

        fetch((far_count[g] + 7) >> 3, 8, entry, table, sent)
    for copy in first:
        copy.wait()
    place = lax.broadcasted_iota(jnp.int32, (BLK, F), 0)
    stores = []
    for g in range(steps):
        for copy in parts[g]:
            copy.wait()
        base = g * ROWS
        total = pre[rows_of(g), :].astype(F32) + dot(sent_rows(sent, base), ws[...])
        message = normed(dot(silu(total).astype(BF), w2[...]), eg_ref[...]).astype(BF)
        for k in range(GROUP):
            b = g * GROUP + k
            part = message[k * BLK : (k + 1) * BLK, :]
            at = pl.ds(base + k * BLK, BLK)
            live = place < lives[b]
            out[at, :] = jnp.where(
                live, edge[at, :].astype(F32) + part.astype(F32), 0.0
            ).astype(BF)
            tile = pl.multiple_of(tiles[b] * BLK, BLK)
            agg[pl.ds(tile, BLK), :] += dot(chosen(recv_ref[b : b + 1, :]), part)
        store = pltpu.make_async_copy(out.at[rows_of(g)], out_hbm.at[rows_of(g)], out_sem.at[g])
        store.start()
        stores.append(store)
    for copy in last:
        copy.wait()
    first_sum = nf[...] + dot(agg[...].astype(BF), wn[...])
    second = dot(silu(first_sum).astype(BF), wn2[...])
    node_out_ref[...] = (node[...].astype(F32) + normed(second, ng_ref[...])).astype(BF)
    for store in stores:
        store.wait()


def far_lists(is_far, far_index, steps):
    place = jnp.arange(ROWS, dtype=jnp.int32)
    slots = steps * ROWS
    far = is_far.reshape(steps, ROWS)
    flag = far.astype(jnp.int32)
    before = place[:, None] > place[None, :]
    rank = jnp.sum(jnp.where(before[None], flag[:, None, :], 0), 2)
    packed = (far_index * 4096 + jnp.arange(slots, dtype=jnp.int32) - slots).reshape(steps, ROWS)
    hit = (rank[:, None, :] == place[None, :, None]) & far[:, None, :]
    return (slots + jnp.sum(jnp.where(hit, packed[:, None, :], 0), 2)).reshape(-1), jnp.sum(flag, 1)


def specs():
    whole = lambda shape: pl.BlockSpec(shape, lambda i, *_: (0,) * len(shape))
    part = pl.BlockSpec((ROWS, F), lambda i, *_: (i, 0))
    recv_spec = pl.BlockSpec((None, GROUP, BLK), lambda i, *_: (i, 0, 0))
    weight = lambda k: pl.BlockSpec((F, F), lambda i, *_: (k, 0))
    anywhere = pl.BlockSpec(memory_space=pl.ANY)
    return whole, part, recv_spec, weight, anywhere


def early_call(block_tile, edge_latent, recv_rows, own_rows, w_first, w_node_first):
    whole, part, recv_spec, weight, anywhere = specs()
    blocks, nodes = block_tile.shape[0], own_rows.shape[0]
    return pl.pallas_call(
        early_kernel,
        name="early",
        grid_spec=pltpu.PrefetchScalarGridSpec(
            num_scalar_prefetch=1,
            grid=(blocks // GROUP,),
            in_specs=[part, recv_spec, whole((nodes, F)), weight(0), weight(2), weight(0)],
            out_specs=[part, whole((nodes, F))],
            scratch_shapes=[pltpu.VMEM((ROWS, F), BF)],
        ),
        out_shape=[
            jax.ShapeDtypeStruct((blocks * BLK, F), F32),
            jax.ShapeDtypeStruct((nodes, F), F32),
        ],
        compiler_params=pltpu.CompilerParams(vmem_limit_bytes=VMEM),
        cost_estimate=pl.CostEstimate(
            flops=3 * 10**9, bytes_accessed=10 * 10**6, transcendentals=0
        ),
    )(block_tile, edge_latent, recv_rows, own_rows, w_first, w_first, w_node_first)


def near_call(near_index, own_rows, rims, partial, w_first):
    whole, part, recv_spec, weight, anywhere = specs()
    slots, nodes = partial.shape[0], own_rows.shape[0]
    near_rows = nodes + sum(rim.shape[0] for rim in rims) + 1
    return pl.pallas_call(
        near_kernel,
        name="near",
        grid_spec=pltpu.PrefetchScalarGridSpec(
            num_scalar_prefetch=1,
            grid=(slots // ROWS,),
            in_specs=[whole((nodes, F))] + [whole(rim.shape) for rim in rims] + [part, weight(1)],
            out_specs=part,
            scratch_shapes=[
                pltpu.VMEM((near_rows * 4 + 4, 128), F32),
                pltpu.VMEM((ROWS * 4, 128), F32),
            ],
        ),
        out_shape=jax.ShapeDtypeStruct((slots, F), BF),
        compiler_params=pltpu.CompilerParams(vmem_limit_bytes=VMEM),
        cost_estimate=pl.CostEstimate(
            flops=2 * 10**9, bytes_accessed=8 * 10**6, transcendentals=0
        ),
    )(near_index, own_rows, *rims, partial, w_first)


def late_call(
    far_list,
    far_count,
    block_tile,
    lives,
    far_pieces,
    pre,
    edge_latent,
    receiver,
    node_first,
    own_rows,
    w_first,
    w_second,
    edge_gain,
    w_node_first,
    w_node_second,
    node_gain,
):
    blocks, nodes = block_tile.shape[0], own_rows.shape[0]
    slots, steps = blocks * BLK, blocks // GROUP
    far_rows = sum(piece.shape[0] for piece in far_pieces)
    anywhere = pl.BlockSpec(memory_space=pl.ANY)
    local = pl.BlockSpec(memory_space=pltpu.VMEM)
    scalars = pl.BlockSpec(memory_space=pltpu.SMEM)
    square = pltpu.VMEM((F, F), BF)
    return pl.pallas_call(
        late_kernel,
        name="late",
        in_specs=[scalars] * 4 + [anywhere] * (FAR + 8) + [local] * 3,
        out_specs=[anywhere, local],
        scratch_shapes=[
            pltpu.VMEM((far_rows, 4, 128), BF),
            pltpu.VMEM((slots * 4 + 32, 128), F32),
            pltpu.VMEM((slots, F), BF),
            pltpu.VMEM((slots, F), BF),
            pltpu.VMEM((slots, F), BF),
            pltpu.VMEM((nodes, F), F32),
            pltpu.VMEM((nodes, F), F32),
            pltpu.VMEM((nodes, F), BF),
            square,
            square,
            square,
            square,
            pltpu.SemaphoreType.DMA((FAR,)),
            pltpu.SemaphoreType.DMA((6 + 2 * steps,)),
            pltpu.SemaphoreType.DMA((steps,)),
        ],
        out_shape=[
            jax.ShapeDtypeStruct((slots, F), BF),
            jax.ShapeDtypeStruct((nodes, F), BF),
        ],
        compiler_params=pltpu.CompilerParams(vmem_limit_bytes=VMEM),
        cost_estimate=pl.CostEstimate(
            flops=4 * 10**9, bytes_accessed=14 * 10**6, transcendentals=2 * 10**6
        ),
    )(
        far_list,
        far_count,
        block_tile,
        lives,
        *far_pieces,
        pre,
        edge_latent,
        node_first,
        own_rows,
        w_first,
        w_second,
        w_node_first,
        w_node_second,
        receiver.reshape(blocks, BLK),
        edge_gain.reshape(1, F),
        node_gain.reshape(1, F),
    )


def per_device(
    node_latent,
    edge_latent,
    sender,
    receiver,
    block_tile,
    w_first,
    w_second,
    edge_gain,
    w_node_first,
    w_node_second,
    node_gain,
):
    patch_rows, patch_cols, features = node_latent.shape
    lat_index = lax.axis_index("lat")
    lon_index = lax.axis_index("lon")
    lat_count, lon_count = lax.axis_size("lat"), lax.axis_size("lon")
    grid_cols = patch_cols * lon_count
    blocks = block_tile.shape[0]
    steps = blocks // GROUP
    nodes = patch_rows * patch_cols
    own_rows = node_latent.reshape(nodes, features)
    lanes = lambda a: a.reshape(-1, 4, 128)

    right = [(i, (i + 1) % lon_count) for i in range(lon_count)]
    left = [(j, i) for i, j in right]
    up = [(i, i + 1) for i in range(lat_count - 1)]
    down = [(j, i) for i, j in up]

    per = patch_rows // 4 * (patch_cols // 4)
    lane_rows = lambda rows: jax.ShapeDtypeStruct((rows, 4, 128), BF)
    copies, first_col, last_col, top, bottom = pl.pallas_call(
        coarse_kernel,
        name="coarse",
        in_specs=[pl.BlockSpec(memory_space=pltpu.VMEM)],
        out_specs=[pl.BlockSpec(memory_space=pl.ANY)] + [pl.BlockSpec(memory_space=pltpu.VMEM)] * 4,
        scratch_shapes=[
            pltpu.VMEM((nodes * 4, 128), F32),
            pltpu.VMEM((4 * (per + 2 * patch_rows + 2 * patch_cols), 128), F32),
            pltpu.VMEM((per, 4, 128), BF),
            pltpu.SemaphoreType.DMA((lon_count,)),
        ],
        out_shape=[
            jax.ShapeDtypeStruct((lon_count, per, 4, 128), BF),
            lane_rows(patch_rows),
            lane_rows(patch_rows),
            lane_rows(patch_cols),
            lane_rows(patch_cols),
        ],
        compiler_params=pltpu.CompilerParams(vmem_limit_bytes=VMEM),
    )(own_rows)
    senders = jnp.maximum(sender, 0)
    send_row = senders // grid_cols
    send_col = senders % grid_cols
    row = send_row - lat_index * patch_rows
    col = (send_col - lon_index * patch_cols + 1) % grid_cols - 1
    is_near = (row >= -1) & (row <= patch_rows) & (col <= patch_cols)
    side = jnp.where(col < 0, nodes + row, nodes + patch_rows + row)
    inner = jnp.where((col < 0) | (col >= patch_cols), side, row * patch_cols + col)
    rim, span = nodes + 2 * patch_rows, patch_cols + 2
    near_index = jnp.where(
        row < 0, rim + col + 1, jnp.where(row >= patch_rows, rim + span + col + 1, inner)
    )
    near_index = jnp.where(is_near, near_index, rim + 2 * span)
    src_lat, src_lon = send_row // patch_rows, send_col // patch_cols
    src_core, core = src_lat % 2, lat_index % 2
    at_x = ring_place((src_lat // 2 - lat_index // 2) % 4, src_core)
    half = jnp.where(src_core == core, 0, 1)
    within = send_row % patch_rows // 4 * (patch_cols // 4) + send_col % patch_cols // 4
    far_index = ((half * 4 + at_x) * lon_count + src_lon) * per + within
    far_list, far_count = far_lists((receiver >= 0) & ~is_near, far_index, steps)
    recv_rows = receiver.reshape(steps, GROUP, BLK)
    lives = jnp.sum((receiver >= 0).astype(jnp.int32).reshape(blocks, BLK), 1)

    west = lax.ppermute(last_col, "lon", right)
    east = lax.ppermute(first_col, "lon", left)
    plane = lanes(lax.all_to_all(copies, "lon", split_axis=0, concat_axis=0, tiled=True))
    wide = lambda r, rows: jnp.concatenate([west[r : r + 1], rows, east[r : r + 1]], 0)
    north = lax.ppermute(wide(patch_rows - 1, bottom), "lat", up)
    south = lax.ppermute(wide(0, top), "lat", down)
    plane, north, south, edges, near_index, far_list, far_count, lives = lax.optimization_barrier(
        (plane, north, south, edge_latent, near_index, far_list, far_count, lives)
    )

    ahead, behind = move(plane, "x", (1, -1)), move(plane, "x", (-1, 1))
    plane_other = other_core(plane)
    partial, node_first = early_call(
        block_tile, edges, recv_rows, own_rows, w_first, w_node_first
    )
    ahead, partial = lax.optimization_barrier((ahead, partial))
    across = move(ahead, "x", (1, -1))
    rims = [west, east, north, south]
    pre = near_call(near_index, own_rows, rims, partial, w_first)
    across, pre = lax.optimization_barrier((across, pre))
    far_pieces = [plane, ahead, behind, across, plane_other]
    far_pieces += [other_core(piece) for piece in (ahead, behind, across)]
    edge_out, node_out = late_call(
        far_list,
        far_count,
        block_tile,
        lives,
        far_pieces,
        pre,
        edge_latent,
        receiver,
        node_first,
        own_rows,
        w_first,
        w_second,
        edge_gain,
        w_node_first,
        w_node_second,
        node_gain,
    )
    return node_out.reshape(patch_rows, patch_cols, features), edge_out


def solution(mesh):
    return jax.shard_map(
        per_device,
        mesh=mesh,
        in_specs=(
            P("lat", "lon", None),
            P(("lat", "lon"), None),
            P(("lat", "lon")),
            P(("lat", "lon")),
            P(("lat", "lon")),
            P(),
            P(),
            P(),
            P(),
            P(),
            P(),
        ),
        out_specs=(P("lat", "lon", None), P(("lat", "lon"), None)),
        check_vma=False,
    )
```

```python
import jax
import jax.numpy as jnp
from jax import lax
from jax.experimental import pallas as pl
from jax.experimental.pallas import tpu as pltpu
from jax.sharding import PartitionSpec as P

F = 512
BLK = 128
GROUP = 4
ROWS = GROUP * BLK
RIMS = 4
FAR = 8
VMEM = 56 << 20
BF = jnp.bfloat16
F32 = jnp.float32


def device_of(x, c, y, z):
    return (x % 4 * 2 + c) * 16 + y % 4 * 4 + z % 4


def shift(axis, by_core):
    pairs = []
    for x in range(4):
        for c in range(2):
            for y in range(4):
                for z in range(4):
                    to = {"x": x, "y": y, "z": z}
                    to[axis] += by_core[c]
                    pairs.append((device_of(x, c, y, z), device_of(to["x"], c, to["y"], to["z"])))
    return pairs


def other_core(value):
    pairs = [
        (device_of(x, c, y, z), device_of(x, 1 - c, y, z))
        for x in range(4)
        for c in range(2)
        for y in range(4)
        for z in range(4)
    ]
    return lax.ppermute(value, ("lat", "lon"), pairs)


def move(value, axis, by_core):
    return lax.ppermute(value, ("lat", "lon"), shift(axis, by_core))


def ring_place(offset, core):
    near = jnp.where((offset == 1) == (core == 1), 1, 2)
    return jnp.where(offset == 0, 0, jnp.where(offset == 2, 3, near))


def silu(v):
    half = 0.5 * v
    return half + half * jnp.tanh(half)


def normed(values, gain):
    centred = values - jnp.mean(values, -1, keepdims=True)
    spread = jnp.mean(centred * centred, -1, keepdims=True)
    return centred * lax.rsqrt(spread + 1e-05) * gain


def dot(a, b):
    return jnp.dot(a, b, preferred_element_type=F32)


def chosen(recv_row):
    return (lax.broadcasted_iota(jnp.int32, (BLK, BLK), 0) == recv_row).astype(BF)


def fetch(count, unroll, entry, table, sent):
    def body(i, carry):
        for u in range(unroll):
            slot, row = entry(i * unroll + u)
            sent[pl.ds(pl.multiple_of(slot * 4, 4), 4), :] = table[row].astype(F32)
        return carry

    lax.fori_loop(0, count, body, 0)


def sent_rows(sent, base=0):
    return jnp.concatenate(
        [sent[pl.ds(base * 4 + j, ROWS, stride=4), :].astype(BF) for j in range(4)], axis=1
    )


def load_table(pieces, table, sem):
    copies = []
    start = 0
    for i, piece in enumerate(pieces):
        rows = piece.shape[0]
        copies.append(pltpu.make_async_copy(piece, table.at[pl.ds(start, rows)], sem.at[i]))
        start += rows
    for copy in copies:
        copy.start()
    return copies


def coarse_kernel(node_ref, out_hbm, west_ref, east_ref, top_ref, bottom_ref, wide, tall, block, sem):
    nodes, sides, cols = node_ref.shape[0], west_ref.shape[0], top_ref.shape[0]
    per = block.shape[0]
    run = cols // 4
    starts = []
    at = 0
    for rows in (per, sides, sides, cols, cols):
        starts.append(at)
        at += rows
    for j in range(4):
        wide[j * nodes : (j + 1) * nodes, :] = node_ref[:, j * 128 : (j + 1) * 128].astype(F32)

    def take(start, count, j, first, stride):
        source = pl.ds(j * nodes + first, count, stride=stride)
        tall[pl.ds(start * 4 + j, count, stride=4), :] = wide[source, :]

    for j in range(4):
        for r in range(sides // 4):
            take(starts[0] + r * run, run, j, 4 * r * cols, 4)
        take(starts[1], sides, j, 0, cols)
        take(starts[2], sides, j, cols - 1, cols)
        take(starts[3], cols, j, 0, 1)
        take(starts[4], cols, j, nodes - cols, 1)
    outs = (block, west_ref, east_ref, top_ref, bottom_ref)
    for start, out in zip(starts, outs):
        for i in range(out.shape[0]):
            out[i] = tall[(start + i) * 4 : (start + i) * 4 + 4, :].astype(BF)
        if out is block:
            stores = [
                pltpu.make_async_copy(block, out_hbm.at[d], sem.at[d])
                for d in range(out_hbm.shape[0])
            ]
            for store in stores:
                store.start()
    for store in stores:
        store.wait()


def early_kernel(tiles, edge_ref, recv_ref, node_ref, we_ref, wr_ref, part_ref, got_ref):
    step = pl.program_id(0)

    for k in range(GROUP):
        tile = pl.multiple_of(tiles[step * GROUP + k] * BLK, BLK)
        hot = chosen(recv_ref[k : k + 1, :])
        rows = lax.dot_general(
            hot,
            node_ref[pl.ds(tile, BLK), :],
            (((0,), (0,)), ((), ())),
            preferred_element_type=F32,
        )
        got_ref[k * BLK : (k + 1) * BLK, :] = rows.astype(BF)
    total = dot(edge_ref[...], we_ref[...]) + dot(got_ref[...], wr_ref[...])
    part_ref[...] = total.astype(BF)


def near_kernel(near_index, node_ref, *refs):
    rims = refs[:RIMS]
    part_ref, ws_ref, pre_ref, tall, sent = refs[RIMS:]
    nodes = node_ref.shape[0]
    step = pl.program_id(0)

    @pl.when(step == 0)
    def _():
        for j in range(4):
            tall[pl.ds(j, nodes, stride=4), :] = node_ref[:, j * 128 : (j + 1) * 128].astype(F32)
        at = nodes * 4
        for rim in rims:
            for i in range(rim.shape[0]):
                tall[at : at + 4, :] = rim[i].astype(F32)
                at += 4
        tall[at : at + 4, :] = jnp.zeros((4, 128), F32)

    def body(i, carry):
        for u in range(16):
            e = i * 16 + u
            row = near_index[step * ROWS + e]
            sent[pl.ds(pl.multiple_of(e * 4, 4), 4), :] = tall[
                pl.ds(pl.multiple_of(row * 4, 4), 4), :
            ]
        return carry

    lax.fori_loop(0, ROWS // 16, body, 0)
    total = part_ref[...].astype(F32) + dot(sent_rows(sent), ws_ref[...])
    pre_ref[...] = total.astype(BF)


def late_kernel(far_list, far_count, tiles, lives, *refs):
    pieces = refs[:FAR]
    (
        pre_hbm,
        edge_hbm,
        node_hbm,
        w1_hbm,
        w2_hbm,
        wn_hbm,
        wn2_hbm,
        recv_ref,
        eg_ref,
        ng_ref,
        out_hbm,
        node_out_ref,
        table,
        sent,
        pre,
        edge,
        out,
        agg,
        node,
        ws,
        w2,
        wn,
        wn2,
        sem,
        in_sem,
        out_sem,
    ) = refs[FAR:]
    steps = recv_ref.shape[0] // GROUP
    rows_of = lambda g: pl.ds(g * ROWS, ROWS)
    copies = load_table(pieces, table, sem)
    first = [
        pltpu.make_async_copy(w1_hbm.at[pl.ds(F, F)], ws, in_sem.at[0]),
        pltpu.make_async_copy(w2_hbm, w2, in_sem.at[1]),
    ]
    parts = []
    for g in range(steps):
        parts.append(
            [
                pltpu.make_async_copy(pre_hbm.at[rows_of(g)], pre.at[rows_of(g)], in_sem.at[6 + 2 * g]),
                pltpu.make_async_copy(edge_hbm.at[rows_of(g)], edge.at[rows_of(g)], in_sem.at[7 + 2 * g]),
            ]
        )
    last = [
        pltpu.make_async_copy(node_hbm, node, in_sem.at[3]),
        pltpu.make_async_copy(wn_hbm, wn, in_sem.at[4]),
        pltpu.make_async_copy(wn2_hbm, wn2, in_sem.at[5]),
    ]
    for copy in first:
        copy.start()
    sent[...] = jnp.zeros_like(sent)
    agg[...] = jnp.zeros_like(agg)
    for copy in copies:
        copy.wait()
    for copy in sum(parts, []) + last:
        copy.start()

    for g in range(steps):

        def entry(i):
            packed = far_list[g * ROWS + i]
            return packed & 4095, packed >> 12

        fetch((far_count[g] + 15) >> 4, 16, entry, table, sent)
    for copy in first:
        copy.wait()
    place = lax.broadcasted_iota(jnp.int32, (BLK, F), 0)
    stores = []
    for g in range(steps):
        for copy in parts[g]:
            copy.wait()
        base = g * ROWS
        total = pre[rows_of(g), :].astype(F32) + dot(sent_rows(sent, base), ws[...])
        message = normed(dot(silu(total).astype(BF), w2[...]), eg_ref[...]).astype(BF)
        for k in range(GROUP):
            b = g * GROUP + k
            part = message[k * BLK : (k + 1) * BLK, :]
            at = pl.ds(base + k * BLK, BLK)
            live = place < lives[b]
            out[at, :] = jnp.where(
                live, edge[at, :].astype(F32) + part.astype(F32), 0.0
            ).astype(BF)
            tile = pl.multiple_of(tiles[b] * BLK, BLK)
            agg[pl.ds(tile, BLK), :] += dot(chosen(recv_ref[b : b + 1, :]), part)
        store = pltpu.make_async_copy(out.at[rows_of(g)], out_hbm.at[rows_of(g)], out_sem.at[g])
        store.start()
        stores.append(store)
    for copy in last:
        copy.wait()
    first_sum = dot(node[...], wn[:F, :]) + dot(agg[...].astype(BF), wn[F:, :])
    second = dot(silu(first_sum).astype(BF), wn2[...])
    node_out_ref[...] = (node[...].astype(F32) + normed(second, ng_ref[...])).astype(BF)
    for store in stores:
        store.wait()


def far_lists(is_far, far_index, steps):
    place = jnp.arange(ROWS, dtype=jnp.int32)
    slots = steps * ROWS
    far = is_far.reshape(steps, ROWS)
    flag = far.astype(jnp.int32)
    before = place[:, None] > place[None, :]
    rank = jnp.sum(jnp.where(before[None], flag[:, None, :], 0), 2)
    packed = (far_index * 4096 + jnp.arange(slots, dtype=jnp.int32) - slots).reshape(steps, ROWS)
    hit = (rank[:, None, :] == place[None, :, None]) & far[:, None, :]
    return (slots + jnp.sum(jnp.where(hit, packed[:, None, :], 0), 2)).reshape(-1), jnp.sum(flag, 1)


def specs():
    whole = lambda shape: pl.BlockSpec(shape, lambda i, *_: (0,) * len(shape))
    part = pl.BlockSpec((ROWS, F), lambda i, *_: (i, 0))
    recv_spec = pl.BlockSpec((None, GROUP, BLK), lambda i, *_: (i, 0, 0))
    weight = lambda k: pl.BlockSpec((F, F), lambda i, *_: (k, 0))
    anywhere = pl.BlockSpec(memory_space=pl.ANY)
    return whole, part, recv_spec, weight, anywhere


def early_call(block_tile, edge_latent, recv_rows, own_rows, w_first):
    whole, part, recv_spec, weight, anywhere = specs()
    blocks, nodes = block_tile.shape[0], own_rows.shape[0]
    return pl.pallas_call(
        early_kernel,
        name="early",
        grid_spec=pltpu.PrefetchScalarGridSpec(
            num_scalar_prefetch=1,
            grid=(blocks // GROUP,),
            in_specs=[part, recv_spec, whole((nodes, F)), weight(0), weight(2)],
            out_specs=part,
            scratch_shapes=[pltpu.VMEM((ROWS, F), BF)],
        ),
        out_shape=jax.ShapeDtypeStruct((blocks * BLK, F), BF),
        compiler_params=pltpu.CompilerParams(vmem_limit_bytes=VMEM),
        cost_estimate=pl.CostEstimate(
            flops=3 * 10**9, bytes_accessed=10 * 10**6, transcendentals=0
        ),
    )(block_tile, edge_latent, recv_rows, own_rows, w_first, w_first)


def near_call(near_index, own_rows, rims, partial, w_first):
    whole, part, recv_spec, weight, anywhere = specs()
    slots, nodes = partial.shape[0], own_rows.shape[0]
    near_rows = nodes + sum(rim.shape[0] for rim in rims) + 1
    return pl.pallas_call(
        near_kernel,
        name="near",
        grid_spec=pltpu.PrefetchScalarGridSpec(
            num_scalar_prefetch=1,
            grid=(slots // ROWS,),
            in_specs=[whole((nodes, F))] + [whole(rim.shape) for rim in rims] + [part, weight(1)],
            out_specs=part,
            scratch_shapes=[
                pltpu.VMEM((near_rows * 4 + 4, 128), F32),
                pltpu.VMEM((ROWS * 4, 128), F32),
            ],
        ),
        out_shape=jax.ShapeDtypeStruct((slots, F), BF),
        compiler_params=pltpu.CompilerParams(vmem_limit_bytes=VMEM),
        cost_estimate=pl.CostEstimate(
            flops=2 * 10**9, bytes_accessed=8 * 10**6, transcendentals=0
        ),
    )(near_index, own_rows, *rims, partial, w_first)


def late_call(
    far_list,
    far_count,
    block_tile,
    lives,
    far_pieces,
    pre,
    edge_latent,
    receiver,
    own_rows,
    w_first,
    w_second,
    edge_gain,
    w_node_first,
    w_node_second,
    node_gain,
):
    blocks, nodes = block_tile.shape[0], own_rows.shape[0]
    slots, steps = blocks * BLK, blocks // GROUP
    far_rows = sum(piece.shape[0] for piece in far_pieces)
    anywhere = pl.BlockSpec(memory_space=pl.ANY)
    local = pl.BlockSpec(memory_space=pltpu.VMEM)
    scalars = pl.BlockSpec(memory_space=pltpu.SMEM)
    square = pltpu.VMEM((F, F), BF)
    return pl.pallas_call(
        late_kernel,
        name="late",
        in_specs=[scalars] * 4 + [anywhere] * (FAR + 7) + [local] * 3,
        out_specs=[anywhere, local],
        scratch_shapes=[
            pltpu.VMEM((far_rows, 4, 128), BF),
            pltpu.VMEM((slots * 4 + 32, 128), F32),
            pltpu.VMEM((slots, F), BF),
            pltpu.VMEM((slots, F), BF),
            pltpu.VMEM((slots, F), BF),
            pltpu.VMEM((nodes, F), F32),
            pltpu.VMEM((nodes, F), BF),
            square,
            square,
            pltpu.VMEM((2 * F, F), BF),
            square,
            pltpu.SemaphoreType.DMA((FAR,)),
            pltpu.SemaphoreType.DMA((6 + 2 * steps,)),
            pltpu.SemaphoreType.DMA((steps,)),
        ],
        out_shape=[
            jax.ShapeDtypeStruct((slots, F), BF),
            jax.ShapeDtypeStruct((nodes, F), BF),
        ],
        compiler_params=pltpu.CompilerParams(vmem_limit_bytes=VMEM),
        cost_estimate=pl.CostEstimate(
            flops=4 * 10**9, bytes_accessed=14 * 10**6, transcendentals=2 * 10**6
        ),
    )(
        far_list,
        far_count,
        block_tile,
        lives,
        *far_pieces,
        pre,
        edge_latent,
        own_rows,
        w_first,
        w_second,
        w_node_first,
        w_node_second,
        receiver.reshape(blocks, BLK),
        edge_gain.reshape(1, F),
        node_gain.reshape(1, F),
    )


def per_device(
    node_latent,
    edge_latent,
    sender,
    receiver,
    block_tile,
    w_first,
    w_second,
    edge_gain,
    w_node_first,
    w_node_second,
    node_gain,
):
    patch_rows, patch_cols, features = node_latent.shape
    lat_index = lax.axis_index("lat")
    lon_index = lax.axis_index("lon")
    lat_count, lon_count = lax.axis_size("lat"), lax.axis_size("lon")
    grid_cols = patch_cols * lon_count
    blocks = block_tile.shape[0]
    steps = blocks // GROUP
    nodes = patch_rows * patch_cols
    own_rows = node_latent.reshape(nodes, features)
    lanes = lambda a: a.reshape(-1, 4, 128)

    right = [(i, (i + 1) % lon_count) for i in range(lon_count)]
    left = [(j, i) for i, j in right]
    up = [(i, i + 1) for i in range(lat_count - 1)]
    down = [(j, i) for i, j in up]

    per = patch_rows // 4 * (patch_cols // 4)
    lane_rows = lambda rows: jax.ShapeDtypeStruct((rows, 4, 128), BF)
    copies, first_col, last_col, top, bottom = pl.pallas_call(
        coarse_kernel,
        name="coarse",
        in_specs=[pl.BlockSpec(memory_space=pltpu.VMEM)],
        out_specs=[pl.BlockSpec(memory_space=pl.ANY)] + [pl.BlockSpec(memory_space=pltpu.VMEM)] * 4,
        scratch_shapes=[
            pltpu.VMEM((nodes * 4, 128), F32),
            pltpu.VMEM((4 * (per + 2 * patch_rows + 2 * patch_cols), 128), F32),
            pltpu.VMEM((per, 4, 128), BF),
            pltpu.SemaphoreType.DMA((lon_count,)),
        ],
        out_shape=[
            jax.ShapeDtypeStruct((lon_count, per, 4, 128), BF),
            lane_rows(patch_rows),
            lane_rows(patch_rows),
            lane_rows(patch_cols),
            lane_rows(patch_cols),
        ],
        compiler_params=pltpu.CompilerParams(vmem_limit_bytes=VMEM),
    )(own_rows)
    senders = jnp.maximum(sender, 0)
    send_row = senders // grid_cols
    send_col = senders % grid_cols
    row = send_row - lat_index * patch_rows
    col = (send_col - lon_index * patch_cols + 1) % grid_cols - 1
    is_near = (row >= -1) & (row <= patch_rows) & (col <= patch_cols)
    side = jnp.where(col < 0, nodes + row, nodes + patch_rows + row)
    inner = jnp.where((col < 0) | (col >= patch_cols), side, row * patch_cols + col)
    rim, span = nodes + 2 * patch_rows, patch_cols + 2
    near_index = jnp.where(
        row < 0, rim + col + 1, jnp.where(row >= patch_rows, rim + span + col + 1, inner)
    )
    near_index = jnp.where(is_near, near_index, rim + 2 * span)
    src_lat, src_lon = send_row // patch_rows, send_col // patch_cols
    src_core, core = src_lat % 2, lat_index % 2
    at_x = ring_place((src_lat // 2 - lat_index // 2) % 4, src_core)
    half = jnp.where(src_core == core, 0, 1)
    within = send_row % patch_rows // 4 * (patch_cols // 4) + send_col % patch_cols // 4
    far_index = ((half * 4 + at_x) * lon_count + src_lon) * per + within
    far_list, far_count = far_lists((receiver >= 0) & ~is_near, far_index, steps)
    recv_rows = receiver.reshape(steps, GROUP, BLK)
    lives = jnp.sum((receiver >= 0).astype(jnp.int32).reshape(blocks, BLK), 1)

    west = lax.ppermute(last_col, "lon", right)
    east = lax.ppermute(first_col, "lon", left)
    plane = lanes(lax.all_to_all(copies, "lon", split_axis=0, concat_axis=0, tiled=True))
    wide = lambda r, rows: jnp.concatenate([west[r : r + 1], rows, east[r : r + 1]], 0)
    north = lax.ppermute(wide(patch_rows - 1, bottom), "lat", up)
    south = lax.ppermute(wide(0, top), "lat", down)
    plane, north, south, edges, near_index, far_list, far_count, lives = lax.optimization_barrier(
        (plane, north, south, edge_latent, near_index, far_list, far_count, lives)
    )

    ahead = move(plane, "x", (1, -1))
    plane_other = other_core(plane)
    partial = early_call(block_tile, edges, recv_rows, own_rows, w_first)
    later, partial = lax.optimization_barrier((plane, partial))
    behind = move(later, "x", (-1, 1))
    ahead, partial = lax.optimization_barrier((ahead, partial))
    across = move(ahead, "x", (1, -1))
    rims = [west, east, north, south]
    pre = near_call(near_index, own_rows, rims, partial, w_first)
    across, behind, pre = lax.optimization_barrier((across, behind, pre))
    far_pieces = [plane, ahead, behind, across, plane_other]
    far_pieces += [other_core(piece) for piece in (ahead, behind, across)]
    edge_out, node_out = late_call(
        far_list,
        far_count,
        block_tile,
        lives,
        far_pieces,
        pre,
        edge_latent,
        receiver,
        own_rows,
        w_first,
        w_second,
        edge_gain,
        w_node_first,
        w_node_second,
        node_gain,
    )
    return node_out.reshape(patch_rows, patch_cols, features), edge_out


def solution(mesh):
    return jax.shard_map(
        per_device,
        mesh=mesh,
        in_specs=(
            P("lat", "lon", None),
            P(("lat", "lon"), None),
            P(("lat", "lon")),
            P(("lat", "lon")),
            P(("lat", "lon")),
            P(),
            P(),
            P(),
            P(),
            P(),
            P(),
        ),
        out_specs=(P("lat", "lon", None), P(("lat", "lon"), None)),
        check_vma=False,
    )
```

```python
import jax
import jax.numpy as jnp
from jax import lax
from jax.experimental import pallas as pl
from jax.experimental.pallas import tpu as pltpu
from jax.sharding import PartitionSpec as P

F = 512
BLK = 128
GROUP = 4
ROWS = GROUP * BLK
RIMS = 4
FAR = 8
VMEM = 16 << 20
BF = jnp.bfloat16
F32 = jnp.float32


def device_of(x, c, y, z):
    return (x % 4 * 2 + c) * 16 + y % 4 * 4 + z % 4


def shift(axis, by_core):
    pairs = []
    for x in range(4):
        for c in range(2):
            for y in range(4):
                for z in range(4):
                    to = {"x": x, "y": y, "z": z}
                    to[axis] += by_core[c]
                    pairs.append((device_of(x, c, y, z), device_of(to["x"], c, to["y"], to["z"])))
    return pairs


def other_core(value):
    pairs = [
        (device_of(x, c, y, z), device_of(x, 1 - c, y, z))
        for x in range(4)
        for c in range(2)
        for y in range(4)
        for z in range(4)
    ]
    return lax.ppermute(value, ("lat", "lon"), pairs)


def move(value, axis, by_core):
    return lax.ppermute(value, ("lat", "lon"), shift(axis, by_core))


def ring_place(offset, core):
    near = jnp.where((offset == 1) == (core == 1), 1, 2)
    return jnp.where(offset == 0, 0, jnp.where(offset == 2, 3, near))


def silu(v):
    half = 0.5 * v
    return half + half * jnp.tanh(half)


def normed(values, gain):
    centred = values - jnp.mean(values, -1, keepdims=True)
    spread = jnp.mean(centred * centred, -1, keepdims=True)
    return centred * lax.rsqrt(spread + 1e-05) * gain


def dot(a, b):
    return jnp.dot(a, b, preferred_element_type=F32)


def chosen(recv_row):
    return (lax.broadcasted_iota(jnp.int32, (BLK, BLK), 0) == recv_row).astype(BF)


def fetch(count, unroll, entry, table, sent):
    def body(i, carry):
        for u in range(unroll):
            slot, row = entry(i * unroll + u)
            sent[pl.ds(pl.multiple_of(slot * 4, 4), 4), :] = table[row].astype(F32)
        return carry

    lax.fori_loop(0, count, body, 0)


def sent_rows(sent, base=0):
    return jnp.concatenate(
        [sent[pl.ds(base * 4 + j, ROWS, stride=4), :].astype(BF) for j in range(4)], axis=1
    )


def load_table(pieces, table, sem):
    copies = []
    start = 0
    for i, piece in enumerate(pieces):
        rows = piece.shape[0]
        copies.append(pltpu.make_async_copy(piece, table.at[pl.ds(start, rows)], sem.at[i]))
        start += rows
    for copy in copies:
        copy.start()
    return copies


def coarse_kernel(node_ref, out_hbm, west_ref, east_ref, top_ref, bottom_ref, wide, tall, block, sem):
    nodes, sides, cols = node_ref.shape[0], west_ref.shape[0], top_ref.shape[0]
    per = block.shape[0]
    run = cols // 4
    starts = []
    at = 0
    for rows in (per, sides, sides, cols, cols):
        starts.append(at)
        at += rows
    for j in range(4):
        wide[j * nodes : (j + 1) * nodes, :] = node_ref[:, j * 128 : (j + 1) * 128].astype(F32)

    def take(start, count, j, first, stride):
        source = pl.ds(j * nodes + first, count, stride=stride)
        tall[pl.ds(start * 4 + j, count, stride=4), :] = wide[source, :]

    for j in range(4):
        for r in range(sides // 4):
            take(starts[0] + r * run, run, j, 4 * r * cols, 4)
        take(starts[1], sides, j, 0, cols)
        take(starts[2], sides, j, cols - 1, cols)
        take(starts[3], cols, j, 0, 1)
        take(starts[4], cols, j, nodes - cols, 1)
    outs = (block, west_ref, east_ref, top_ref, bottom_ref)
    for start, out in zip(starts, outs):
        for i in range(out.shape[0]):
            out[i] = tall[(start + i) * 4 : (start + i) * 4 + 4, :].astype(BF)
        if out is block:
            stores = [
                pltpu.make_async_copy(block, out_hbm.at[d], sem.at[d])
                for d in range(out_hbm.shape[0])
            ]
            for store in stores:
                store.start()
    for store in stores:
        store.wait()


def early_kernel(tiles, edge_ref, recv_ref, node_ref, we_ref, wr_ref, part_ref, got_ref):
    step = pl.program_id(0)

    for k in range(GROUP):
        tile = pl.multiple_of(tiles[step * GROUP + k] * BLK, BLK)
        hot = chosen(recv_ref[k : k + 1, :])
        rows = lax.dot_general(
            hot,
            node_ref[pl.ds(tile, BLK), :],
            (((0,), (0,)), ((), ())),
            preferred_element_type=F32,
        )
        got_ref[k * BLK : (k + 1) * BLK, :] = rows.astype(BF)
    total = dot(edge_ref[...], we_ref[...]) + dot(got_ref[...], wr_ref[...])
    part_ref[...] = total.astype(BF)


def near_kernel(near_index, node_ref, *refs):
    rims = refs[:RIMS]
    part_ref, ws_ref, pre_ref, tall, sent = refs[RIMS:]
    nodes = node_ref.shape[0]
    step = pl.program_id(0)

    @pl.when(step == 0)
    def _():
        for j in range(4):
            tall[pl.ds(j, nodes, stride=4), :] = node_ref[:, j * 128 : (j + 1) * 128].astype(F32)
        at = nodes * 4
        for rim in rims:
            for i in range(rim.shape[0]):
                tall[at : at + 4, :] = rim[i].astype(F32)
                at += 4
        tall[at : at + 4, :] = jnp.zeros((4, 128), F32)

    def body(i, carry):
        for u in range(16):
            e = i * 16 + u
            row = near_index[step * ROWS + e]
            sent[pl.ds(pl.multiple_of(e * 4, 4), 4), :] = tall[
                pl.ds(pl.multiple_of(row * 4, 4), 4), :
            ]
        return carry

    lax.fori_loop(0, ROWS // 16, body, 0)
    total = part_ref[...].astype(F32) + dot(sent_rows(sent), ws_ref[...])
    pre_ref[...] = total.astype(BF)


def late_kernel(far_list, far_count, tiles, lives, *refs):
    pieces = refs[:FAR]
    (
        pre_hbm,
        edge_hbm,
        node_hbm,
        w1_hbm,
        w2_hbm,
        wn_hbm,
        wn2_hbm,
        recv_ref,
        eg_ref,
        ng_ref,
        out_hbm,
        node_out_ref,
        table,
        sent,
        pre,
        edge,
        out,
        agg,
        node,
        ws,
        w2,
        wn,
        wn2,
        sem,
        in_sem,
        out_sem,
    ) = refs[FAR:]
    steps = recv_ref.shape[0] // GROUP
    rows_of = lambda g: pl.ds(g * ROWS, ROWS)
    copies = load_table(pieces, table, sem)
    first = [
        pltpu.make_async_copy(w1_hbm.at[pl.ds(F, F)], ws, in_sem.at[0]),
        pltpu.make_async_copy(w2_hbm, w2, in_sem.at[1]),
    ]
    parts = []
    for g in range(steps):
        parts.append(
            [
                pltpu.make_async_copy(pre_hbm.at[rows_of(g)], pre.at[rows_of(g)], in_sem.at[6 + 2 * g]),
                pltpu.make_async_copy(edge_hbm.at[rows_of(g)], edge.at[rows_of(g)], in_sem.at[7 + 2 * g]),
            ]
        )
    last = [
        pltpu.make_async_copy(node_hbm, node, in_sem.at[3]),
        pltpu.make_async_copy(wn_hbm, wn, in_sem.at[4]),
        pltpu.make_async_copy(wn2_hbm, wn2, in_sem.at[5]),
    ]
    for copy in first:
        copy.start()
    sent[...] = jnp.zeros_like(sent)
    agg[...] = jnp.zeros_like(agg)
    for copy in copies:
        copy.wait()
    for copy in sum(parts, []) + last:
        copy.start()

    for g in range(steps):

        def entry(i):
            packed = far_list[g * ROWS + i]
            return packed & 4095, packed >> 12

        fetch((far_count[g] + 15) >> 4, 16, entry, table, sent)
    for copy in first:
        copy.wait()
    place = lax.broadcasted_iota(jnp.int32, (BLK, F), 0)
    stores = []
    for g in range(steps):
        for copy in parts[g]:
            copy.wait()
        base = g * ROWS
        total = pre[rows_of(g), :].astype(F32) + dot(sent_rows(sent, base), ws[...])
        message = normed(dot(silu(total).astype(BF), w2[...]), eg_ref[...]).astype(BF)
        for k in range(GROUP):
            b = g * GROUP + k
            part = message[k * BLK : (k + 1) * BLK, :]
            at = pl.ds(base + k * BLK, BLK)
            live = place < lives[b]
            out[at, :] = jnp.where(
                live, edge[at, :].astype(F32) + part.astype(F32), 0.0
            ).astype(BF)
            tile = pl.multiple_of(tiles[b] * BLK, BLK)
            agg[pl.ds(tile, BLK), :] += dot(chosen(recv_ref[b : b + 1, :]), part)
        store = pltpu.make_async_copy(out.at[rows_of(g)], out_hbm.at[rows_of(g)], out_sem.at[g])
        store.start()
        stores.append(store)
    for copy in last:
        copy.wait()
    first_sum = dot(node[...], wn[:F, :]) + dot(agg[...].astype(BF), wn[F:, :])
    second = dot(silu(first_sum).astype(BF), wn2[...])
    node_out_ref[...] = (node[...].astype(F32) + normed(second, ng_ref[...])).astype(BF)
    for store in stores:
        store.wait()


def far_lists(is_far, far_index, steps):
    place = jnp.arange(ROWS, dtype=jnp.int32)
    slots = steps * ROWS
    far = is_far.reshape(steps, ROWS)
    flag = far.astype(jnp.int32)
    before = place[:, None] > place[None, :]
    rank = jnp.sum(jnp.where(before[None], flag[:, None, :], 0), 2)
    packed = (far_index * 4096 + jnp.arange(slots, dtype=jnp.int32) - slots).reshape(steps, ROWS)
    hit = (rank[:, None, :] == place[None, :, None]) & far[:, None, :]
    return (slots + jnp.sum(jnp.where(hit, packed[:, None, :], 0), 2)).reshape(-1), jnp.sum(flag, 1)


def specs():
    whole = lambda shape: pl.BlockSpec(shape, lambda i, *_: (0,) * len(shape))
    part = pl.BlockSpec((ROWS, F), lambda i, *_: (i, 0))
    recv_spec = pl.BlockSpec((None, GROUP, BLK), lambda i, *_: (i, 0, 0))
    weight = lambda k: pl.BlockSpec((F, F), lambda i, *_: (k, 0))
    anywhere = pl.BlockSpec(memory_space=pl.ANY)
    return whole, part, recv_spec, weight, anywhere


def early_call(block_tile, edge_latent, recv_rows, own_rows, w_first):
    whole, part, recv_spec, weight, anywhere = specs()
    blocks, nodes = block_tile.shape[0], own_rows.shape[0]
    return pl.pallas_call(
        early_kernel,
        name="early",
        grid_spec=pltpu.PrefetchScalarGridSpec(
            num_scalar_prefetch=1,
            grid=(blocks // GROUP,),
            in_specs=[part, recv_spec, whole((nodes, F)), weight(0), weight(2)],
            out_specs=part,
            scratch_shapes=[pltpu.VMEM((ROWS, F), BF)],
        ),
        out_shape=jax.ShapeDtypeStruct((blocks * BLK, F), BF),
        compiler_params=pltpu.CompilerParams(vmem_limit_bytes=16 << 20),
        cost_estimate=pl.CostEstimate(
            flops=3 * 10**9, bytes_accessed=10 * 10**6, transcendentals=0
        ),
    )(block_tile, edge_latent, recv_rows, own_rows, w_first, w_first)


def near_call(near_index, own_rows, rims, partial, w_first):
    whole, part, recv_spec, weight, anywhere = specs()
    slots, nodes = partial.shape[0], own_rows.shape[0]
    near_rows = nodes + sum(rim.shape[0] for rim in rims) + 1
    return pl.pallas_call(
        near_kernel,
        name="near",
        grid_spec=pltpu.PrefetchScalarGridSpec(
            num_scalar_prefetch=1,
            grid=(slots // ROWS,),
            in_specs=[whole((nodes, F))] + [whole(rim.shape) for rim in rims] + [part, weight(1)],
            out_specs=part,
            scratch_shapes=[
                pltpu.VMEM((near_rows * 4 + 4, 128), F32),
                pltpu.VMEM((ROWS * 4, 128), F32),
            ],
        ),
        out_shape=jax.ShapeDtypeStruct((slots, F), BF),
        compiler_params=pltpu.CompilerParams(vmem_limit_bytes=16 << 20),
        cost_estimate=pl.CostEstimate(
            flops=2 * 10**9, bytes_accessed=8 * 10**6, transcendentals=0
        ),
    )(near_index, own_rows, *rims, partial, w_first)


def late_call(
    far_list,
    far_count,
    block_tile,
    lives,
    far_pieces,
    pre,
    edge_latent,
    receiver,
    own_rows,
    w_first,
    w_second,
    edge_gain,
    w_node_first,
    w_node_second,
    node_gain,
):
    blocks, nodes = block_tile.shape[0], own_rows.shape[0]
    slots, steps = blocks * BLK, blocks // GROUP
    far_rows = sum(piece.shape[0] for piece in far_pieces)
    anywhere = pl.BlockSpec(memory_space=pl.ANY)
    local = pl.BlockSpec(memory_space=pltpu.VMEM)
    scalars = pl.BlockSpec(memory_space=pltpu.SMEM)
    square = pltpu.VMEM((F, F), BF)
    return pl.pallas_call(
        late_kernel,
        name="late",
        in_specs=[scalars] * 4 + [anywhere] * (FAR + 7) + [local] * 3,
        out_specs=[anywhere, local],
        scratch_shapes=[
            pltpu.VMEM((far_rows, 4, 128), BF),
            pltpu.VMEM((slots * 4 + 32, 128), F32),
            pltpu.VMEM((slots, F), BF),
            pltpu.VMEM((slots, F), BF),
            pltpu.VMEM((slots, F), BF),
            pltpu.VMEM((nodes, F), F32),
            pltpu.VMEM((nodes, F), BF),
            square,
            square,
            pltpu.VMEM((2 * F, F), BF),
            square,
            pltpu.SemaphoreType.DMA((FAR,)),
            pltpu.SemaphoreType.DMA((6 + 2 * steps,)),
            pltpu.SemaphoreType.DMA((steps,)),
        ],
        out_shape=[
            jax.ShapeDtypeStruct((slots, F), BF),
            jax.ShapeDtypeStruct((nodes, F), BF),
        ],
        compiler_params=pltpu.CompilerParams(vmem_limit_bytes=40 << 20),
        cost_estimate=pl.CostEstimate(
            flops=4 * 10**9, bytes_accessed=14 * 10**6, transcendentals=2 * 10**6
        ),
    )(
        far_list,
        far_count,
        block_tile,
        lives,
        *far_pieces,
        pre,
        edge_latent,
        own_rows,
        w_first,
        w_second,
        w_node_first,
        w_node_second,
        receiver.reshape(blocks, BLK),
        edge_gain.reshape(1, F),
        node_gain.reshape(1, F),
    )


def per_device(
    node_latent,
    edge_latent,
    sender,
    receiver,
    block_tile,
    w_first,
    w_second,
    edge_gain,
    w_node_first,
    w_node_second,
    node_gain,
):
    patch_rows, patch_cols, features = node_latent.shape
    lat_index = lax.axis_index("lat")
    lon_index = lax.axis_index("lon")
    lat_count, lon_count = lax.axis_size("lat"), lax.axis_size("lon")
    grid_cols = patch_cols * lon_count
    blocks = block_tile.shape[0]
    steps = blocks // GROUP
    nodes = patch_rows * patch_cols
    own_rows = node_latent.reshape(nodes, features)
    lanes = lambda a: a.reshape(-1, 4, 128)

    right = [(i, (i + 1) % lon_count) for i in range(lon_count)]
    left = [(j, i) for i, j in right]
    up = [(i, i + 1) for i in range(lat_count - 1)]
    down = [(j, i) for i, j in up]

    per = patch_rows // 4 * (patch_cols // 4)
    lane_rows = lambda rows: jax.ShapeDtypeStruct((rows, 4, 128), BF)
    copies, first_col, last_col, top, bottom = pl.pallas_call(
        coarse_kernel,
        name="coarse",
        in_specs=[pl.BlockSpec(memory_space=pltpu.VMEM)],
        out_specs=[pl.BlockSpec(memory_space=pl.ANY)] + [pl.BlockSpec(memory_space=pltpu.VMEM)] * 4,
        scratch_shapes=[
            pltpu.VMEM((nodes * 4, 128), F32),
            pltpu.VMEM((4 * (per + 2 * patch_rows + 2 * patch_cols), 128), F32),
            pltpu.VMEM((per, 4, 128), BF),
            pltpu.SemaphoreType.DMA((lon_count,)),
        ],
        out_shape=[
            jax.ShapeDtypeStruct((lon_count, per, 4, 128), BF),
            lane_rows(patch_rows),
            lane_rows(patch_rows),
            lane_rows(patch_cols),
            lane_rows(patch_cols),
        ],
        compiler_params=pltpu.CompilerParams(vmem_limit_bytes=VMEM),
    )(own_rows)
    senders = jnp.maximum(sender, 0)
    send_row = senders // grid_cols
    send_col = senders % grid_cols
    row = send_row - lat_index * patch_rows
    col = (send_col - lon_index * patch_cols + 1) % grid_cols - 1
    is_near = (row >= -1) & (row <= patch_rows) & (col <= patch_cols)
    side = jnp.where(col < 0, nodes + row, nodes + patch_rows + row)
    inner = jnp.where((col < 0) | (col >= patch_cols), side, row * patch_cols + col)
    rim, span = nodes + 2 * patch_rows, patch_cols + 2
    near_index = jnp.where(
        row < 0, rim + col + 1, jnp.where(row >= patch_rows, rim + span + col + 1, inner)
    )
    near_index = jnp.where(is_near, near_index, rim + 2 * span)
    src_lat, src_lon = send_row // patch_rows, send_col // patch_cols
    src_core, core = src_lat % 2, lat_index % 2
    at_x = ring_place((src_lat // 2 - lat_index // 2) % 4, src_core)
    half = jnp.where(src_core == core, 0, 1)
    within = send_row % patch_rows // 4 * (patch_cols // 4) + send_col % patch_cols // 4
    far_index = ((half * 4 + at_x) * lon_count + src_lon) * per + within
    far_list, far_count = far_lists((receiver >= 0) & ~is_near, far_index, steps)
    recv_rows = receiver.reshape(steps, GROUP, BLK)
    lives = jnp.sum((receiver >= 0).astype(jnp.int32).reshape(blocks, BLK), 1)

    west = lax.ppermute(last_col, "lon", right)
    east = lax.ppermute(first_col, "lon", left)
    plane = lanes(lax.all_to_all(copies, "lon", split_axis=0, concat_axis=0, tiled=True))
    wide = lambda r, rows: jnp.concatenate([west[r : r + 1], rows, east[r : r + 1]], 0)
    north = lax.ppermute(wide(patch_rows - 1, bottom), "lat", up)
    south = lax.ppermute(wide(0, top), "lat", down)
    plane, north, south, tiles, near_index, far_list, far_count, lives = lax.optimization_barrier(
        (plane, north, south, block_tile, near_index, far_list, far_count, lives)
    )

    ahead = move(plane, "x", (1, -1))
    plane_other = other_core(plane)
    partial = early_call(tiles, edge_latent, recv_rows, own_rows, w_first)
    later, partial = lax.optimization_barrier((plane, partial))
    behind = move(later, "x", (-1, 1))
    ahead, partial = lax.optimization_barrier((ahead, partial))
    across = move(ahead, "x", (1, -1))
    rims = [west, east, north, south]
    pre = near_call(near_index, own_rows, rims, partial, w_first)
    across, behind, pre = lax.optimization_barrier((across, behind, pre))
    far_pieces = [plane, ahead, behind, across, plane_other]
    far_pieces += [other_core(piece) for piece in (ahead, behind, across)]
    edge_out, node_out = late_call(
        far_list,
        far_count,
        block_tile,
        lives,
        far_pieces,
        pre,
        edge_latent,
        receiver,
        own_rows,
        w_first,
        w_second,
        edge_gain,
        w_node_first,
        w_node_second,
        node_gain,
    )
    return node_out.reshape(patch_rows, patch_cols, features), edge_out


def solution(mesh):
    return jax.shard_map(
        per_device,
        mesh=mesh,
        in_specs=(
            P("lat", "lon", None),
            P(("lat", "lon"), None),
            P(("lat", "lon")),
            P(("lat", "lon")),
            P(("lat", "lon")),
            P(),
            P(),
            P(),
            P(),
            P(),
            P(),
        ),
        out_specs=(P("lat", "lon", None), P(("lat", "lon"), None)),
        check_vma=False,
    )
```

```python
import jax
import jax.numpy as jnp
from jax import lax
from jax.experimental import pallas as pl
from jax.experimental.pallas import tpu as pltpu
from jax.sharding import PartitionSpec as P

F = 512
BLK = 128
GROUP = 4
ROWS = GROUP * BLK
RIMS = 4
FAR = 8
VMEM = 16 << 20
BF = jnp.bfloat16
F32 = jnp.float32


def device_of(x, c, y, z):
    return (x % 4 * 2 + c) * 16 + y % 4 * 4 + z % 4


def shift(axis, by_core):
    pairs = []
    for x in range(4):
        for c in range(2):
            for y in range(4):
                for z in range(4):
                    to = {"x": x, "y": y, "z": z}
                    to[axis] += by_core[c]
                    pairs.append((device_of(x, c, y, z), device_of(to["x"], c, to["y"], to["z"])))
    return pairs


def other_core(value):
    pairs = [
        (device_of(x, c, y, z), device_of(x, 1 - c, y, z))
        for x in range(4)
        for c in range(2)
        for y in range(4)
        for z in range(4)
    ]
    return lax.ppermute(value, ("lat", "lon"), pairs)


def move(value, axis, by_core):
    return lax.ppermute(value, ("lat", "lon"), shift(axis, by_core))


def ring_place(offset, core):
    near = jnp.where((offset == 1) == (core == 1), 1, 2)
    return jnp.where(offset == 0, 0, jnp.where(offset == 2, 3, near))


def silu(v):
    half = 0.5 * v
    return half + half * jnp.tanh(half)


def normed(values, gain):
    centred = values - jnp.mean(values, -1, keepdims=True)
    spread = jnp.mean(centred * centred, -1, keepdims=True)
    return centred * lax.rsqrt(spread + 1e-05) * gain


def dot(a, b):
    return jnp.dot(a, b, preferred_element_type=F32)


def chosen(recv_row):
    return (lax.broadcasted_iota(jnp.int32, (BLK, BLK), 0) == recv_row).astype(BF)


def fetch(count, unroll, entry, table, sent):
    def body(i, carry):
        for u in range(unroll):
            slot, row = entry(i * unroll + u)
            sent[pl.ds(pl.multiple_of(slot * 4, 4), 4), :] = table[row].astype(F32)
        return carry

    lax.fori_loop(0, count, body, 0)


def sent_rows(sent, base=0):
    return jnp.concatenate(
        [sent[pl.ds(base * 4 + j, ROWS, stride=4), :].astype(BF) for j in range(4)], axis=1
    )


def load_table(pieces, table, sem):
    copies = []
    start = 0
    for i, piece in enumerate(pieces):
        rows = piece.shape[0]
        copies.append(pltpu.make_async_copy(piece, table.at[pl.ds(start, rows)], sem.at[i]))
        start += rows
    for copy in copies:
        copy.start()
    return copies


def coarse_kernel(odd, node_ref, out_hbm, *refs):
    col_refs, row_refs = refs[0:2], refs[2:4]
    wide, tall, block, sem = refs[4:]
    nodes, sides, cols = node_ref.shape[0], col_refs[0].shape[0], row_refs[0].shape[0]
    per = block.shape[0]
    run = cols // 4
    starts = []
    at = 0
    for rows in (per, sides, sides, cols, cols):
        starts.append(at)
        at += rows
    for j in range(4):
        wide[j * nodes : (j + 1) * nodes, :] = node_ref[:, j * 128 : (j + 1) * 128].astype(F32)

    def take(start, count, j, first, stride):
        source = pl.ds(j * nodes + first, count, stride=stride)
        tall[pl.ds(start * 4 + j, count, stride=4), :] = wide[source, :]

    for j in range(4):
        for r in range(sides // 4):
            take(starts[0] + r * run, run, j, 4 * r * cols, 4)
        take(starts[1], sides, j, 0, cols)
        take(starts[2], sides, j, cols - 1, cols)
        take(starts[3], cols, j, 0, 1)
        take(starts[4], cols, j, nodes - cols, 1)
    row = lambda k, i: tall[(starts[k] + i) * 4 : (starts[k] + i) * 4 + 4, :]
    for i in range(per):
        block[i] = row(0, i).astype(BF)
    stores = [
        pltpu.make_async_copy(block, out_hbm.at[d], sem.at[d]) for d in range(out_hbm.shape[0])
    ]
    for store in stores:
        store.start()
    for refs_of, low, high, is_odd in ((col_refs, 1, 2, odd[1] == 1), (row_refs, 3, 4, odd[0] == 1)):
        for i in range(refs_of[0].shape[0]):
            first, last = row(low, i), row(high, i)
            refs_of[0][i] = jnp.where(is_odd, first, last).astype(BF)
            refs_of[1][i] = jnp.where(is_odd, last, first).astype(BF)
    for store in stores:
        store.wait()


def early_kernel(tiles, edge_ref, recv_ref, node_ref, we_ref, wr_ref, part_ref, got_ref):
    step = pl.program_id(0)

    for k in range(GROUP):
        tile = pl.multiple_of(tiles[step * GROUP + k] * BLK, BLK)
        hot = chosen(recv_ref[k : k + 1, :])
        rows = lax.dot_general(
            hot,
            node_ref[pl.ds(tile, BLK), :],
            (((0,), (0,)), ((), ())),
            preferred_element_type=F32,
        )
        got_ref[k * BLK : (k + 1) * BLK, :] = rows.astype(BF)
    total = dot(edge_ref[...], we_ref[...]) + dot(got_ref[...], wr_ref[...])
    part_ref[...] = total.astype(BF)


def near_kernel(near_index, node_ref, *refs):
    rims = refs[:RIMS]
    part_ref, ws_ref, pre_ref, tall, sent = refs[RIMS:]
    nodes = node_ref.shape[0]
    step = pl.program_id(0)

    @pl.when(step == 0)
    def _():
        for j in range(4):
            tall[pl.ds(j, nodes, stride=4), :] = node_ref[:, j * 128 : (j + 1) * 128].astype(F32)
        at = nodes * 4
        for rim in rims:
            for i in range(rim.shape[0]):
                tall[at : at + 4, :] = rim[i].astype(F32)
                at += 4
        tall[at : at + 4, :] = jnp.zeros((4, 128), F32)

    def body(i, carry):
        for u in range(16):
            e = i * 16 + u
            row = near_index[step * ROWS + e]
            sent[pl.ds(pl.multiple_of(e * 4, 4), 4), :] = tall[
                pl.ds(pl.multiple_of(row * 4, 4), 4), :
            ]
        return carry

    lax.fori_loop(0, ROWS // 16, body, 0)
    total = part_ref[...].astype(F32) + dot(sent_rows(sent), ws_ref[...])
    pre_ref[...] = total.astype(BF)


def late_kernel(far_list, far_count, tiles, lives, *refs):
    pieces = refs[:FAR]
    (
        pre,
        edge,
        node,
        w1,
        w2,
        wn,
        wn2,
        recv_ref,
        eg_ref,
        ng_ref,
        out_hbm,
        node_out_ref,
        table,
        sent,
        out,
        agg,
        sem,
        out_sem,
    ) = refs[FAR:]
    steps = recv_ref.shape[0] // GROUP
    copies = load_table(pieces, table, sem)
    sent[...] = jnp.zeros_like(sent)
    agg[...] = jnp.zeros_like(agg)
    for copy in copies:
        copy.wait()

    for g in range(steps):

        def entry(i):
            packed = far_list[g * ROWS + i]
            return packed & 4095, packed >> 12

        fetch((far_count[g] + 15) >> 4, 16, entry, table, sent)
    place = lax.broadcasted_iota(jnp.int32, (BLK, F), 0)
    stores = []
    for g in range(steps):
        base = g * ROWS
        rows = pl.ds(base, ROWS)
        total = pre[rows, :].astype(F32) + dot(sent_rows(sent, base), w1[F : 2 * F, :])
        message = normed(dot(silu(total).astype(BF), w2[...]), eg_ref[...]).astype(BF)
        for k in range(GROUP):
            b = g * GROUP + k
            part = message[k * BLK : (k + 1) * BLK, :]
            at = pl.ds(base + k * BLK, BLK)
            live = place < lives[b]
            out[at, :] = jnp.where(
                live, edge[at, :].astype(F32) + part.astype(F32), 0.0
            ).astype(BF)
            tile = pl.multiple_of(tiles[b] * BLK, BLK)
            agg[pl.ds(tile, BLK), :] += dot(chosen(recv_ref[b : b + 1, :]), part)
        store = pltpu.make_async_copy(out.at[rows], out_hbm.at[rows], out_sem.at[g])
        store.start()
        stores.append(store)
    first_sum = dot(node[...], wn[:F, :]) + dot(agg[...].astype(BF), wn[F:, :])
    second = dot(silu(first_sum).astype(BF), wn2[...])
    node_out_ref[...] = (node[...].astype(F32) + normed(second, ng_ref[...])).astype(BF)
    for store in stores:
        store.wait()


def far_lists(is_far, far_index, steps):
    place = jnp.arange(ROWS, dtype=jnp.int32)
    slots = steps * ROWS
    far = is_far.reshape(steps, ROWS)
    flag = far.astype(jnp.int32)
    before = place[:, None] > place[None, :]
    rank = jnp.sum(jnp.where(before[None], flag[:, None, :], 0), 2)
    packed = (far_index * 4096 + jnp.arange(slots, dtype=jnp.int32) - slots).reshape(steps, ROWS)
    hit = (rank[:, None, :] == place[None, :, None]) & far[:, None, :]
    return (slots + jnp.sum(jnp.where(hit, packed[:, None, :], 0), 2)).reshape(-1), jnp.sum(flag, 1)


def specs():
    whole = lambda shape: pl.BlockSpec(shape, lambda i, *_: (0,) * len(shape))
    part = pl.BlockSpec((ROWS, F), lambda i, *_: (i, 0))
    recv_spec = pl.BlockSpec((None, GROUP, BLK), lambda i, *_: (i, 0, 0))
    weight = lambda k: pl.BlockSpec((F, F), lambda i, *_: (k, 0))
    anywhere = pl.BlockSpec(memory_space=pl.ANY)
    return whole, part, recv_spec, weight, anywhere


def early_call(block_tile, edge_latent, recv_rows, own_rows, w_first):
    whole, part, recv_spec, weight, anywhere = specs()
    blocks, nodes = block_tile.shape[0], own_rows.shape[0]
    return pl.pallas_call(
        early_kernel,
        name="early",
        grid_spec=pltpu.PrefetchScalarGridSpec(
            num_scalar_prefetch=1,
            grid=(blocks // GROUP,),
            in_specs=[part, recv_spec, whole((nodes, F)), weight(0), weight(2)],
            out_specs=part,
            scratch_shapes=[pltpu.VMEM((ROWS, F), BF)],
        ),
        out_shape=jax.ShapeDtypeStruct((blocks * BLK, F), BF),
        compiler_params=pltpu.CompilerParams(vmem_limit_bytes=16 << 20),
        cost_estimate=pl.CostEstimate(
            flops=3 * 10**9, bytes_accessed=10 * 10**6, transcendentals=0
        ),
    )(block_tile, edge_latent, recv_rows, own_rows, w_first, w_first)


def near_call(near_index, own_rows, rims, partial, w_first):
    whole, part, recv_spec, weight, anywhere = specs()
    slots, nodes = partial.shape[0], own_rows.shape[0]
    near_rows = nodes + sum(rim.shape[0] for rim in rims) + 1
    return pl.pallas_call(
        near_kernel,
        name="near",
        grid_spec=pltpu.PrefetchScalarGridSpec(
            num_scalar_prefetch=1,
            grid=(slots // ROWS,),
            in_specs=[whole((nodes, F))] + [whole(rim.shape) for rim in rims] + [part, weight(1)],
            out_specs=part,
            scratch_shapes=[
                pltpu.VMEM((near_rows * 4 + 4, 128), F32),
                pltpu.VMEM((ROWS * 4, 128), F32),
            ],
        ),
        out_shape=jax.ShapeDtypeStruct((slots, F), BF),
        compiler_params=pltpu.CompilerParams(vmem_limit_bytes=16 << 20),
        cost_estimate=pl.CostEstimate(
            flops=2 * 10**9, bytes_accessed=8 * 10**6, transcendentals=0
        ),
    )(near_index, own_rows, *rims, partial, w_first)


def late_call(
    far_list,
    far_count,
    block_tile,
    lives,
    far_pieces,
    pre,
    edge_latent,
    receiver,
    own_rows,
    w_first,
    w_second,
    edge_gain,
    w_node_first,
    w_node_second,
    node_gain,
):
    blocks, nodes = block_tile.shape[0], own_rows.shape[0]
    slots, steps = blocks * BLK, blocks // GROUP
    far_rows = sum(piece.shape[0] for piece in far_pieces)
    anywhere = pl.BlockSpec(memory_space=pl.ANY)
    local = pl.BlockSpec(memory_space=pltpu.VMEM)
    scalars = pl.BlockSpec(memory_space=pltpu.SMEM)
    return pl.pallas_call(
        late_kernel,
        name="late",
        in_specs=[scalars] * 4 + [anywhere] * FAR + [local] * 10,
        out_specs=[anywhere, local],
        scratch_shapes=[
            pltpu.VMEM((far_rows, 4, 128), BF),
            pltpu.VMEM((slots * 4 + 32, 128), F32),
            pltpu.VMEM((slots, F), BF),
            pltpu.VMEM((nodes, F), F32),
            pltpu.SemaphoreType.DMA((FAR,)),
            pltpu.SemaphoreType.DMA((steps,)),
        ],
        out_shape=[
            jax.ShapeDtypeStruct((slots, F), BF),
            jax.ShapeDtypeStruct((nodes, F), BF),
        ],
        compiler_params=pltpu.CompilerParams(vmem_limit_bytes=40 << 20),
        cost_estimate=pl.CostEstimate(
            flops=4 * 10**9, bytes_accessed=14 * 10**6, transcendentals=2 * 10**6
        ),
    )(
        far_list,
        far_count,
        block_tile,
        lives,
        *far_pieces,
        pre,
        edge_latent,
        own_rows,
        w_first,
        w_second,
        w_node_first,
        w_node_second,
        receiver.reshape(blocks, BLK),
        edge_gain.reshape(1, F),
        node_gain.reshape(1, F),
    )


def per_device(
    node_latent,
    edge_latent,
    sender,
    receiver,
    block_tile,
    w_first,
    w_second,
    edge_gain,
    w_node_first,
    w_node_second,
    node_gain,
):
    patch_rows, patch_cols, features = node_latent.shape
    lat_index = lax.axis_index("lat")
    lon_index = lax.axis_index("lon")
    lat_count, lon_count = lax.axis_size("lat"), lax.axis_size("lon")
    grid_cols = patch_cols * lon_count
    blocks = block_tile.shape[0]
    steps = blocks // GROUP
    nodes = patch_rows * patch_cols
    own_rows = node_latent.reshape(nodes, features)
    lanes = lambda a: a.reshape(-1, 4, 128)

    def pairs(first, count, wrap):
        couples = [(i, (i + 1) % count) for i in range(first, count if wrap else count - 1, 2)]
        return couples + [(j, i) for i, j in couples]

    lat_odd, lon_odd = lat_index % 2, lon_index % 2
    per = patch_rows // 4 * (patch_cols // 4)
    lane_rows = lambda rows: jax.ShapeDtypeStruct((rows, 4, 128), BF)
    copies, col_a, col_b, row_a, row_b = pl.pallas_call(
        coarse_kernel,
        name="coarse",
        in_specs=[pl.BlockSpec(memory_space=pltpu.SMEM), pl.BlockSpec(memory_space=pltpu.VMEM)],
        out_specs=[pl.BlockSpec(memory_space=pl.ANY)] + [pl.BlockSpec(memory_space=pltpu.VMEM)] * 4,
        scratch_shapes=[
            pltpu.VMEM((nodes * 4, 128), F32),
            pltpu.VMEM((4 * (per + 2 * patch_rows + 2 * patch_cols), 128), F32),
            pltpu.VMEM((per, 4, 128), BF),
            pltpu.SemaphoreType.DMA((lon_count,)),
        ],
        out_shape=[
            jax.ShapeDtypeStruct((lon_count, per, 4, 128), BF),
            lane_rows(patch_rows),
            lane_rows(patch_rows),
            lane_rows(patch_cols),
            lane_rows(patch_cols),
        ],
        compiler_params=pltpu.CompilerParams(vmem_limit_bytes=VMEM),
    )(jnp.stack([lat_odd, lon_odd]).astype(jnp.int32), own_rows)
    senders = jnp.maximum(sender, 0)
    send_row = senders // grid_cols
    send_col = senders % grid_cols
    row = send_row - lat_index * patch_rows
    col = (send_col - lon_index * patch_cols + 1) % grid_cols - 1
    is_near = (row >= -1) & (row <= patch_rows) & (col <= patch_cols)
    side = nodes + row + patch_rows * jnp.where(col < 0, 1 - lon_odd, lon_odd)
    inner = jnp.where((col < 0) | (col >= patch_cols), side, row * patch_cols + col)
    rim, span = nodes + 2 * patch_rows, patch_cols + 2
    strip = rim + col + 1 + span * jnp.where(row < 0, 1 - lat_odd, lat_odd)
    near_index = jnp.where((row < 0) | (row >= patch_rows), strip, inner)
    near_index = jnp.where(is_near, near_index, rim + 2 * span)
    src_lat, src_lon = send_row // patch_rows, send_col // patch_cols
    src_core, core = src_lat % 2, lat_index % 2
    at_x = ring_place((src_lat // 2 - lat_index // 2) % 4, src_core)
    half = jnp.where(src_core == core, 0, 1)
    within = send_row % patch_rows // 4 * (patch_cols // 4) + send_col % patch_cols // 4
    far_index = ((half * 4 + at_x) * lon_count + src_lon) * per + within
    far_list, far_count = far_lists((receiver >= 0) & ~is_near, far_index, steps)
    recv_rows = receiver.reshape(steps, GROUP, BLK)
    lives = jnp.sum((receiver >= 0).astype(jnp.int32).reshape(blocks, BLK), 1)

    side_a = lax.ppermute(col_a, "lon", pairs(0, lon_count, True))
    side_b = lax.ppermute(col_b, "lon", pairs(1, lon_count, True))
    plane = lanes(lax.all_to_all(copies, "lon", split_axis=0, concat_axis=0, tiled=True))
    west = jnp.where(lon_odd == 1, side_a, side_b)
    east = jnp.where(lon_odd == 1, side_b, side_a)
    wide = lambda r, rows: jnp.concatenate(
        [lax.dynamic_slice_in_dim(west, r, 1), rows, lax.dynamic_slice_in_dim(east, r, 1)], 0
    )
    edge_row = (1 - lat_odd) * (patch_rows - 1)
    strip_a = lax.ppermute(wide(edge_row, row_a), "lat", pairs(0, lat_count, False))
    strip_b = lax.ppermute(
        wide(patch_rows - 1 - edge_row, row_b), "lat", pairs(1, lat_count, False)
    )
    plane, strip_a, strip_b, tiles, near_index, far_list, far_count, lives = lax.optimization_barrier(
        (plane, strip_a, strip_b, block_tile, near_index, far_list, far_count, lives)
    )

    ahead = move(plane, "x", (1, -1))
    plane_other = other_core(plane)
    partial = early_call(tiles, edge_latent, recv_rows, own_rows, w_first)
    later, partial = lax.optimization_barrier((plane, partial))
    behind = move(later, "x", (-1, 1))
    ahead, partial = lax.optimization_barrier((ahead, partial))
    across = move(ahead, "x", (1, -1))
    rims = [side_a, side_b, strip_a, strip_b]
    pre = near_call(near_index, own_rows, rims, partial, w_first)
    across, behind, pre = lax.optimization_barrier((across, behind, pre))
    far_pieces = [plane, ahead, behind, across, plane_other]
    far_pieces += [other_core(piece) for piece in (ahead, behind, across)]
    edge_out, node_out = late_call(
        far_list,
        far_count,
        block_tile,
        lives,
        far_pieces,
        pre,
        edge_latent,
        receiver,
        own_rows,
        w_first,
        w_second,
        edge_gain,
        w_node_first,
        w_node_second,
        node_gain,
    )
    return node_out.reshape(patch_rows, patch_cols, features), edge_out


def solution(mesh):
    return jax.shard_map(
        per_device,
        mesh=mesh,
        in_specs=(
            P("lat", "lon", None),
            P(("lat", "lon"), None),
            P(("lat", "lon")),
            P(("lat", "lon")),
            P(("lat", "lon")),
            P(),
            P(),
            P(),
            P(),
            P(),
            P(),
        ),
        out_specs=(P("lat", "lon", None), P(("lat", "lon"), None)),
        check_vma=False,
    )
```

```python
import jax
import jax.numpy as jnp
from jax import lax
from jax.experimental import pallas as pl
from jax.experimental.pallas import tpu as pltpu
from jax.sharding import PartitionSpec as P

F = 512
BLK = 128
GROUP = 4
ROWS = GROUP * BLK
RIMS = 4
FAR = 8
VMEM = 16 << 20
BF = jnp.bfloat16
F32 = jnp.float32


def device_of(x, c, y, z):
    return (x % 4 * 2 + c) * 16 + y % 4 * 4 + z % 4


def shift(axis, by_core):
    pairs = []
    for x in range(4):
        for c in range(2):
            for y in range(4):
                for z in range(4):
                    to = {"x": x, "y": y, "z": z}
                    to[axis] += by_core[c]
                    pairs.append((device_of(x, c, y, z), device_of(to["x"], c, to["y"], to["z"])))
    return pairs


def other_core(value):
    pairs = [
        (device_of(x, c, y, z), device_of(x, 1 - c, y, z))
        for x in range(4)
        for c in range(2)
        for y in range(4)
        for z in range(4)
    ]
    return lax.ppermute(value, ("lat", "lon"), pairs)


def move(value, axis, by_core):
    return lax.ppermute(value, ("lat", "lon"), shift(axis, by_core))


def ring_place(offset, core):
    near = jnp.where((offset == 1) == (core == 1), 1, 2)
    return jnp.where(offset == 0, 0, jnp.where(offset == 2, 3, near))


def silu(v):
    half = 0.5 * v
    return half + half * jnp.tanh(half)


def normed(values, gain):
    centred = values - jnp.mean(values, -1, keepdims=True)
    spread = jnp.mean(centred * centred, -1, keepdims=True)
    return centred * lax.rsqrt(spread + 1e-05) * gain


def dot(a, b):
    return jnp.dot(a, b, preferred_element_type=F32)


def chosen(recv_row):
    return (lax.broadcasted_iota(jnp.int32, (BLK, BLK), 0) == recv_row).astype(BF)


def fetch(count, unroll, entry, table, sent):
    def body(i, carry):
        for u in range(unroll):
            slot, row = entry(i * unroll + u)
            sent[pl.ds(pl.multiple_of(slot * 4, 4), 4), :] = table[row].astype(F32)
        return carry

    lax.fori_loop(0, count, body, 0)


def sent_rows(sent, base=0):
    return jnp.concatenate(
        [sent[pl.ds(base * 4 + j, ROWS, stride=4), :].astype(BF) for j in range(4)], axis=1
    )


def load_table(pieces, table, sem):
    copies = []
    start = 0
    for i, piece in enumerate(pieces):
        rows = piece.shape[0]
        copies.append(pltpu.make_async_copy(piece, table.at[pl.ds(start, rows)], sem.at[i]))
        start += rows
    for copy in copies:
        copy.start()
    return copies


def coarse_kernel(odd, node_ref, out_hbm, *refs):
    col_refs, row_refs = refs[0:2], refs[2:4]
    wide, tall, block, sem = refs[4:]
    nodes, sides, cols = node_ref.shape[0], col_refs[0].shape[0], row_refs[0].shape[0]
    per = block.shape[0]
    run = cols // 4
    starts = []
    at = 0
    for rows in (per, sides, sides, cols, cols):
        starts.append(at)
        at += rows
    for j in range(4):
        wide[j * nodes : (j + 1) * nodes, :] = node_ref[:, j * 128 : (j + 1) * 128].astype(F32)

    def take(start, count, j, first, stride):
        source = pl.ds(j * nodes + first, count, stride=stride)
        tall[pl.ds(start * 4 + j, count, stride=4), :] = wide[source, :]

    for j in range(4):
        for r in range(sides // 4):
            take(starts[0] + r * run, run, j, 4 * r * cols, 4)
        take(starts[1], sides, j, 0, cols)
        take(starts[2], sides, j, cols - 1, cols)
        take(starts[3], cols, j, 0, 1)
        take(starts[4], cols, j, nodes - cols, 1)
    row = lambda k, i: tall[(starts[k] + i) * 4 : (starts[k] + i) * 4 + 4, :]
    for i in range(per):
        block[i] = row(0, i).astype(BF)
    stores = [
        pltpu.make_async_copy(block, out_hbm.at[d], sem.at[d]) for d in range(out_hbm.shape[0])
    ]
    for store in stores:
        store.start()
    for refs_of, low, high, is_odd in ((col_refs, 1, 2, odd[1] == 1), (row_refs, 3, 4, odd[0] == 1)):
        for i in range(refs_of[0].shape[0]):
            first, last = row(low, i), row(high, i)
            refs_of[0][i] = jnp.where(is_odd, first, last).astype(BF)
            refs_of[1][i] = jnp.where(is_odd, last, first).astype(BF)
    for store in stores:
        store.wait()


def early_kernel(tiles, edge_ref, recv_ref, node_ref, we_ref, wr_ref, part_ref, got_ref):
    step = pl.program_id(0)

    for k in range(GROUP):
        tile = pl.multiple_of(tiles[step * GROUP + k] * BLK, BLK)
        hot = chosen(recv_ref[k : k + 1, :])
        rows = lax.dot_general(
            hot,
            node_ref[pl.ds(tile, BLK), :],
            (((0,), (0,)), ((), ())),
            preferred_element_type=F32,
        )
        got_ref[k * BLK : (k + 1) * BLK, :] = rows.astype(BF)
    total = dot(edge_ref[...], we_ref[...]) + dot(got_ref[...], wr_ref[...])
    part_ref[...] = total.astype(BF)


def near_kernel(near_index, node_ref, *refs):
    rims = refs[:RIMS]
    part_ref, ws_ref, pre_ref, tall, sent = refs[RIMS:]
    nodes = node_ref.shape[0]
    step = pl.program_id(0)

    @pl.when(step == 0)
    def _():
        for j in range(4):
            tall[pl.ds(j, nodes, stride=4), :] = node_ref[:, j * 128 : (j + 1) * 128].astype(F32)
        at = nodes * 4
        for rim in rims:
            for i in range(rim.shape[0]):
                tall[at : at + 4, :] = rim[i].astype(F32)
                at += 4
        tall[at : at + 4, :] = jnp.zeros((4, 128), F32)

    def body(i, carry):
        for u in range(16):
            e = i * 16 + u
            row = near_index[step * ROWS + e]
            sent[pl.ds(pl.multiple_of(e * 4, 4), 4), :] = tall[
                pl.ds(pl.multiple_of(row * 4, 4), 4), :
            ]
        return carry

    lax.fori_loop(0, ROWS // 16, body, 0)
    total = part_ref[...].astype(F32) + dot(sent_rows(sent), ws_ref[...])
    pre_ref[...] = total.astype(BF)


def late_kernel(far_list, far_count, tiles, lives, *refs):
    pieces = refs[:FAR]
    (
        pre,
        edge,
        node,
        w1,
        w2,
        wn,
        wn2,
        recv_ref,
        eg_ref,
        ng_ref,
        out_hbm,
        node_out_ref,
        table,
        sent,
        out,
        agg,
        sem,
        out_sem,
    ) = refs[FAR:]
    steps = recv_ref.shape[0] // GROUP
    copies = load_table(pieces, table, sem)
    sent[...] = jnp.zeros_like(sent)
    agg[...] = jnp.zeros_like(agg)
    for copy in copies:
        copy.wait()

    for g in range(steps):

        def entry(i):
            packed = far_list[g * ROWS + i]
            return packed & 4095, packed >> 12

        fetch((far_count[g] + 15) >> 4, 16, entry, table, sent)
    place = lax.broadcasted_iota(jnp.int32, (BLK, F), 0)
    stores = []
    for g in range(steps):
        base = g * ROWS
        rows = pl.ds(base, ROWS)
        total = pre[rows, :].astype(F32) + dot(sent_rows(sent, base), w1[F : 2 * F, :])
        message = normed(dot(silu(total).astype(BF), w2[...]), eg_ref[...]).astype(BF)
        for k in range(GROUP):
            b = g * GROUP + k
            part = message[k * BLK : (k + 1) * BLK, :]
            at = pl.ds(base + k * BLK, BLK)
            live = place < lives[b]
            out[at, :] = jnp.where(
                live, edge[at, :].astype(F32) + part.astype(F32), 0.0
            ).astype(BF)
            tile = pl.multiple_of(tiles[b] * BLK, BLK)
            agg[pl.ds(tile, BLK), :] += dot(chosen(recv_ref[b : b + 1, :]), part)
        store = pltpu.make_async_copy(out.at[rows], out_hbm.at[rows], out_sem.at[g])
        store.start()
        stores.append(store)
    first_sum = dot(node[...], wn[:F, :]) + dot(agg[...].astype(BF), wn[F:, :])
    second = dot(silu(first_sum).astype(BF), wn2[...])
    node_out_ref[...] = (node[...].astype(F32) + normed(second, ng_ref[...])).astype(BF)
    for store in stores:
        store.wait()


def far_lists(is_far, far_index, steps):
    place = jnp.arange(ROWS, dtype=jnp.int32)
    slots = steps * ROWS
    far = is_far.reshape(steps, ROWS)
    flag = far.astype(jnp.int32)
    before = place[:, None] > place[None, :]
    rank = jnp.sum(jnp.where(before[None], flag[:, None, :], 0), 2)
    packed = (far_index * 4096 + jnp.arange(slots, dtype=jnp.int32) - slots).reshape(steps, ROWS)
    hit = (rank[:, None, :] == place[None, :, None]) & far[:, None, :]
    return (slots + jnp.sum(jnp.where(hit, packed[:, None, :], 0), 2)).reshape(-1), jnp.sum(flag, 1)


def specs():
    whole = lambda shape: pl.BlockSpec(shape, lambda i, *_: (0,) * len(shape))
    part = pl.BlockSpec((ROWS, F), lambda i, *_: (i, 0))
    recv_spec = pl.BlockSpec((None, GROUP, BLK), lambda i, *_: (i, 0, 0))
    weight = lambda k: pl.BlockSpec((F, F), lambda i, *_: (k, 0))
    anywhere = pl.BlockSpec(memory_space=pl.ANY)
    return whole, part, recv_spec, weight, anywhere


def early_call(block_tile, edge_latent, recv_rows, own_rows, w_first):
    whole, part, recv_spec, weight, anywhere = specs()
    blocks, nodes = block_tile.shape[0], own_rows.shape[0]
    return pl.pallas_call(
        early_kernel,
        name="early",
        grid_spec=pltpu.PrefetchScalarGridSpec(
            num_scalar_prefetch=1,
            grid=(blocks // GROUP,),
            in_specs=[part, recv_spec, whole((nodes, F)), weight(0), weight(2)],
            out_specs=part,
            scratch_shapes=[pltpu.VMEM((ROWS, F), BF)],
        ),
        out_shape=jax.ShapeDtypeStruct((blocks * BLK, F), BF),
        compiler_params=pltpu.CompilerParams(vmem_limit_bytes=16 << 20),
        cost_estimate=pl.CostEstimate(
            flops=3 * 10**9, bytes_accessed=10 * 10**6, transcendentals=0
        ),
    )(block_tile, edge_latent, recv_rows, own_rows, w_first, w_first)


def near_call(near_index, own_rows, rims, partial, w_first):
    whole, part, recv_spec, weight, anywhere = specs()
    slots, nodes = partial.shape[0], own_rows.shape[0]
    near_rows = nodes + sum(rim.shape[0] for rim in rims) + 1
    return pl.pallas_call(
        near_kernel,
        name="near",
        grid_spec=pltpu.PrefetchScalarGridSpec(
            num_scalar_prefetch=1,
            grid=(slots // ROWS,),
            in_specs=[whole((nodes, F))] + [whole(rim.shape) for rim in rims] + [part, weight(1)],
            out_specs=part,
            scratch_shapes=[
                pltpu.VMEM((near_rows * 4 + 4, 128), F32),
                pltpu.VMEM((ROWS * 4, 128), F32),
            ],
        ),
        out_shape=jax.ShapeDtypeStruct((slots, F), BF),
        compiler_params=pltpu.CompilerParams(vmem_limit_bytes=16 << 20),
        cost_estimate=pl.CostEstimate(
            flops=2 * 10**9, bytes_accessed=8 * 10**6, transcendentals=0
        ),
    )(near_index, own_rows, *rims, partial, w_first)


def late_call(
    far_list,
    far_count,
    block_tile,
    lives,
    far_pieces,
    pre,
    edge_latent,
    receiver,
    own_rows,
    w_first,
    w_second,
    edge_gain,
    w_node_first,
    w_node_second,
    node_gain,
):
    blocks, nodes = block_tile.shape[0], own_rows.shape[0]
    slots, steps = blocks * BLK, blocks // GROUP
    far_rows = sum(piece.shape[0] for piece in far_pieces)
    anywhere = pl.BlockSpec(memory_space=pl.ANY)
    local = pl.BlockSpec(memory_space=pltpu.VMEM)
    scalars = pl.BlockSpec(memory_space=pltpu.SMEM)
    return pl.pallas_call(
        late_kernel,
        name="late",
        in_specs=[scalars] * 4 + [anywhere] * FAR + [local] * 10,
        out_specs=[anywhere, local],
        scratch_shapes=[
            pltpu.VMEM((far_rows, 4, 128), BF),
            pltpu.VMEM((slots * 4 + 32, 128), F32),
            pltpu.VMEM((slots, F), BF),
            pltpu.VMEM((nodes, F), F32),
            pltpu.SemaphoreType.DMA((FAR,)),
            pltpu.SemaphoreType.DMA((steps,)),
        ],
        out_shape=[
            jax.ShapeDtypeStruct((slots, F), BF),
            jax.ShapeDtypeStruct((nodes, F), BF),
        ],
        compiler_params=pltpu.CompilerParams(vmem_limit_bytes=40 << 20),
        cost_estimate=pl.CostEstimate(
            flops=4 * 10**9, bytes_accessed=14 * 10**6, transcendentals=2 * 10**6
        ),
    )(
        far_list,
        far_count,
        block_tile,
        lives,
        *far_pieces,
        pre,
        edge_latent,
        own_rows,
        w_first,
        w_second,
        w_node_first,
        w_node_second,
        receiver.reshape(blocks, BLK),
        edge_gain.reshape(1, F),
        node_gain.reshape(1, F),
    )


def per_device(
    node_latent,
    edge_latent,
    sender,
    receiver,
    block_tile,
    w_first,
    w_second,
    edge_gain,
    w_node_first,
    w_node_second,
    node_gain,
):
    patch_rows, patch_cols, features = node_latent.shape
    lat_index = lax.axis_index("lat")
    lon_index = lax.axis_index("lon")
    lat_count, lon_count = lax.axis_size("lat"), lax.axis_size("lon")
    grid_cols = patch_cols * lon_count
    blocks = block_tile.shape[0]
    steps = blocks // GROUP
    nodes = patch_rows * patch_cols
    own_rows = node_latent.reshape(nodes, features)
    lanes = lambda a: a.reshape(-1, 4, 128)

    def pairs(first, count, wrap):
        couples = [(i, (i + 1) % count) for i in range(first, count if wrap else count - 1, 2)]
        return couples + [(j, i) for i, j in couples]

    lat_odd, lon_odd = lat_index % 2, lon_index % 2
    per = patch_rows // 4 * (patch_cols // 4)
    lane_rows = lambda rows: jax.ShapeDtypeStruct((rows, 4, 128), BF)
    copies, col_a, col_b, row_a, row_b = pl.pallas_call(
        coarse_kernel,
        name="coarse",
        in_specs=[pl.BlockSpec(memory_space=pltpu.SMEM), pl.BlockSpec(memory_space=pltpu.VMEM)],
        out_specs=[pl.BlockSpec(memory_space=pl.ANY)] + [pl.BlockSpec(memory_space=pltpu.VMEM)] * 4,
        scratch_shapes=[
            pltpu.VMEM((nodes * 4, 128), F32),
            pltpu.VMEM((4 * (per + 2 * patch_rows + 2 * patch_cols), 128), F32),
            pltpu.VMEM((per, 4, 128), BF),
            pltpu.SemaphoreType.DMA((lon_count,)),
        ],
        out_shape=[
            jax.ShapeDtypeStruct((lon_count, per, 4, 128), BF),
            lane_rows(patch_rows),
            lane_rows(patch_rows),
            lane_rows(patch_cols),
            lane_rows(patch_cols),
        ],
        compiler_params=pltpu.CompilerParams(vmem_limit_bytes=VMEM),
    )(jnp.stack([lat_odd, lon_odd]).astype(jnp.int32), own_rows)
    senders = jnp.maximum(sender, 0)
    send_row = senders // grid_cols
    send_col = senders % grid_cols
    row = send_row - lat_index * patch_rows
    col = (send_col - lon_index * patch_cols + 1) % grid_cols - 1
    is_near = (row >= -1) & (row <= patch_rows) & (col <= patch_cols)
    side = nodes + row + patch_rows * jnp.where(col < 0, 1 - lon_odd, lon_odd)
    inner = jnp.where((col < 0) | (col >= patch_cols), side, row * patch_cols + col)
    rim, span = nodes + 2 * patch_rows, patch_cols + 2
    strip = rim + col + 1 + span * jnp.where(row < 0, 1 - lat_odd, lat_odd)
    near_index = jnp.where((row < 0) | (row >= patch_rows), strip, inner)
    near_index = jnp.where(is_near, near_index, rim + 2 * span)
    src_lat, src_lon = send_row // patch_rows, send_col // patch_cols
    src_core, core = src_lat % 2, lat_index % 2
    at_x = ring_place((src_lat // 2 - lat_index // 2) % 4, src_core)
    half = jnp.where(src_core == core, 0, 1)
    within = send_row % patch_rows // 4 * (patch_cols // 4) + send_col % patch_cols // 4
    far_index = ((half * 4 + at_x) * lon_count + src_lon) * per + within
    far_list, far_count = far_lists((receiver >= 0) & ~is_near, far_index, steps)
    recv_rows = receiver.reshape(steps, GROUP, BLK)
    lives = jnp.sum((receiver >= 0).astype(jnp.int32).reshape(blocks, BLK), 1)

    side_a = lax.ppermute(col_a, "lon", pairs(0, lon_count, True))
    side_b = lax.ppermute(col_b, "lon", pairs(1, lon_count, True))
    plane = lanes(lax.all_to_all(copies, "lon", split_axis=0, concat_axis=0, tiled=True))
    plane, side_a, side_b, tiles, near_index, far_list, far_count, lives = lax.optimization_barrier(
        (plane, side_a, side_b, block_tile, near_index, far_list, far_count, lives)
    )

    ahead = move(plane, "x", (1, -1))
    plane_other = other_core(plane)
    west = jnp.where(lon_odd == 1, side_a, side_b)
    east = jnp.where(lon_odd == 1, side_b, side_a)
    wide = lambda r, rows: jnp.concatenate(
        [lax.dynamic_slice_in_dim(west, r, 1), rows, lax.dynamic_slice_in_dim(east, r, 1)], 0
    )
    edge_row = (1 - lat_odd) * (patch_rows - 1)
    strip_a = lax.ppermute(wide(edge_row, row_a), "lat", pairs(0, lat_count, False))
    strip_b = lax.ppermute(
        wide(patch_rows - 1 - edge_row, row_b), "lat", pairs(1, lat_count, False)
    )
    partial = early_call(tiles, edge_latent, recv_rows, own_rows, w_first)
    later, partial = lax.optimization_barrier((plane, partial))
    behind = move(later, "x", (-1, 1))
    ahead, partial = lax.optimization_barrier((ahead, partial))
    across = move(ahead, "x", (1, -1))
    rims = [side_a, side_b, strip_a, strip_b]
    pre = near_call(near_index, own_rows, rims, partial, w_first)
    across, behind, pre = lax.optimization_barrier((across, behind, pre))
    far_pieces = [plane, ahead, behind, across, plane_other]
    far_pieces += [other_core(piece) for piece in (ahead, behind, across)]
    edge_out, node_out = late_call(
        far_list,
        far_count,
        block_tile,
        lives,
        far_pieces,
        pre,
        edge_latent,
        receiver,
        own_rows,
        w_first,
        w_second,
        edge_gain,
        w_node_first,
        w_node_second,
        node_gain,
    )
    return node_out.reshape(patch_rows, patch_cols, features), edge_out


def solution(mesh):
    return jax.shard_map(
        per_device,
        mesh=mesh,
        in_specs=(
            P("lat", "lon", None),
            P(("lat", "lon"), None),
            P(("lat", "lon")),
            P(("lat", "lon")),
            P(("lat", "lon")),
            P(),
            P(),
            P(),
            P(),
            P(),
            P(),
        ),
        out_specs=(P("lat", "lon", None), P(("lat", "lon"), None)),
        check_vma=False,
    )
```

```python
import jax
import jax.numpy as jnp
from jax import lax
from jax.experimental import pallas as pl
from jax.experimental.pallas import tpu as pltpu
from jax.sharding import PartitionSpec as P

F = 512
BLK = 128
GROUP = 4
ROWS = GROUP * BLK
RIMS = 4
FAR = 8
VMEM = 16 << 20
BF = jnp.bfloat16
F32 = jnp.float32


def device_of(x, c, y, z):
    return (x % 4 * 2 + c) * 16 + y % 4 * 4 + z % 4


def shift(axis, by_core):
    pairs = []
    for x in range(4):
        for c in range(2):
            for y in range(4):
                for z in range(4):
                    to = {"x": x, "y": y, "z": z}
                    to[axis] += by_core[c]
                    pairs.append((device_of(x, c, y, z), device_of(to["x"], c, to["y"], to["z"])))
    return pairs


def other_core(value):
    pairs = [
        (device_of(x, c, y, z), device_of(x, 1 - c, y, z))
        for x in range(4)
        for c in range(2)
        for y in range(4)
        for z in range(4)
    ]
    return lax.ppermute(value, ("lat", "lon"), pairs)


def move(value, axis, by_core):
    return lax.ppermute(value, ("lat", "lon"), shift(axis, by_core))


def ring_place(offset, core):
    near = jnp.where((offset == 1) == (core == 1), 1, 2)
    return jnp.where(offset == 0, 0, jnp.where(offset == 2, 3, near))


def silu(v):
    half = 0.5 * v
    return half + half * jnp.tanh(half)


def normed(values, gain):
    centred = values - jnp.mean(values, -1, keepdims=True)
    spread = jnp.mean(centred * centred, -1, keepdims=True)
    return centred * lax.rsqrt(spread + 1e-05) * gain


def dot(a, b):
    return jnp.dot(a, b, preferred_element_type=F32)


def chosen(recv_row):
    return (lax.broadcasted_iota(jnp.int32, (BLK, BLK), 0) == recv_row).astype(BF)


def fetch(count, unroll, entry, table, sent):
    def body(i, carry):
        for u in range(unroll):
            slot, row = entry(i * unroll + u)
            sent[pl.ds(pl.multiple_of(slot * 4, 4), 4), :] = table[row].astype(F32)
        return carry

    lax.fori_loop(0, count, body, 0)


def sent_rows(sent, base=0):
    return jnp.concatenate(
        [sent[pl.ds(base * 4 + j, ROWS, stride=4), :].astype(BF) for j in range(4)], axis=1
    )


def load_table(pieces, table, sem):
    copies = []
    start = 0
    for i, piece in enumerate(pieces):
        rows = piece.shape[0]
        copies.append(pltpu.make_async_copy(piece, table.at[pl.ds(start, rows)], sem.at[i]))
        start += rows
    for copy in copies:
        copy.start()
    return copies


def coarse_kernel(odd, node_ref, out_hbm, *refs):
    col_refs, row_refs = refs[0:2], refs[2:4]
    wide, tall, block, sem = refs[4:]
    nodes, sides, cols = node_ref.shape[0], col_refs[0].shape[0], row_refs[0].shape[0]
    per = block.shape[0]
    run = cols // 4
    starts = []
    at = 0
    for rows in (per, sides, sides, cols, cols):
        starts.append(at)
        at += rows
    for j in range(4):
        wide[j * nodes : (j + 1) * nodes, :] = node_ref[:, j * 128 : (j + 1) * 128].astype(F32)

    def take(start, count, j, first, stride):
        source = pl.ds(j * nodes + first, count, stride=stride)
        tall[pl.ds(start * 4 + j, count, stride=4), :] = wide[source, :]

    for j in range(4):
        for r in range(sides // 4):
            take(starts[0] + r * run, run, j, 4 * r * cols, 4)
        take(starts[1], sides, j, 0, cols)
        take(starts[2], sides, j, cols - 1, cols)
        take(starts[3], cols, j, 0, 1)
        take(starts[4], cols, j, nodes - cols, 1)
    row = lambda k, i: tall[(starts[k] + i) * 4 : (starts[k] + i) * 4 + 4, :]
    for i in range(per):
        block[i] = row(0, i).astype(BF)
    stores = [
        pltpu.make_async_copy(block, out_hbm.at[d], sem.at[d]) for d in range(out_hbm.shape[0])
    ]
    for store in stores:
        store.start()
    for refs_of, low, high, is_odd in ((col_refs, 1, 2, odd[1] == 1), (row_refs, 3, 4, odd[0] == 1)):
        for i in range(refs_of[0].shape[0]):
            first, last = row(low, i), row(high, i)
            refs_of[0][i] = jnp.where(is_odd, first, last).astype(BF)
            refs_of[1][i] = jnp.where(is_odd, last, first).astype(BF)
    for store in stores:
        store.wait()


def early_kernel(tiles, edge_ref, recv_ref, node_ref, we_ref, wr_ref, part_ref, got_ref):
    step = pl.program_id(0)

    for k in range(GROUP):
        tile = pl.multiple_of(tiles[step * GROUP + k] * BLK, BLK)
        hot = chosen(recv_ref[k : k + 1, :])
        rows = lax.dot_general(
            hot,
            node_ref[pl.ds(tile, BLK), :],
            (((0,), (0,)), ((), ())),
            preferred_element_type=F32,
        )
        got_ref[k * BLK : (k + 1) * BLK, :] = rows.astype(BF)
    total = dot(edge_ref[...], we_ref[...]) + dot(got_ref[...], wr_ref[...])
    part_ref[...] = total.astype(BF)


def near_kernel(near_index, node_ref, *refs):
    rims = refs[:RIMS]
    part_ref, ws_ref, pre_ref, tall, sent = refs[RIMS:]
    nodes = node_ref.shape[0]
    step = pl.program_id(0)

    @pl.when(step == 0)
    def _():
        for j in range(4):
            tall[pl.ds(j, nodes, stride=4), :] = node_ref[:, j * 128 : (j + 1) * 128].astype(F32)
        at = nodes * 4
        for rim in rims:
            for i in range(rim.shape[0]):
                tall[at : at + 4, :] = rim[i].astype(F32)
                at += 4
        tall[at : at + 4, :] = jnp.zeros((4, 128), F32)

    def body(i, carry):
        for u in range(16):
            e = i * 16 + u
            row = near_index[step * ROWS + e]
            sent[pl.ds(pl.multiple_of(e * 4, 4), 4), :] = tall[
                pl.ds(pl.multiple_of(row * 4, 4), 4), :
            ]
        return carry

    lax.fori_loop(0, ROWS // 16, body, 0)
    total = part_ref[...].astype(F32) + dot(sent_rows(sent), ws_ref[...])
    pre_ref[...] = total.astype(BF)


def late_kernel(far_list, far_count, tiles, lives, *refs):
    pieces = refs[:FAR]
    (
        pre,
        edge,
        node,
        w1,
        w2,
        wn,
        wn2,
        recv_ref,
        eg_ref,
        ng_ref,
        out_hbm,
        node_out_ref,
        table,
        sent,
        out,
        agg,
        sem,
        out_sem,
    ) = refs[FAR:]
    steps = recv_ref.shape[0] // GROUP
    copies = load_table(pieces, table, sem)
    sent[...] = jnp.zeros_like(sent)
    agg[...] = jnp.zeros_like(agg)
    for copy in copies:
        copy.wait()

    for g in range(steps):

        def entry(i):
            packed = far_list[g * ROWS + i]
            return packed & 4095, packed >> 12

        fetch((far_count[g] + 15) >> 4, 16, entry, table, sent)
    place = lax.broadcasted_iota(jnp.int32, (BLK, F), 0)
    stores = []
    for g in range(steps):
        base = g * ROWS
        rows = pl.ds(base, ROWS)
        total = pre[rows, :].astype(F32) + dot(sent_rows(sent, base), w1[F : 2 * F, :])
        message = normed(dot(silu(total).astype(BF), w2[...]), eg_ref[...]).astype(BF)
        for k in range(GROUP):
            b = g * GROUP + k
            part = message[k * BLK : (k + 1) * BLK, :]
            at = pl.ds(base + k * BLK, BLK)
            live = place < lives[b]
            out[at, :] = jnp.where(
                live, edge[at, :].astype(F32) + part.astype(F32), 0.0
            ).astype(BF)
            tile = pl.multiple_of(tiles[b] * BLK, BLK)
            agg[pl.ds(tile, BLK), :] += dot(chosen(recv_ref[b : b + 1, :]), part)
        store = pltpu.make_async_copy(out.at[rows], out_hbm.at[rows], out_sem.at[g])
        store.start()
        stores.append(store)
    first_sum = dot(node[...], wn[:F, :]) + dot(agg[...].astype(BF), wn[F:, :])
    second = dot(silu(first_sum).astype(BF), wn2[...])
    node_out_ref[...] = (node[...].astype(F32) + normed(second, ng_ref[...])).astype(BF)
    for store in stores:
        store.wait()


def far_lists(is_far, far_index, steps):
    place = jnp.arange(ROWS, dtype=jnp.int32)
    slots = steps * ROWS
    far = is_far.reshape(steps, ROWS)
    flag = far.astype(jnp.int32)
    before = place[:, None] > place[None, :]
    rank = jnp.sum(jnp.where(before[None], flag[:, None, :], 0), 2)
    packed = (far_index * 4096 + jnp.arange(slots, dtype=jnp.int32) - slots).reshape(steps, ROWS)
    hit = (rank[:, None, :] == place[None, :, None]) & far[:, None, :]
    return (slots + jnp.sum(jnp.where(hit, packed[:, None, :], 0), 2)).reshape(-1), jnp.sum(flag, 1)


def specs():
    whole = lambda shape: pl.BlockSpec(shape, lambda i, *_: (0,) * len(shape))
    part = pl.BlockSpec((ROWS, F), lambda i, *_: (i, 0))
    recv_spec = pl.BlockSpec((None, GROUP, BLK), lambda i, *_: (i, 0, 0))
    weight = lambda k: pl.BlockSpec((F, F), lambda i, *_: (k, 0))
    anywhere = pl.BlockSpec(memory_space=pl.ANY)
    return whole, part, recv_spec, weight, anywhere


def early_call(block_tile, edge_latent, recv_rows, own_rows, w_first):
    whole, part, recv_spec, weight, anywhere = specs()
    blocks, nodes = block_tile.shape[0], own_rows.shape[0]
    return pl.pallas_call(
        early_kernel,
        name="early",
        grid_spec=pltpu.PrefetchScalarGridSpec(
            num_scalar_prefetch=1,
            grid=(blocks // GROUP,),
            in_specs=[part, recv_spec, whole((nodes, F)), weight(0), weight(2)],
            out_specs=part,
            scratch_shapes=[pltpu.VMEM((ROWS, F), BF)],
        ),
        out_shape=jax.ShapeDtypeStruct((blocks * BLK, F), BF),
        compiler_params=pltpu.CompilerParams(vmem_limit_bytes=16 << 20),
        cost_estimate=pl.CostEstimate(
            flops=3 * 10**9, bytes_accessed=10 * 10**6, transcendentals=0
        ),
    )(block_tile, edge_latent, recv_rows, own_rows, w_first, w_first)


def near_call(near_index, own_rows, rims, partial, w_first):
    whole, part, recv_spec, weight, anywhere = specs()
    slots, nodes = partial.shape[0], own_rows.shape[0]
    near_rows = nodes + sum(rim.shape[0] for rim in rims) + 1
    return pl.pallas_call(
        near_kernel,
        name="near",
        grid_spec=pltpu.PrefetchScalarGridSpec(
            num_scalar_prefetch=1,
            grid=(slots // ROWS,),
            in_specs=[whole((nodes, F))] + [whole(rim.shape) for rim in rims] + [part, weight(1)],
            out_specs=part,
            scratch_shapes=[
                pltpu.VMEM((near_rows * 4 + 4, 128), F32),
                pltpu.VMEM((ROWS * 4, 128), F32),
            ],
        ),
        out_shape=jax.ShapeDtypeStruct((slots, F), BF),
        compiler_params=pltpu.CompilerParams(vmem_limit_bytes=16 << 20),
        cost_estimate=pl.CostEstimate(
            flops=2 * 10**9, bytes_accessed=8 * 10**6, transcendentals=0
        ),
    )(near_index, own_rows, *rims, partial, w_first)


def late_call(
    far_list,
    far_count,
    block_tile,
    lives,
    far_pieces,
    pre,
    edge_latent,
    receiver,
    own_rows,
    w_first,
    w_second,
    edge_gain,
    w_node_first,
    w_node_second,
    node_gain,
):
    blocks, nodes = block_tile.shape[0], own_rows.shape[0]
    slots, steps = blocks * BLK, blocks // GROUP
    far_rows = sum(piece.shape[0] for piece in far_pieces)
    anywhere = pl.BlockSpec(memory_space=pl.ANY)
    local = pl.BlockSpec(memory_space=pltpu.VMEM)
    scalars = pl.BlockSpec(memory_space=pltpu.SMEM)
    return pl.pallas_call(
        late_kernel,
        name="late",
        in_specs=[scalars] * 4 + [anywhere] * FAR + [local] * 10,
        out_specs=[anywhere, local],
        scratch_shapes=[
            pltpu.VMEM((far_rows, 4, 128), BF),
            pltpu.VMEM((slots * 4 + 32, 128), F32),
            pltpu.VMEM((slots, F), BF),
            pltpu.VMEM((nodes, F), F32),
            pltpu.SemaphoreType.DMA((FAR,)),
            pltpu.SemaphoreType.DMA((steps,)),
        ],
        out_shape=[
            jax.ShapeDtypeStruct((slots, F), BF),
            jax.ShapeDtypeStruct((nodes, F), BF),
        ],
        compiler_params=pltpu.CompilerParams(vmem_limit_bytes=40 << 20),
        cost_estimate=pl.CostEstimate(
            flops=4 * 10**9, bytes_accessed=14 * 10**6, transcendentals=2 * 10**6
        ),
    )(
        far_list,
        far_count,
        block_tile,
        lives,
        *far_pieces,
        pre,
        edge_latent,
        own_rows,
        w_first,
        w_second,
        w_node_first,
        w_node_second,
        receiver.reshape(blocks, BLK),
        edge_gain.reshape(1, F),
        node_gain.reshape(1, F),
    )


def per_device(
    node_latent,
    edge_latent,
    sender,
    receiver,
    block_tile,
    w_first,
    w_second,
    edge_gain,
    w_node_first,
    w_node_second,
    node_gain,
):
    patch_rows, patch_cols, features = node_latent.shape
    lat_index = lax.axis_index("lat")
    lon_index = lax.axis_index("lon")
    lat_count, lon_count = lax.axis_size("lat"), lax.axis_size("lon")
    grid_cols = patch_cols * lon_count
    blocks = block_tile.shape[0]
    steps = blocks // GROUP
    nodes = patch_rows * patch_cols
    own_rows = node_latent.reshape(nodes, features)
    lanes = lambda a: a.reshape(-1, 4, 128)

    def pairs(first, count, wrap):
        couples = [(i, (i + 1) % count) for i in range(first, count if wrap else count - 1, 2)]
        return couples + [(j, i) for i, j in couples]

    lat_odd, lon_odd = lat_index % 2, lon_index % 2
    per = patch_rows // 4 * (patch_cols // 4)
    lane_rows = lambda rows: jax.ShapeDtypeStruct((rows, 4, 128), BF)
    copies, col_a, col_b, row_a, row_b = pl.pallas_call(
        coarse_kernel,
        name="coarse",
        in_specs=[pl.BlockSpec(memory_space=pltpu.SMEM), pl.BlockSpec(memory_space=pltpu.VMEM)],
        out_specs=[pl.BlockSpec(memory_space=pl.ANY)] + [pl.BlockSpec(memory_space=pltpu.VMEM)] * 4,
        scratch_shapes=[
            pltpu.VMEM((nodes * 4, 128), F32),
            pltpu.VMEM((4 * (per + 2 * patch_rows + 2 * patch_cols), 128), F32),
            pltpu.VMEM((per, 4, 128), BF),
            pltpu.SemaphoreType.DMA((lon_count,)),
        ],
        out_shape=[
            jax.ShapeDtypeStruct((lon_count, per, 4, 128), BF),
            lane_rows(patch_rows),
            lane_rows(patch_rows),
            lane_rows(patch_cols),
            lane_rows(patch_cols),
        ],
        compiler_params=pltpu.CompilerParams(vmem_limit_bytes=VMEM),
    )(jnp.stack([lat_odd, lon_odd]).astype(jnp.int32), own_rows)
    senders = jnp.maximum(sender, 0)
    send_row = senders // grid_cols
    send_col = senders % grid_cols
    row = send_row - lat_index * patch_rows
    col = (send_col - lon_index * patch_cols + 1) % grid_cols - 1
    is_near = (row >= -1) & (row <= patch_rows) & (col <= patch_cols)
    side = nodes + row + patch_rows * jnp.where(col < 0, 1 - lon_odd, lon_odd)
    inner = jnp.where((col < 0) | (col >= patch_cols), side, row * patch_cols + col)
    rim, span = nodes + 2 * patch_rows, patch_cols + 2
    strip = rim + col + 1 + span * jnp.where(row < 0, 1 - lat_odd, lat_odd)
    near_index = jnp.where((row < 0) | (row >= patch_rows), strip, inner)
    near_index = jnp.where(is_near, near_index, rim + 2 * span)
    src_lat, src_lon = send_row // patch_rows, send_col // patch_cols
    src_core, core = src_lat % 2, lat_index % 2
    at_x = ring_place((src_lat // 2 - lat_index // 2) % 4, src_core)
    half = jnp.where(src_core == core, 0, 1)
    within = send_row % patch_rows // 4 * (patch_cols // 4) + send_col % patch_cols // 4
    far_index = ((half * 4 + at_x) * lon_count + src_lon) * per + within
    far_list, far_count = far_lists((receiver >= 0) & ~is_near, far_index, steps)
    recv_rows = receiver.reshape(steps, GROUP, BLK)
    lives = jnp.sum((receiver >= 0).astype(jnp.int32).reshape(blocks, BLK), 1)

    side_a = lax.ppermute(col_a, "lon", pairs(0, lon_count, True))
    side_b = lax.ppermute(col_b, "lon", pairs(1, lon_count, True))
    plane = lanes(lax.all_to_all(copies, "lon", split_axis=0, concat_axis=0, tiled=True))
    plane, side_a, side_b, tiles, near_index, far_list, far_count, lives = lax.optimization_barrier(
        (plane, side_a, side_b, block_tile, near_index, far_list, far_count, lives)
    )

    ahead = move(plane, "x", (1, -1))
    plane_other = other_core(plane)
    west = jnp.where(lon_odd == 1, side_a, side_b)
    east = jnp.where(lon_odd == 1, side_b, side_a)
    wide = lambda r, rows: jnp.concatenate(
        [lax.dynamic_slice_in_dim(west, r, 1), rows, lax.dynamic_slice_in_dim(east, r, 1)], 0
    )
    edge_row = (1 - lat_odd) * (patch_rows - 1)
    strip_a = lax.ppermute(wide(edge_row, row_a), "lat", pairs(0, lat_count, False))
    strip_b = lax.ppermute(
        wide(patch_rows - 1 - edge_row, row_b), "lat", pairs(1, lat_count, False)
    )
    partial = early_call(tiles, edge_latent, recv_rows, own_rows, w_first)
    later, partial, strip_a, strip_b = lax.optimization_barrier((plane, partial, strip_a, strip_b))
    behind = move(later, "x", (-1, 1))
    ahead, partial = lax.optimization_barrier((ahead, partial))
    across = move(ahead, "x", (1, -1))
    rims = [side_a, side_b, strip_a, strip_b]
    pre = near_call(near_index, own_rows, rims, partial, w_first)
    across, behind, pre = lax.optimization_barrier((across, behind, pre))
    far_pieces = [plane, ahead, behind, across, plane_other]
    far_pieces += [other_core(piece) for piece in (ahead, behind, across)]
    edge_out, node_out = late_call(
        far_list,
        far_count,
        block_tile,
        lives,
        far_pieces,
        pre,
        edge_latent,
        receiver,
        own_rows,
        w_first,
        w_second,
        edge_gain,
        w_node_first,
        w_node_second,
        node_gain,
    )
    return node_out.reshape(patch_rows, patch_cols, features), edge_out


def solution(mesh):
    return jax.shard_map(
        per_device,
        mesh=mesh,
        in_specs=(
            P("lat", "lon", None),
            P(("lat", "lon"), None),
            P(("lat", "lon")),
            P(("lat", "lon")),
            P(("lat", "lon")),
            P(),
            P(),
            P(),
            P(),
            P(),
            P(),
        ),
        out_specs=(P("lat", "lon", None), P(("lat", "lon"), None)),
        check_vma=False,
    )
```

```python
import jax
import jax.numpy as jnp
from jax import lax
from jax.experimental import pallas as pl
from jax.experimental.pallas import tpu as pltpu
from jax.sharding import PartitionSpec as P

F = 512
BLK = 128
GROUP = 4
ROWS = GROUP * BLK
RIMS = 4
FAR = 8
VMEM = 16 << 20
BF = jnp.bfloat16
F32 = jnp.float32


def device_of(x, c, y, z):
    return (x % 4 * 2 + c) * 16 + y % 4 * 4 + z % 4


def shift(axis, by_core):
    pairs = []
    for x in range(4):
        for c in range(2):
            for y in range(4):
                for z in range(4):
                    to = {"x": x, "y": y, "z": z}
                    to[axis] += by_core[c]
                    pairs.append((device_of(x, c, y, z), device_of(to["x"], c, to["y"], to["z"])))
    return pairs


def other_core(value):
    pairs = [
        (device_of(x, c, y, z), device_of(x, 1 - c, y, z))
        for x in range(4)
        for c in range(2)
        for y in range(4)
        for z in range(4)
    ]
    return lax.ppermute(value, ("lat", "lon"), pairs)


def move(value, axis, by_core):
    return lax.ppermute(value, ("lat", "lon"), shift(axis, by_core))


def ring_place(offset, core):
    near = jnp.where((offset == 1) == (core == 1), 1, 2)
    return jnp.where(offset == 0, 0, jnp.where(offset == 2, 3, near))


def silu(v):
    half = 0.5 * v
    return half + half * jnp.tanh(half)


def normed(values, gain):
    centred = values - jnp.mean(values, -1, keepdims=True)
    spread = jnp.mean(centred * centred, -1, keepdims=True)
    return centred * lax.rsqrt(spread + 1e-05) * gain


def dot(a, b):
    return jnp.dot(a, b, preferred_element_type=F32)


def chosen(recv_row):
    return (lax.broadcasted_iota(jnp.int32, (BLK, BLK), 0) == recv_row).astype(BF)


def fetch(count, unroll, entry, table, sent):
    def body(i, carry):
        for u in range(unroll):
            slot, row = entry(i * unroll + u)
            sent[pl.ds(pl.multiple_of(slot * 4, 4), 4), :] = table[row].astype(F32)
        return carry

    lax.fori_loop(0, count, body, 0)


def sent_rows(sent, base=0):
    return jnp.concatenate(
        [sent[pl.ds(base * 4 + j, ROWS, stride=4), :].astype(BF) for j in range(4)], axis=1
    )


def load_table(pieces, table, sem):
    copies = []
    start = 0
    for i, piece in enumerate(pieces):
        rows = piece.shape[0]
        copies.append(pltpu.make_async_copy(piece, table.at[pl.ds(start, rows)], sem.at[i]))
        start += rows
    for copy in copies:
        copy.start()
    return copies


def coarse_kernel(odd, node_ref, out_hbm, *refs):
    col_refs, row_refs = refs[0:2], refs[2:4]
    wide, tall, block, sem = refs[4:]
    nodes, sides, cols = node_ref.shape[0], col_refs[0].shape[0], row_refs[0].shape[0]
    per = block.shape[0]
    run = cols // 4
    starts = []
    at = 0
    for rows in (per, sides, sides, cols, cols):
        starts.append(at)
        at += rows
    for j in range(4):
        wide[j * nodes : (j + 1) * nodes, :] = node_ref[:, j * 128 : (j + 1) * 128].astype(F32)

    def take(start, count, j, first, stride):
        source = pl.ds(j * nodes + first, count, stride=stride)
        tall[pl.ds(start * 4 + j, count, stride=4), :] = wide[source, :]

    for j in range(4):
        for r in range(sides // 4):
            take(starts[0] + r * run, run, j, 4 * r * cols, 4)
        take(starts[1], sides, j, 0, cols)
        take(starts[2], sides, j, cols - 1, cols)
        take(starts[3], cols, j, 0, 1)
        take(starts[4], cols, j, nodes - cols, 1)
    row = lambda k, i: tall[(starts[k] + i) * 4 : (starts[k] + i) * 4 + 4, :]
    for i in range(per):
        block[i] = row(0, i).astype(BF)
    stores = [
        pltpu.make_async_copy(block, out_hbm.at[d], sem.at[d]) for d in range(out_hbm.shape[0])
    ]
    for store in stores:
        store.start()
    for refs_of, low, high, is_odd in ((col_refs, 1, 2, odd[1] == 1), (row_refs, 3, 4, odd[0] == 1)):
        for i in range(refs_of[0].shape[0]):
            first, last = row(low, i), row(high, i)
            refs_of[0][i] = jnp.where(is_odd, first, last).astype(BF)
            refs_of[1][i] = jnp.where(is_odd, last, first).astype(BF)
    for store in stores:
        store.wait()


def early_kernel(tiles, edge_ref, recv_ref, node_ref, we_ref, wr_ref, part_ref, got_ref):
    step = pl.program_id(0)

    for k in range(GROUP):
        tile = pl.multiple_of(tiles[step * GROUP + k] * BLK, BLK)
        hot = chosen(recv_ref[k : k + 1, :])
        rows = lax.dot_general(
            hot,
            node_ref[pl.ds(tile, BLK), :],
            (((0,), (0,)), ((), ())),
            preferred_element_type=F32,
        )
        got_ref[k * BLK : (k + 1) * BLK, :] = rows.astype(BF)
    total = dot(edge_ref[...], we_ref[...]) + dot(got_ref[...], wr_ref[...])
    part_ref[...] = total.astype(BF)


def near_kernel(near_index, node_ref, *refs):
    rims = refs[:RIMS]
    part_ref, ws_ref, pre_ref, tall, sent = refs[RIMS:]
    nodes = node_ref.shape[0]
    step = pl.program_id(0)

    @pl.when(step == 0)
    def _():
        for j in range(4):
            tall[pl.ds(j, nodes, stride=4), :] = node_ref[:, j * 128 : (j + 1) * 128].astype(F32)
        at = nodes * 4
        for rim in rims:
            for i in range(rim.shape[0]):
                tall[at : at + 4, :] = rim[i].astype(F32)
                at += 4
        tall[at : at + 4, :] = jnp.zeros((4, 128), F32)

    def body(i, carry):
        for u in range(16):
            e = i * 16 + u
            row = near_index[step * ROWS + e]
            sent[pl.ds(pl.multiple_of(e * 4, 4), 4), :] = tall[
                pl.ds(pl.multiple_of(row * 4, 4), 4), :
            ]
        return carry

    lax.fori_loop(0, ROWS // 16, body, 0)
    total = part_ref[...].astype(F32) + dot(sent_rows(sent), ws_ref[...])
    pre_ref[...] = total.astype(BF)


def late_kernel(far_list, far_count, tiles, lives, *refs):
    pieces = refs[:FAR]
    (
        pre,
        edge,
        node,
        w1,
        w2,
        wn,
        wn2,
        recv_ref,
        eg_ref,
        ng_ref,
        out_hbm,
        node_out_ref,
        table,
        sent,
        out,
        agg,
        sem,
        out_sem,
    ) = refs[FAR:]
    steps = recv_ref.shape[0] // GROUP
    copies = load_table(pieces, table, sem)
    sent[...] = jnp.zeros_like(sent)
    agg[...] = jnp.zeros_like(agg)
    for copy in copies:
        copy.wait()

    for g in range(steps):

        def entry(i):
            packed = far_list[g * ROWS + i]
            return packed & 4095, packed >> 12

        fetch((far_count[g] + 15) >> 4, 16, entry, table, sent)
    place = lax.broadcasted_iota(jnp.int32, (BLK, F), 0)
    stores = []
    for g in range(steps):
        base = g * ROWS
        rows = pl.ds(base, ROWS)
        total = pre[rows, :].astype(F32) + dot(sent_rows(sent, base), w1[F : 2 * F, :])
        message = normed(dot(silu(total).astype(BF), w2[...]), eg_ref[...]).astype(BF)
        for k in range(GROUP):
            b = g * GROUP + k
            part = message[k * BLK : (k + 1) * BLK, :]
            at = pl.ds(base + k * BLK, BLK)
            live = place < lives[b]
            out[at, :] = jnp.where(
                live, edge[at, :].astype(F32) + part.astype(F32), 0.0
            ).astype(BF)
            tile = pl.multiple_of(tiles[b] * BLK, BLK)
            agg[pl.ds(tile, BLK), :] += dot(chosen(recv_ref[b : b + 1, :]), part)
        store = pltpu.make_async_copy(out.at[rows], out_hbm.at[rows], out_sem.at[g])
        store.start()
        stores.append(store)
    first_sum = dot(node[...], wn[:F, :]) + dot(agg[...].astype(BF), wn[F:, :])
    second = dot(silu(first_sum).astype(BF), wn2[...])
    node_out_ref[...] = (node[...].astype(F32) + normed(second, ng_ref[...])).astype(BF)
    for store in stores:
        store.wait()


def far_lists(is_far, far_index, steps):
    place = jnp.arange(ROWS, dtype=jnp.int32)
    slots = steps * ROWS
    far = is_far.reshape(steps, ROWS)
    flag = far.astype(jnp.int32)
    before = place[:, None] > place[None, :]
    rank = jnp.sum(jnp.where(before[None], flag[:, None, :], 0), 2)
    packed = (far_index * 4096 + jnp.arange(slots, dtype=jnp.int32) - slots).reshape(steps, ROWS)
    hit = (rank[:, None, :] == place[None, :, None]) & far[:, None, :]
    return (slots + jnp.sum(jnp.where(hit, packed[:, None, :], 0), 2)).reshape(-1), jnp.sum(flag, 1)


def specs():
    whole = lambda shape: pl.BlockSpec(shape, lambda i, *_: (0,) * len(shape))
    part = pl.BlockSpec((ROWS, F), lambda i, *_: (i, 0))
    recv_spec = pl.BlockSpec((None, GROUP, BLK), lambda i, *_: (i, 0, 0))
    weight = lambda k: pl.BlockSpec((F, F), lambda i, *_: (k, 0))
    anywhere = pl.BlockSpec(memory_space=pl.ANY)
    return whole, part, recv_spec, weight, anywhere


def early_call(block_tile, edge_latent, recv_rows, own_rows, w_first):
    whole, part, recv_spec, weight, anywhere = specs()
    blocks, nodes = block_tile.shape[0], own_rows.shape[0]
    return pl.pallas_call(
        early_kernel,
        name="early",
        grid_spec=pltpu.PrefetchScalarGridSpec(
            num_scalar_prefetch=1,
            grid=(blocks // GROUP,),
            in_specs=[part, recv_spec, whole((nodes, F)), weight(0), weight(2)],
            out_specs=part,
            scratch_shapes=[pltpu.VMEM((ROWS, F), BF)],
        ),
        out_shape=jax.ShapeDtypeStruct((blocks * BLK, F), BF),
        compiler_params=pltpu.CompilerParams(vmem_limit_bytes=16 << 20),
        cost_estimate=pl.CostEstimate(
            flops=3 * 10**9, bytes_accessed=10 * 10**6, transcendentals=0
        ),
    )(block_tile, edge_latent, recv_rows, own_rows, w_first, w_first)


def near_call(near_index, own_rows, rims, partial, w_first):
    whole, part, recv_spec, weight, anywhere = specs()
    slots, nodes = partial.shape[0], own_rows.shape[0]
    near_rows = nodes + sum(rim.shape[0] for rim in rims) + 1
    return pl.pallas_call(
        near_kernel,
        name="near",
        grid_spec=pltpu.PrefetchScalarGridSpec(
            num_scalar_prefetch=1,
            grid=(slots // ROWS,),
            in_specs=[whole((nodes, F))] + [whole(rim.shape) for rim in rims] + [part, weight(1)],
            out_specs=part,
            scratch_shapes=[
                pltpu.VMEM((near_rows * 4 + 4, 128), F32),
                pltpu.VMEM((ROWS * 4, 128), F32),
            ],
        ),
        out_shape=jax.ShapeDtypeStruct((slots, F), BF),
        compiler_params=pltpu.CompilerParams(vmem_limit_bytes=16 << 20),
        cost_estimate=pl.CostEstimate(
            flops=2 * 10**9, bytes_accessed=8 * 10**6, transcendentals=0
        ),
    )(near_index, own_rows, *rims, partial, w_first)


def late_call(
    far_list,
    far_count,
    block_tile,
    lives,
    far_pieces,
    pre,
    edge_latent,
    receiver,
    own_rows,
    w_first,
    w_second,
    edge_gain,
    w_node_first,
    w_node_second,
    node_gain,
):
    blocks, nodes = block_tile.shape[0], own_rows.shape[0]
    slots, steps = blocks * BLK, blocks // GROUP
    far_rows = sum(piece.shape[0] for piece in far_pieces)
    anywhere = pl.BlockSpec(memory_space=pl.ANY)
    local = pl.BlockSpec(memory_space=pltpu.VMEM)
    scalars = pl.BlockSpec(memory_space=pltpu.SMEM)
    return pl.pallas_call(
        late_kernel,
        name="late",
        in_specs=[scalars] * 4 + [anywhere] * FAR + [local] * 10,
        out_specs=[anywhere, local],
        scratch_shapes=[
            pltpu.VMEM((far_rows, 4, 128), BF),
            pltpu.VMEM((slots * 4 + 32, 128), F32),
            pltpu.VMEM((slots, F), BF),
            pltpu.VMEM((nodes, F), F32),
            pltpu.SemaphoreType.DMA((FAR,)),
            pltpu.SemaphoreType.DMA((steps,)),
        ],
        out_shape=[
            jax.ShapeDtypeStruct((slots, F), BF),
            jax.ShapeDtypeStruct((nodes, F), BF),
        ],
        compiler_params=pltpu.CompilerParams(vmem_limit_bytes=40 << 20),
        cost_estimate=pl.CostEstimate(
            flops=4 * 10**9, bytes_accessed=14 * 10**6, transcendentals=2 * 10**6
        ),
    )(
        far_list,
        far_count,
        block_tile,
        lives,
        *far_pieces,
        pre,
        edge_latent,
        own_rows,
        w_first,
        w_second,
        w_node_first,
        w_node_second,
        receiver.reshape(blocks, BLK),
        edge_gain.reshape(1, F),
        node_gain.reshape(1, F),
    )


def per_device(
    node_latent,
    edge_latent,
    sender,
    receiver,
    block_tile,
    w_first,
    w_second,
    edge_gain,
    w_node_first,
    w_node_second,
    node_gain,
):
    patch_rows, patch_cols, features = node_latent.shape
    lat_index = lax.axis_index("lat")
    lon_index = lax.axis_index("lon")
    lat_count, lon_count = lax.axis_size("lat"), lax.axis_size("lon")
    grid_cols = patch_cols * lon_count
    blocks = block_tile.shape[0]
    steps = blocks // GROUP
    nodes = patch_rows * patch_cols
    own_rows = node_latent.reshape(nodes, features)
    lanes = lambda a: a.reshape(-1, 4, 128)

    def pairs(first, count, wrap):
        couples = [(i, (i + 1) % count) for i in range(first, count if wrap else count - 1, 2)]
        return couples + [(j, i) for i, j in couples]

    lat_odd, lon_odd = lat_index % 2, lon_index % 2
    per = patch_rows // 4 * (patch_cols // 4)
    lane_rows = lambda rows: jax.ShapeDtypeStruct((rows, 4, 128), BF)
    copies, col_a, col_b, row_a, row_b = pl.pallas_call(
        coarse_kernel,
        name="coarse",
        in_specs=[pl.BlockSpec(memory_space=pltpu.SMEM), pl.BlockSpec(memory_space=pltpu.VMEM)],
        out_specs=[pl.BlockSpec(memory_space=pl.ANY)] + [pl.BlockSpec(memory_space=pltpu.VMEM)] * 4,
        scratch_shapes=[
            pltpu.VMEM((nodes * 4, 128), F32),
            pltpu.VMEM((4 * (per + 2 * patch_rows + 2 * patch_cols), 128), F32),
            pltpu.VMEM((per, 4, 128), BF),
            pltpu.SemaphoreType.DMA((lon_count,)),
        ],
        out_shape=[
            jax.ShapeDtypeStruct((lon_count, per, 4, 128), BF),
            lane_rows(patch_rows),
            lane_rows(patch_rows),
            lane_rows(patch_cols),
            lane_rows(patch_cols),
        ],
        compiler_params=pltpu.CompilerParams(vmem_limit_bytes=VMEM),
    )(jnp.stack([lat_odd, lon_odd]).astype(jnp.int32), own_rows)
    senders = jnp.maximum(sender, 0)
    send_row = senders // grid_cols
    send_col = senders % grid_cols
    row = send_row - lat_index * patch_rows
    col = (send_col - lon_index * patch_cols + 1) % grid_cols - 1
    is_near = (row >= -1) & (row <= patch_rows) & (col <= patch_cols)
    side = nodes + row + patch_rows * jnp.where(col < 0, 1 - lon_odd, lon_odd)
    inner = jnp.where((col < 0) | (col >= patch_cols), side, row * patch_cols + col)
    rim, span = nodes + 2 * patch_rows, patch_cols + 2
    strip = rim + col + 1 + span * jnp.where(row < 0, 1 - lat_odd, lat_odd)
    near_index = jnp.where((row < 0) | (row >= patch_rows), strip, inner)
    near_index = jnp.where(is_near, near_index, rim + 2 * span)
    src_lat, src_lon = send_row // patch_rows, send_col // patch_cols
    src_core, core = src_lat % 2, lat_index % 2
    at_x = ring_place((src_lat // 2 - lat_index // 2) % 4, src_core)
    half = jnp.where(src_core == core, 0, 1)
    within = send_row % patch_rows // 4 * (patch_cols // 4) + send_col % patch_cols // 4
    far_index = ((half * 4 + at_x) * lon_count + src_lon) * per + within
    far_list, far_count = far_lists((receiver >= 0) & ~is_near, far_index, steps)
    recv_rows = receiver.reshape(steps, GROUP, BLK)
    lives = jnp.sum((receiver >= 0).astype(jnp.int32).reshape(blocks, BLK), 1)

    side_a = lax.ppermute(col_a, "lon", pairs(0, lon_count, True))
    side_b = lax.ppermute(col_b, "lon", pairs(1, lon_count, True))
    plane = lanes(lax.all_to_all(copies, "lon", split_axis=0, concat_axis=0, tiled=True))
    plane, side_a, side_b, tiles, near_index, far_list, far_count, lives = lax.optimization_barrier(
        (plane, side_a, side_b, block_tile, near_index, far_list, far_count, lives)
    )

    ahead = move(plane, "x", (1, -1))
    plane_other = other_core(plane)
    west = jnp.where(lon_odd == 1, side_a, side_b)
    east = jnp.where(lon_odd == 1, side_b, side_a)
    wide = lambda r, rows: jnp.concatenate(
        [lax.dynamic_slice_in_dim(west, r, 1), rows, lax.dynamic_slice_in_dim(east, r, 1)], 0
    )
    edge_row = (1 - lat_odd) * (patch_rows - 1)
    strip_a = lax.ppermute(wide(edge_row, row_a), "lat", pairs(0, lat_count, False))
    strip_b = lax.ppermute(
        wide(patch_rows - 1 - edge_row, row_b), "lat", pairs(1, lat_count, False)
    )
    later, tiles, strip_a, strip_b = lax.optimization_barrier((plane, tiles, strip_a, strip_b))
    behind = move(later, "x", (-1, 1))
    partial = early_call(tiles, edge_latent, recv_rows, own_rows, w_first)
    ahead, partial = lax.optimization_barrier((ahead, partial))
    across = move(ahead, "x", (1, -1))
    rims = [side_a, side_b, strip_a, strip_b]
    pre = near_call(near_index, own_rows, rims, partial, w_first)
    across, behind, pre = lax.optimization_barrier((across, behind, pre))
    far_pieces = [plane, ahead, behind, across, plane_other]
    far_pieces += [other_core(piece) for piece in (ahead, behind, across)]
    edge_out, node_out = late_call(
        far_list,
        far_count,
        block_tile,
        lives,
        far_pieces,
        pre,
        edge_latent,
        receiver,
        own_rows,
        w_first,
        w_second,
        edge_gain,
        w_node_first,
        w_node_second,
        node_gain,
    )
    return node_out.reshape(patch_rows, patch_cols, features), edge_out


def solution(mesh):
    return jax.shard_map(
        per_device,
        mesh=mesh,
        in_specs=(
            P("lat", "lon", None),
            P(("lat", "lon"), None),
            P(("lat", "lon")),
            P(("lat", "lon")),
            P(("lat", "lon")),
            P(),
            P(),
            P(),
            P(),
            P(),
            P(),
        ),
        out_specs=(P("lat", "lon", None), P(("lat", "lon"), None)),
        check_vma=False,
    )
```

```python
import jax
import jax.numpy as jnp
from jax import lax
from jax.experimental import pallas as pl
from jax.experimental.pallas import tpu as pltpu
from jax.sharding import PartitionSpec as P

F = 512
BLK = 128
GROUP = 4
ROWS = GROUP * BLK
RIMS = 4
FAR = 8
VMEM = 16 << 20
BF = jnp.bfloat16
F32 = jnp.float32


def device_of(x, c, y, z):
    return (x % 4 * 2 + c) * 16 + y % 4 * 4 + z % 4


def shift(axis, by_core):
    pairs = []
    for x in range(4):
        for c in range(2):
            for y in range(4):
                for z in range(4):
                    to = {"x": x, "y": y, "z": z}
                    to[axis] += by_core[c]
                    pairs.append((device_of(x, c, y, z), device_of(to["x"], c, to["y"], to["z"])))
    return pairs


def other_core(value):
    pairs = [
        (device_of(x, c, y, z), device_of(x, 1 - c, y, z))
        for x in range(4)
        for c in range(2)
        for y in range(4)
        for z in range(4)
    ]
    return lax.ppermute(value, ("lat", "lon"), pairs)


def move(value, axis, by_core):
    return lax.ppermute(value, ("lat", "lon"), shift(axis, by_core))


def ring_place(offset, core):
    near = jnp.where((offset == 1) == (core == 1), 1, 2)
    return jnp.where(offset == 0, 0, jnp.where(offset == 2, 3, near))


def silu(v):
    half = 0.5 * v
    return half + half * jnp.tanh(half)


def normed(values, gain):
    centred = values - jnp.mean(values, -1, keepdims=True)
    spread = jnp.mean(centred * centred, -1, keepdims=True)
    return centred * lax.rsqrt(spread + 1e-05) * gain


def dot(a, b):
    return jnp.dot(a, b, preferred_element_type=F32)


def chosen(recv_row):
    return (lax.broadcasted_iota(jnp.int32, (BLK, BLK), 0) == recv_row).astype(BF)


def fetch(count, unroll, entry, table, sent):
    def body(i, carry):
        for u in range(unroll):
            slot, row = entry(i * unroll + u)
            sent[pl.ds(pl.multiple_of(slot * 4, 4), 4), :] = table[row].astype(F32)
        return carry

    lax.fori_loop(0, count, body, 0)


def sent_rows(sent, base=0):
    return jnp.concatenate(
        [sent[pl.ds(base * 4 + j, ROWS, stride=4), :].astype(BF) for j in range(4)], axis=1
    )


def load_table(pieces, table, sem):
    copies = []
    start = 0
    for i, piece in enumerate(pieces):
        rows = piece.shape[0]
        copies.append(pltpu.make_async_copy(piece, table.at[pl.ds(start, rows)], sem.at[i]))
        start += rows
    for copy in copies:
        copy.start()
    return copies


def coarse_kernel(odd, node_ref, out_hbm, *refs):
    col_refs, row_refs = refs[0:2], refs[2:4]
    wide, tall, block, sem = refs[4:]
    nodes, sides, cols = node_ref.shape[0], col_refs[0].shape[0], row_refs[0].shape[0]
    per = block.shape[0]
    run = cols // 4
    starts = []
    at = 0
    for rows in (per, sides, sides, cols, cols):
        starts.append(at)
        at += rows
    for j in range(4):
        wide[j * nodes : (j + 1) * nodes, :] = node_ref[:, j * 128 : (j + 1) * 128].astype(F32)

    def take(start, count, j, first, stride):
        source = pl.ds(j * nodes + first, count, stride=stride)
        tall[pl.ds(start * 4 + j, count, stride=4), :] = wide[source, :]

    for j in range(4):
        for r in range(sides // 4):
            take(starts[0] + r * run, run, j, 4 * r * cols, 4)
        take(starts[1], sides, j, 0, cols)
        take(starts[2], sides, j, cols - 1, cols)
        take(starts[3], cols, j, 0, 1)
        take(starts[4], cols, j, nodes - cols, 1)
    row = lambda k, i: tall[(starts[k] + i) * 4 : (starts[k] + i) * 4 + 4, :]
    for i in range(per):
        block[i] = row(0, i).astype(BF)
    stores = [
        pltpu.make_async_copy(block, out_hbm.at[d], sem.at[d]) for d in range(out_hbm.shape[0])
    ]
    for store in stores:
        store.start()
    for refs_of, low, high, is_odd in ((col_refs, 1, 2, odd[1] == 1), (row_refs, 3, 4, odd[0] == 1)):
        for i in range(refs_of[0].shape[0]):
            first, last = row(low, i), row(high, i)
            refs_of[0][i] = jnp.where(is_odd, first, last).astype(BF)
            refs_of[1][i] = jnp.where(is_odd, last, first).astype(BF)
    for store in stores:
        store.wait()


def early_kernel(tiles, edge_ref, recv_ref, node_ref, we_ref, wr_ref, part_ref, got_ref):
    step = pl.program_id(0)

    for k in range(GROUP):
        tile = pl.multiple_of(tiles[step * GROUP + k] * BLK, BLK)
        hot = chosen(recv_ref[k : k + 1, :])
        rows = lax.dot_general(
            hot,
            node_ref[pl.ds(tile, BLK), :],
            (((0,), (0,)), ((), ())),
            preferred_element_type=F32,
        )
        got_ref[k * BLK : (k + 1) * BLK, :] = rows.astype(BF)
    total = dot(edge_ref[...], we_ref[...]) + dot(got_ref[...], wr_ref[...])
    part_ref[...] = total.astype(BF)


def near_kernel(near_index, node_ref, *refs):
    rims = refs[:RIMS]
    part_ref, ws_ref, pre_ref, tall, sent = refs[RIMS:]
    nodes = node_ref.shape[0]
    step = pl.program_id(0)

    @pl.when(step == 0)
    def _():
        for j in range(4):
            tall[pl.ds(j, nodes, stride=4), :] = node_ref[:, j * 128 : (j + 1) * 128].astype(F32)
        at = nodes * 4
        for rim in rims:
            for i in range(rim.shape[0]):
                tall[at : at + 4, :] = rim[i].astype(F32)
                at += 4
        tall[at : at + 4, :] = jnp.zeros((4, 128), F32)

    def body(i, carry):
        for u in range(16):
            e = i * 16 + u
            row = near_index[step * ROWS + e]
            sent[pl.ds(pl.multiple_of(e * 4, 4), 4), :] = tall[
                pl.ds(pl.multiple_of(row * 4, 4), 4), :
            ]
        return carry

    lax.fori_loop(0, ROWS // 16, body, 0)
    total = part_ref[...].astype(F32) + dot(sent_rows(sent), ws_ref[...])
    pre_ref[...] = total.astype(BF)


def late_kernel(far_list, far_count, tiles, lives, *refs):
    pieces = refs[:FAR]
    (
        pre,
        edge,
        node,
        w1,
        w2,
        wn,
        wn2,
        recv_ref,
        eg_ref,
        ng_ref,
        out_hbm,
        node_out_ref,
        table,
        sent,
        out,
        agg,
        sem,
        out_sem,
    ) = refs[FAR:]
    steps = recv_ref.shape[0] // GROUP
    copies = load_table(pieces, table, sem)
    sent[...] = jnp.zeros_like(sent)
    agg[...] = jnp.zeros_like(agg)
    for copy in copies:
        copy.wait()

    for g in range(steps):

        def entry(i):
            packed = far_list[g * ROWS + i]
            return packed & 4095, packed >> 12

        fetch((far_count[g] + 15) >> 4, 16, entry, table, sent)
    place = lax.broadcasted_iota(jnp.int32, (BLK, F), 0)
    stores = []
    for g in range(steps):
        base = g * ROWS
        rows = pl.ds(base, ROWS)
        total = pre[rows, :].astype(F32) + dot(sent_rows(sent, base), w1[F : 2 * F, :])
        message = normed(dot(silu(total).astype(BF), w2[...]), eg_ref[...]).astype(BF)
        for k in range(GROUP):
            b = g * GROUP + k
            part = message[k * BLK : (k + 1) * BLK, :]
            at = pl.ds(base + k * BLK, BLK)
            live = place < lives[b]
            out[at, :] = jnp.where(
                live, edge[at, :].astype(F32) + part.astype(F32), 0.0
            ).astype(BF)
            tile = pl.multiple_of(tiles[b] * BLK, BLK)
            agg[pl.ds(tile, BLK), :] += dot(chosen(recv_ref[b : b + 1, :]), part)
        store = pltpu.make_async_copy(out.at[rows], out_hbm.at[rows], out_sem.at[g])
        store.start()
        stores.append(store)
    first_sum = dot(node[...], wn[:F, :]) + dot(agg[...].astype(BF), wn[F:, :])
    second = dot(silu(first_sum).astype(BF), wn2[...])
    node_out_ref[...] = (node[...].astype(F32) + normed(second, ng_ref[...])).astype(BF)
    for store in stores:
        store.wait()


def far_lists(is_far, far_index, steps):
    place = jnp.arange(ROWS, dtype=jnp.int32)
    slots = steps * ROWS
    far = is_far.reshape(steps, ROWS)
    flag = far.astype(jnp.int32)
    before = place[:, None] > place[None, :]
    rank = jnp.sum(jnp.where(before[None], flag[:, None, :], 0), 2)
    packed = (far_index * 4096 + jnp.arange(slots, dtype=jnp.int32) - slots).reshape(steps, ROWS)
    hit = (rank[:, None, :] == place[None, :, None]) & far[:, None, :]
    return (slots + jnp.sum(jnp.where(hit, packed[:, None, :], 0), 2)).reshape(-1), jnp.sum(flag, 1)


def specs():
    whole = lambda shape: pl.BlockSpec(shape, lambda i, *_: (0,) * len(shape))
    part = pl.BlockSpec((ROWS, F), lambda i, *_: (i, 0))
    recv_spec = pl.BlockSpec((None, GROUP, BLK), lambda i, *_: (i, 0, 0))
    weight = lambda k: pl.BlockSpec((F, F), lambda i, *_: (k, 0))
    anywhere = pl.BlockSpec(memory_space=pl.ANY)
    return whole, part, recv_spec, weight, anywhere


def early_call(block_tile, edge_latent, recv_rows, own_rows, w_first):
    whole, part, recv_spec, weight, anywhere = specs()
    blocks, nodes = block_tile.shape[0], own_rows.shape[0]
    return pl.pallas_call(
        early_kernel,
        name="early",
        grid_spec=pltpu.PrefetchScalarGridSpec(
            num_scalar_prefetch=1,
            grid=(blocks // GROUP,),
            in_specs=[part, recv_spec, whole((nodes, F)), weight(0), weight(2)],
            out_specs=part,
            scratch_shapes=[pltpu.VMEM((ROWS, F), BF)],
        ),
        out_shape=jax.ShapeDtypeStruct((blocks * BLK, F), BF),
        compiler_params=pltpu.CompilerParams(vmem_limit_bytes=16 << 20),
        cost_estimate=pl.CostEstimate(
            flops=3 * 10**9, bytes_accessed=10 * 10**6, transcendentals=0
        ),
    )(block_tile, edge_latent, recv_rows, own_rows, w_first, w_first)


def near_call(near_index, own_rows, rims, partial, w_first):
    whole, part, recv_spec, weight, anywhere = specs()
    slots, nodes = partial.shape[0], own_rows.shape[0]
    near_rows = nodes + sum(rim.shape[0] for rim in rims) + 1
    return pl.pallas_call(
        near_kernel,
        name="near",
        grid_spec=pltpu.PrefetchScalarGridSpec(
            num_scalar_prefetch=1,
            grid=(slots // ROWS,),
            in_specs=[whole((nodes, F))] + [whole(rim.shape) for rim in rims] + [part, weight(1)],
            out_specs=part,
            scratch_shapes=[
                pltpu.VMEM((near_rows * 4 + 4, 128), F32),
                pltpu.VMEM((ROWS * 4, 128), F32),
            ],
        ),
        out_shape=jax.ShapeDtypeStruct((slots, F), BF),
        compiler_params=pltpu.CompilerParams(vmem_limit_bytes=16 << 20),
        cost_estimate=pl.CostEstimate(
            flops=2 * 10**9, bytes_accessed=8 * 10**6, transcendentals=0
        ),
    )(near_index, own_rows, *rims, partial, w_first)


def late_call(
    far_list,
    far_count,
    block_tile,
    lives,
    far_pieces,
    pre,
    edge_latent,
    receiver,
    own_rows,
    w_first,
    w_second,
    edge_gain,
    w_node_first,
    w_node_second,
    node_gain,
):
    blocks, nodes = block_tile.shape[0], own_rows.shape[0]
    slots, steps = blocks * BLK, blocks // GROUP
    far_rows = sum(piece.shape[0] for piece in far_pieces)
    anywhere = pl.BlockSpec(memory_space=pl.ANY)
    local = pl.BlockSpec(memory_space=pltpu.VMEM)
    scalars = pl.BlockSpec(memory_space=pltpu.SMEM)
    return pl.pallas_call(
        late_kernel,
        name="late",
        in_specs=[scalars] * 4 + [anywhere] * FAR + [local] * 10,
        out_specs=[anywhere, local],
        scratch_shapes=[
            pltpu.VMEM((far_rows, 4, 128), BF),
            pltpu.VMEM((slots * 4 + 32, 128), F32),
            pltpu.VMEM((slots, F), BF),
            pltpu.VMEM((nodes, F), F32),
            pltpu.SemaphoreType.DMA((FAR,)),
            pltpu.SemaphoreType.DMA((steps,)),
        ],
        out_shape=[
            jax.ShapeDtypeStruct((slots, F), BF),
            jax.ShapeDtypeStruct((nodes, F), BF),
        ],
        compiler_params=pltpu.CompilerParams(vmem_limit_bytes=40 << 20),
        cost_estimate=pl.CostEstimate(
            flops=4 * 10**9, bytes_accessed=14 * 10**6, transcendentals=2 * 10**6
        ),
    )(
        far_list,
        far_count,
        block_tile,
        lives,
        *far_pieces,
        pre,
        edge_latent,
        own_rows,
        w_first,
        w_second,
        w_node_first,
        w_node_second,
        receiver.reshape(blocks, BLK),
        edge_gain.reshape(1, F),
        node_gain.reshape(1, F),
    )


def per_device(
    node_latent,
    edge_latent,
    sender,
    receiver,
    block_tile,
    w_first,
    w_second,
    edge_gain,
    w_node_first,
    w_node_second,
    node_gain,
):
    patch_rows, patch_cols, features = node_latent.shape
    lat_index = lax.axis_index("lat")
    lon_index = lax.axis_index("lon")
    lat_count, lon_count = lax.axis_size("lat"), lax.axis_size("lon")
    grid_cols = patch_cols * lon_count
    blocks = block_tile.shape[0]
    steps = blocks // GROUP
    nodes = patch_rows * patch_cols
    own_rows = node_latent.reshape(nodes, features)
    lanes = lambda a: a.reshape(-1, 4, 128)

    def pairs(first, count, wrap):
        couples = [(i, (i + 1) % count) for i in range(first, count if wrap else count - 1, 2)]
        return couples + [(j, i) for i, j in couples]

    lat_odd, lon_odd = lat_index % 2, lon_index % 2
    per = patch_rows // 4 * (patch_cols // 4)
    lane_rows = lambda rows: jax.ShapeDtypeStruct((rows, 4, 128), BF)
    copies, col_a, col_b, row_a, row_b = pl.pallas_call(
        coarse_kernel,
        name="coarse",
        in_specs=[pl.BlockSpec(memory_space=pltpu.SMEM), pl.BlockSpec(memory_space=pltpu.VMEM)],
        out_specs=[pl.BlockSpec(memory_space=pl.ANY)] + [pl.BlockSpec(memory_space=pltpu.VMEM)] * 4,
        scratch_shapes=[
            pltpu.VMEM((nodes * 4, 128), F32),
            pltpu.VMEM((4 * (per + 2 * patch_rows + 2 * patch_cols), 128), F32),
            pltpu.VMEM((per, 4, 128), BF),
            pltpu.SemaphoreType.DMA((lon_count,)),
        ],
        out_shape=[
            jax.ShapeDtypeStruct((lon_count, per, 4, 128), BF),
            lane_rows(patch_rows),
            lane_rows(patch_rows),
            lane_rows(patch_cols),
            lane_rows(patch_cols),
        ],
        compiler_params=pltpu.CompilerParams(vmem_limit_bytes=VMEM),
    )(jnp.stack([lat_odd, lon_odd]).astype(jnp.int32), own_rows)
    senders = jnp.maximum(sender, 0)
    send_row = senders // grid_cols
    send_col = senders % grid_cols
    row = send_row - lat_index * patch_rows
    col = (send_col - lon_index * patch_cols + 1) % grid_cols - 1
    is_near = (row >= -1) & (row <= patch_rows) & (col <= patch_cols)
    side = nodes + row + patch_rows * jnp.where(col < 0, 1 - lon_odd, lon_odd)
    inner = jnp.where((col < 0) | (col >= patch_cols), side, row * patch_cols + col)
    rim, span = nodes + 2 * patch_rows, patch_cols + 2
    strip = rim + col + 1 + span * jnp.where(row < 0, 1 - lat_odd, lat_odd)
    near_index = jnp.where((row < 0) | (row >= patch_rows), strip, inner)
    near_index = jnp.where(is_near, near_index, rim + 2 * span)
    src_lat, src_lon = send_row // patch_rows, send_col // patch_cols
    src_core, core = src_lat % 2, lat_index % 2
    at_x = ring_place((src_lat // 2 - lat_index // 2) % 4, src_core)
    half = jnp.where(src_core == core, 0, 1)
    within = send_row % patch_rows // 4 * (patch_cols // 4) + send_col % patch_cols // 4
    far_index = ((half * 4 + at_x) * lon_count + src_lon) * per + within
    far_list, far_count = far_lists((receiver >= 0) & ~is_near, far_index, steps)
    recv_rows = receiver.reshape(steps, GROUP, BLK)
    lives = jnp.sum((receiver >= 0).astype(jnp.int32).reshape(blocks, BLK), 1)

    side_a = lax.ppermute(col_a, "lon", pairs(0, lon_count, True))
    side_b = lax.ppermute(col_b, "lon", pairs(1, lon_count, True))
    plane = lanes(lax.all_to_all(copies, "lon", split_axis=0, concat_axis=0, tiled=True))
    plane, side_a, side_b, tiles, near_index, far_list, far_count, lives = lax.optimization_barrier(
        (plane, side_a, side_b, block_tile, near_index, far_list, far_count, lives)
    )

    ahead = move(plane, "x", (1, -1))
    plane_other = other_core(plane)
    west = jnp.where(lon_odd == 1, side_a, side_b)
    east = jnp.where(lon_odd == 1, side_b, side_a)
    wide = lambda r, rows: jnp.concatenate(
        [lax.dynamic_slice_in_dim(west, r, 1), rows, lax.dynamic_slice_in_dim(east, r, 1)], 0
    )
    edge_row = (1 - lat_odd) * (patch_rows - 1)
    strip_a = lax.ppermute(wide(edge_row, row_a), "lat", pairs(0, lat_count, False))
    strip_b = lax.ppermute(
        wide(patch_rows - 1 - edge_row, row_b), "lat", pairs(1, lat_count, False)
    )
    later, tiles, strip_a, strip_b = lax.optimization_barrier((plane, tiles, strip_a, strip_b))
    behind = move(later, "x", (-1, 1))
    ahead, tiles, strip_a, strip_b = lax.optimization_barrier((ahead, tiles, strip_a, strip_b))
    across = move(ahead, "x", (1, -1))
    partial = early_call(tiles, edge_latent, recv_rows, own_rows, w_first)
    rims = [side_a, side_b, strip_a, strip_b]
    pre = near_call(near_index, own_rows, rims, partial, w_first)
    across, behind, pre = lax.optimization_barrier((across, behind, pre))
    far_pieces = [plane, ahead, behind, across, plane_other]
    far_pieces += [other_core(piece) for piece in (ahead, behind, across)]
    edge_out, node_out = late_call(
        far_list,
        far_count,
        block_tile,
        lives,
        far_pieces,
        pre,
        edge_latent,
        receiver,
        own_rows,
        w_first,
        w_second,
        edge_gain,
        w_node_first,
        w_node_second,
        node_gain,
    )
    return node_out.reshape(patch_rows, patch_cols, features), edge_out


def solution(mesh):
    return jax.shard_map(
        per_device,
        mesh=mesh,
        in_specs=(
            P("lat", "lon", None),
            P(("lat", "lon"), None),
            P(("lat", "lon")),
            P(("lat", "lon")),
            P(("lat", "lon")),
            P(),
            P(),
            P(),
            P(),
            P(),
            P(),
        ),
        out_specs=(P("lat", "lon", None), P(("lat", "lon"), None)),
        check_vma=False,
    )
```

```python
import jax
import jax.numpy as jnp
from jax import lax
from jax.experimental import pallas as pl
from jax.experimental.pallas import tpu as pltpu
from jax.sharding import PartitionSpec as P

F = 512
BLK = 128
GROUP = 4
ROWS = GROUP * BLK
RIMS = 4
FAR = 8
VMEM = 16 << 20
BF = jnp.bfloat16
F32 = jnp.float32


def device_of(x, c, y, z):
    return (x % 4 * 2 + c) * 16 + y % 4 * 4 + z % 4


def shift(axis, by_core):
    pairs = []
    for x in range(4):
        for c in range(2):
            for y in range(4):
                for z in range(4):
                    to = {"x": x, "y": y, "z": z}
                    to[axis] += by_core[c]
                    pairs.append((device_of(x, c, y, z), device_of(to["x"], c, to["y"], to["z"])))
    return pairs


def other_core(value):
    pairs = [
        (device_of(x, c, y, z), device_of(x, 1 - c, y, z))
        for x in range(4)
        for c in range(2)
        for y in range(4)
        for z in range(4)
    ]
    return lax.ppermute(value, ("lat", "lon"), pairs)


def move(value, axis, by_core):
    return lax.ppermute(value, ("lat", "lon"), shift(axis, by_core))


def ring_place(offset, core):
    near = jnp.where((offset == 1) == (core == 1), 1, 2)
    return jnp.where(offset == 0, 0, jnp.where(offset == 2, 3, near))


def silu(v):
    half = 0.5 * v
    return half + half * jnp.tanh(half)


def normed(values, gain):
    centred = values - jnp.mean(values, -1, keepdims=True)
    spread = jnp.mean(centred * centred, -1, keepdims=True)
    return centred * lax.rsqrt(spread + 1e-05) * gain


def dot(a, b):
    return jnp.dot(a, b, preferred_element_type=F32)


def chosen(recv_row):
    return (lax.broadcasted_iota(jnp.int32, (BLK, BLK), 0) == recv_row).astype(BF)


def fetch(count, unroll, entry, table, sent):
    def body(i, carry):
        for u in range(unroll):
            slot, row = entry(i * unroll + u)
            sent[pl.ds(pl.multiple_of(slot * 4, 4), 4), :] = table[row].astype(F32)
        return carry

    lax.fori_loop(0, count, body, 0)


def sent_rows(sent, base=0):
    return jnp.concatenate(
        [sent[pl.ds(base * 4 + j, ROWS, stride=4), :].astype(BF) for j in range(4)], axis=1
    )


def load_table(pieces, table, sem):
    copies = []
    start = 0
    for i, piece in enumerate(pieces):
        rows = piece.shape[0]
        copies.append(pltpu.make_async_copy(piece, table.at[pl.ds(start, rows)], sem.at[i]))
        start += rows
    for copy in copies:
        copy.start()
    return copies


def coarse_kernel(odd, node_ref, out_hbm, *refs):
    col_refs, row_refs = refs[0:2], refs[2:4]
    wide, tall, block, sem = refs[4:]
    nodes, sides, cols = node_ref.shape[0], col_refs[0].shape[0], row_refs[0].shape[0]
    per = block.shape[0]
    run = cols // 4
    starts = []
    at = 0
    for rows in (per, sides, sides, cols, cols):
        starts.append(at)
        at += rows
    for j in range(4):
        wide[j * nodes : (j + 1) * nodes, :] = node_ref[:, j * 128 : (j + 1) * 128].astype(F32)

    def take(start, count, j, first, stride):
        source = pl.ds(j * nodes + first, count, stride=stride)
        tall[pl.ds(start * 4 + j, count, stride=4), :] = wide[source, :]

    for j in range(4):
        for r in range(sides // 4):
            take(starts[0] + r * run, run, j, 4 * r * cols, 4)
        take(starts[1], sides, j, 0, cols)
        take(starts[2], sides, j, cols - 1, cols)
        take(starts[3], cols, j, 0, 1)
        take(starts[4], cols, j, nodes - cols, 1)
    row = lambda k, i: tall[(starts[k] + i) * 4 : (starts[k] + i) * 4 + 4, :]
    for i in range(per):
        block[i] = row(0, i).astype(BF)
    stores = [
        pltpu.make_async_copy(block, out_hbm.at[d], sem.at[d]) for d in range(out_hbm.shape[0])
    ]
    for store in stores:
        store.start()
    for refs_of, low, high, is_odd in ((col_refs, 1, 2, odd[1] == 1), (row_refs, 3, 4, odd[0] == 1)):
        for i in range(refs_of[0].shape[0]):
            first, last = row(low, i), row(high, i)
            refs_of[0][i] = jnp.where(is_odd, first, last).astype(BF)
            refs_of[1][i] = jnp.where(is_odd, last, first).astype(BF)
    for store in stores:
        store.wait()


def early_kernel(tiles, edge_ref, recv_ref, node_ref, we_ref, wr_ref, part_ref, got_ref):
    step = pl.program_id(0)

    for k in range(GROUP):
        tile = pl.multiple_of(tiles[step * GROUP + k] * BLK, BLK)
        hot = chosen(recv_ref[k : k + 1, :])
        rows = lax.dot_general(
            hot,
            node_ref[pl.ds(tile, BLK), :],
            (((0,), (0,)), ((), ())),
            preferred_element_type=F32,
        )
        got_ref[k * BLK : (k + 1) * BLK, :] = rows.astype(BF)
    total = dot(edge_ref[...], we_ref[...]) + dot(got_ref[...], wr_ref[...])
    part_ref[...] = total.astype(BF)


def near_kernel(near_index, node_ref, *refs):
    rims = refs[:RIMS]
    part_ref, ws_ref, pre_ref, tall, sent = refs[RIMS:]
    nodes = node_ref.shape[0]
    step = pl.program_id(0)

    @pl.when(step == 0)
    def _():
        for j in range(4):
            tall[pl.ds(j, nodes, stride=4), :] = node_ref[:, j * 128 : (j + 1) * 128].astype(F32)
        at = nodes * 4
        for rim in rims:
            for i in range(rim.shape[0]):
                tall[at : at + 4, :] = rim[i].astype(F32)
                at += 4
        tall[at : at + 4, :] = jnp.zeros((4, 128), F32)

    def body(i, carry):
        for u in range(16):
            e = i * 16 + u
            row = near_index[step * ROWS + e]
            sent[pl.ds(pl.multiple_of(e * 4, 4), 4), :] = tall[
                pl.ds(pl.multiple_of(row * 4, 4), 4), :
            ]
        return carry

    lax.fori_loop(0, ROWS // 16, body, 0)
    total = part_ref[...].astype(F32) + dot(sent_rows(sent), ws_ref[...])
    pre_ref[...] = total.astype(BF)


def late_kernel(far_list, far_count, tiles, lives, *refs):
    pieces = refs[:FAR]
    (
        pre,
        edge,
        node,
        w1,
        w2,
        wn,
        wn2,
        recv_ref,
        eg_ref,
        ng_ref,
        out_hbm,
        node_out_ref,
        table,
        sent,
        out,
        agg,
        sem,
        out_sem,
    ) = refs[FAR:]
    steps = recv_ref.shape[0] // GROUP
    copies = load_table(pieces, table, sem)
    sent[...] = jnp.zeros_like(sent)
    agg[...] = jnp.zeros_like(agg)
    for copy in copies:
        copy.wait()

    for g in range(steps):

        def entry(i):
            packed = far_list[g * ROWS + i]
            return packed & 4095, packed >> 12

        fetch((far_count[g] + 15) >> 4, 16, entry, table, sent)
    place = lax.broadcasted_iota(jnp.int32, (BLK, F), 0)
    stores = []
    for g in range(steps):
        base = g * ROWS
        rows = pl.ds(base, ROWS)
        total = pre[rows, :].astype(F32) + dot(sent_rows(sent, base), w1[F : 2 * F, :])
        message = normed(dot(silu(total).astype(BF), w2[...]), eg_ref[...]).astype(BF)
        for k in range(GROUP):
            b = g * GROUP + k
            part = message[k * BLK : (k + 1) * BLK, :]
            at = pl.ds(base + k * BLK, BLK)
            live = place < lives[b]
            out[at, :] = jnp.where(
                live, edge[at, :].astype(F32) + part.astype(F32), 0.0
            ).astype(BF)
            tile = pl.multiple_of(tiles[b] * BLK, BLK)
            agg[pl.ds(tile, BLK), :] += dot(chosen(recv_ref[b : b + 1, :]), part)
        store = pltpu.make_async_copy(out.at[rows], out_hbm.at[rows], out_sem.at[g])
        store.start()
        stores.append(store)
    first_sum = dot(node[...], wn[:F, :]) + dot(agg[...].astype(BF), wn[F:, :])
    second = dot(silu(first_sum).astype(BF), wn2[...])
    node_out_ref[...] = (node[...].astype(F32) + normed(second, ng_ref[...])).astype(BF)
    for store in stores:
        store.wait()


def far_lists(is_far, far_index, steps):
    place = jnp.arange(ROWS, dtype=jnp.int32)
    slots = steps * ROWS
    far = is_far.reshape(steps, ROWS)
    flag = far.astype(jnp.int32)
    before = place[:, None] > place[None, :]
    rank = jnp.sum(jnp.where(before[None], flag[:, None, :], 0), 2)
    packed = (far_index * 4096 + jnp.arange(slots, dtype=jnp.int32) - slots).reshape(steps, ROWS)
    hit = (rank[:, None, :] == place[None, :, None]) & far[:, None, :]
    return (slots + jnp.sum(jnp.where(hit, packed[:, None, :], 0), 2)).reshape(-1), jnp.sum(flag, 1)


def specs():
    whole = lambda shape: pl.BlockSpec(shape, lambda i, *_: (0,) * len(shape))
    part = pl.BlockSpec((ROWS, F), lambda i, *_: (i, 0))
    recv_spec = pl.BlockSpec((None, GROUP, BLK), lambda i, *_: (i, 0, 0))
    weight = lambda k: pl.BlockSpec((F, F), lambda i, *_: (k, 0))
    anywhere = pl.BlockSpec(memory_space=pl.ANY)
    return whole, part, recv_spec, weight, anywhere


def early_call(block_tile, edge_latent, recv_rows, own_rows, w_first):
    whole, part, recv_spec, weight, anywhere = specs()
    blocks, nodes = block_tile.shape[0], own_rows.shape[0]
    return pl.pallas_call(
        early_kernel,
        name="early",
        grid_spec=pltpu.PrefetchScalarGridSpec(
            num_scalar_prefetch=1,
            grid=(blocks // GROUP,),
            in_specs=[part, recv_spec, whole((nodes, F)), weight(0), weight(2)],
            out_specs=part,
            scratch_shapes=[pltpu.VMEM((ROWS, F), BF)],
        ),
        out_shape=jax.ShapeDtypeStruct((blocks * BLK, F), BF),
        compiler_params=pltpu.CompilerParams(vmem_limit_bytes=16 << 20),
        cost_estimate=pl.CostEstimate(
            flops=3 * 10**9, bytes_accessed=10 * 10**6, transcendentals=0
        ),
    )(block_tile, edge_latent, recv_rows, own_rows, w_first, w_first)


def near_call(near_index, own_rows, rims, partial, w_first):
    whole, part, recv_spec, weight, anywhere = specs()
    slots, nodes = partial.shape[0], own_rows.shape[0]
    near_rows = nodes + sum(rim.shape[0] for rim in rims) + 1
    return pl.pallas_call(
        near_kernel,
        name="near",
        grid_spec=pltpu.PrefetchScalarGridSpec(
            num_scalar_prefetch=1,
            grid=(slots // ROWS,),
            in_specs=[whole((nodes, F))] + [whole(rim.shape) for rim in rims] + [part, weight(1)],
            out_specs=part,
            scratch_shapes=[
                pltpu.VMEM((near_rows * 4 + 4, 128), F32),
                pltpu.VMEM((ROWS * 4, 128), F32),
            ],
        ),
        out_shape=jax.ShapeDtypeStruct((slots, F), BF),
        compiler_params=pltpu.CompilerParams(vmem_limit_bytes=16 << 20),
        cost_estimate=pl.CostEstimate(
            flops=2 * 10**9, bytes_accessed=8 * 10**6, transcendentals=0
        ),
    )(near_index, own_rows, *rims, partial, w_first)


def late_call(
    far_list,
    far_count,
    block_tile,
    lives,
    far_pieces,
    pre,
    edge_latent,
    receiver,
    own_rows,
    w_first,
    w_second,
    edge_gain,
    w_node_first,
    w_node_second,
    node_gain,
):
    blocks, nodes = block_tile.shape[0], own_rows.shape[0]
    slots, steps = blocks * BLK, blocks // GROUP
    far_rows = sum(piece.shape[0] for piece in far_pieces)
    anywhere = pl.BlockSpec(memory_space=pl.ANY)
    local = pl.BlockSpec(memory_space=pltpu.VMEM)
    scalars = pl.BlockSpec(memory_space=pltpu.SMEM)
    return pl.pallas_call(
        late_kernel,
        name="late",
        in_specs=[scalars] * 4 + [anywhere] * FAR + [local] * 10,
        out_specs=[anywhere, local],
        scratch_shapes=[
            pltpu.VMEM((far_rows, 4, 128), BF),
            pltpu.VMEM((slots * 4 + 32, 128), F32),
            pltpu.VMEM((slots, F), BF),
            pltpu.VMEM((nodes, F), F32),
            pltpu.SemaphoreType.DMA((FAR,)),
            pltpu.SemaphoreType.DMA((steps,)),
        ],
        out_shape=[
            jax.ShapeDtypeStruct((slots, F), BF),
            jax.ShapeDtypeStruct((nodes, F), BF),
        ],
        compiler_params=pltpu.CompilerParams(vmem_limit_bytes=40 << 20),
        cost_estimate=pl.CostEstimate(
            flops=4 * 10**9, bytes_accessed=14 * 10**6, transcendentals=2 * 10**6
        ),
    )(
        far_list,
        far_count,
        block_tile,
        lives,
        *far_pieces,
        pre,
        edge_latent,
        own_rows,
        w_first,
        w_second,
        w_node_first,
        w_node_second,
        receiver.reshape(blocks, BLK),
        edge_gain.reshape(1, F),
        node_gain.reshape(1, F),
    )


def per_device(
    node_latent,
    edge_latent,
    sender,
    receiver,
    block_tile,
    w_first,
    w_second,
    edge_gain,
    w_node_first,
    w_node_second,
    node_gain,
):
    patch_rows, patch_cols, features = node_latent.shape
    lat_index = lax.axis_index("lat")
    lon_index = lax.axis_index("lon")
    lat_count, lon_count = lax.axis_size("lat"), lax.axis_size("lon")
    grid_cols = patch_cols * lon_count
    blocks = block_tile.shape[0]
    steps = blocks // GROUP
    nodes = patch_rows * patch_cols
    own_rows = node_latent.reshape(nodes, features)
    lanes = lambda a: a.reshape(-1, 4, 128)

    def pairs(first, count, wrap):
        couples = [(i, (i + 1) % count) for i in range(first, count if wrap else count - 1, 2)]
        return couples + [(j, i) for i, j in couples]

    lat_odd, lon_odd = lat_index % 2, lon_index % 2
    per = patch_rows // 4 * (patch_cols // 4)
    lane_rows = lambda rows: jax.ShapeDtypeStruct((rows, 4, 128), BF)
    copies, col_a, col_b, row_a, row_b = pl.pallas_call(
        coarse_kernel,
        name="coarse",
        in_specs=[pl.BlockSpec(memory_space=pltpu.SMEM), pl.BlockSpec(memory_space=pltpu.VMEM)],
        out_specs=[pl.BlockSpec(memory_space=pl.ANY)] + [pl.BlockSpec(memory_space=pltpu.VMEM)] * 4,
        scratch_shapes=[
            pltpu.VMEM((nodes * 4, 128), F32),
            pltpu.VMEM((4 * (per + 2 * patch_rows + 2 * patch_cols), 128), F32),
            pltpu.VMEM((per, 4, 128), BF),
            pltpu.SemaphoreType.DMA((lon_count,)),
        ],
        out_shape=[
            jax.ShapeDtypeStruct((lon_count, per, 4, 128), BF),
            lane_rows(patch_rows),
            lane_rows(patch_rows),
            lane_rows(patch_cols),
            lane_rows(patch_cols),
        ],
        compiler_params=pltpu.CompilerParams(vmem_limit_bytes=VMEM),
    )(jnp.stack([lat_odd, lon_odd]).astype(jnp.int32), own_rows)
    senders = jnp.maximum(sender, 0)
    send_row = senders // grid_cols
    send_col = senders % grid_cols
    row = send_row - lat_index * patch_rows
    col = (send_col - lon_index * patch_cols + 1) % grid_cols - 1
    is_near = (row >= -1) & (row <= patch_rows) & (col <= patch_cols)
    side = nodes + row + patch_rows * jnp.where(col < 0, 1 - lon_odd, lon_odd)
    inner = jnp.where((col < 0) | (col >= patch_cols), side, row * patch_cols + col)
    rim, span = nodes + 2 * patch_rows, patch_cols + 2
    strip = rim + col + 1 + span * jnp.where(row < 0, 1 - lat_odd, lat_odd)
    near_index = jnp.where((row < 0) | (row >= patch_rows), strip, inner)
    near_index = jnp.where(is_near, near_index, rim + 2 * span)
    src_lat, src_lon = send_row // patch_rows, send_col // patch_cols
    src_core, core = src_lat % 2, lat_index % 2
    at_x = ring_place((src_lat // 2 - lat_index // 2) % 4, src_core)
    half = jnp.where(src_core == core, 0, 1)
    within = send_row % patch_rows // 4 * (patch_cols // 4) + send_col % patch_cols // 4
    far_index = ((half * 4 + at_x) * lon_count + src_lon) * per + within
    far_list, far_count = far_lists((receiver >= 0) & ~is_near, far_index, steps)
    recv_rows = receiver.reshape(steps, GROUP, BLK)
    lives = jnp.sum((receiver >= 0).astype(jnp.int32).reshape(blocks, BLK), 1)

    side_a = lax.ppermute(col_a, "lon", pairs(0, lon_count, True))
    side_b = lax.ppermute(col_b, "lon", pairs(1, lon_count, True))
    plane = lanes(lax.all_to_all(copies, "lon", split_axis=0, concat_axis=0, tiled=True))
    plane, side_a, side_b, tiles, near_index, far_list, far_count, lives = lax.optimization_barrier(
        (plane, side_a, side_b, block_tile, near_index, far_list, far_count, lives)
    )

    ahead = move(plane, "x", (1, -1))
    plane_other = other_core(plane)
    west = jnp.where(lon_odd == 1, side_a, side_b)
    east = jnp.where(lon_odd == 1, side_b, side_a)
    wide = lambda r, rows: jnp.concatenate(
        [lax.dynamic_slice_in_dim(west, r, 1), rows, lax.dynamic_slice_in_dim(east, r, 1)], 0
    )
    edge_row = (1 - lat_odd) * (patch_rows - 1)
    strip_a = lax.ppermute(wide(edge_row, row_a), "lat", pairs(0, lat_count, False))
    strip_b = lax.ppermute(
        wide(patch_rows - 1 - edge_row, row_b), "lat", pairs(1, lat_count, False)
    )
    later, tiles, strip_a, strip_b = lax.optimization_barrier((plane, tiles, strip_a, strip_b))
    behind = move(later, "x", (-1, 1))
    ahead, tiles, strip_a, strip_b = lax.optimization_barrier((ahead, tiles, strip_a, strip_b))
    across = move(ahead, "x", (1, -1))
    held = pltpu.with_memory_space_constraint(edge_latent, pltpu.HBM)
    partial = early_call(tiles, held, recv_rows, own_rows, w_first)
    rims = [side_a, side_b, strip_a, strip_b]
    pre = near_call(near_index, own_rows, rims, partial, w_first)
    across, behind, pre = lax.optimization_barrier((across, behind, pre))
    far_pieces = [plane, ahead, behind, across, plane_other]
    far_pieces += [other_core(piece) for piece in (ahead, behind, across)]
    edge_out, node_out = late_call(
        far_list,
        far_count,
        block_tile,
        lives,
        far_pieces,
        pre,
        edge_latent,
        receiver,
        own_rows,
        w_first,
        w_second,
        edge_gain,
        w_node_first,
        w_node_second,
        node_gain,
    )
    return node_out.reshape(patch_rows, patch_cols, features), edge_out


def solution(mesh):
    return jax.shard_map(
        per_device,
        mesh=mesh,
        in_specs=(
            P("lat", "lon", None),
            P(("lat", "lon"), None),
            P(("lat", "lon")),
            P(("lat", "lon")),
            P(("lat", "lon")),
            P(),
            P(),
            P(),
            P(),
            P(),
            P(),
        ),
        out_specs=(P("lat", "lon", None), P(("lat", "lon"), None)),
        check_vma=False,
    )
```
